512 devices in a mesh: tile: 64 (over z_hi, y, x), section: 8 (over z_lo, core).
Axes of the slice: x: 4, y: 8, z: 8 (z_hi: 2, z_lo: 4; z = z_hi * 4 + z_lo), core: 2. Of those that a mesh axis runs over, the one named last changes fastest.
Arguments:
- fields: bfloat16 [4, 2, 18, 147456], P(None, None, None, 'tile'), may hold values from -6 to 6, as said below
- land_mask: int32 [18, 768], P(None, 'tile'), may hold values 0 or 1
- land_vector: float32 [192], replicated, may hold values from -4 to 4
- w_qkv: bfloat16 [8, 192, 576], P('section'), may hold values from -3 to 3, as said below
- w_proj: bfloat16 [8, 192, 192], P('section'), may hold values from -0.4375 to 0.4375
- w_up: bfloat16 [8, 192, 768], P('section'), may hold values from -0.4375 to 0.4375
- w_down: bfloat16 [8, 768, 192], P('section'), may hold values from -0.21875 to 0.21875
Outputs:
- streams: bfloat16 [8, 4, 2, 18, 147456], P('section', None, None, None, 'tile')
The draws below stay inside these ranges and needn't reach their ends.
Inputs may be any that keep to these rules, and one draw needn't show every extreme that they name: `fields`: finite values. `w_qkv`: finite values.
All inputs are finite; a program needn't handle non-finite values. No bound on the sum of `land_mask` on one device may be relied on, other than what follows from the above.
Results may differ from the reference program's by a relative error of at most 0.02.
Values may be sent and summed in bfloat16 or wider, within the bound.
No kernel may reach another device: no remote copies, remote signals or barrier semaphores. Data moves between devices by JAX's collectives and lax.ppermute only.
A program may use at most 64 MiB of HBM per device.

```python
import jax
import jax.numpy as jnp
from jax import lax

C = 192
HEADS = 6
FF = 768
WZ = 2
WLAT = 6
WLON = 12
Z = 2
LAT = 18
MICRO = 4
LON = 768
BLOCKS = 8


def draw_fields(key, part):
    shape_five = (MICRO, Z, LAT, LON, C)
    key_one = jax.random.fold_in(jax.random.fold_in(key, 11), 0)
    values = jnp.clip(jax.random.normal(key_one, shape_five, jnp.float32), -6.0, 6.0)
    return values.reshape(MICRO, Z, LAT, LON * C).astype(jnp.bfloat16)


def draw_w_qkv(key, part):
    key_one = jax.random.fold_in(jax.random.fold_in(key, 23), 0)
    base = jnp.clip(jax.random.normal(key_one, (BLOCKS, C, 3 * C), jnp.float32), -4.0, 4.0) * C ** (-0.5)
    return jnp.clip(base, -3.0, 3.0).astype(jnp.bfloat16)


def touch_ends(result, rng, smallest, top_value):
    index_at = [jax.random.randint(jax.random.fold_in(rng, axis), (), 0, length) for axis, length in enumerate(result.shape)]
    main_axis = result.shape.index(max(result.shape))
    next_to = index_at[:main_axis] + [(index_at[main_axis] + 1) % result.shape[main_axis]] + index_at[main_axis + 1:]
    return result.at[tuple(index_at)].set(smallest).at[tuple(next_to)].set(top_value)


def block_scale(rng, shape, cuts, low, top_value):
    gain = 1.0
    for dim, shards_of in cuts:
        steps = jax.random.uniform(jax.random.fold_in(jax.random.fold_in(rng, 6), dim), (shards_of,), jnp.float32, low / len(cuts), top_value / len(cuts))
        gain = gain * jnp.repeat(jnp.exp(steps), shape[dim] // shards_of).reshape((-1,) + (1,) * (len(shape) - 1 - dim))
    return gain


def centred(rng, extent, scale, bound, pieces=(), held_as=jnp.bfloat16):
    loudness = block_scale(rng, extent, pieces, -0.22, 0.18) if pieces else 1.0
    drawn = jax.random.normal(rng, extent, jnp.float32) * scale * loudness
    return jnp.minimum(jnp.maximum(drawn, -bound), bound).astype(held_as)


def setup_inputs(seed: int = 0) -> dict:
    splits = jax.random.split(jax.random.key(seed), 8)
    return {
        "fields": draw_fields(jax.random.fold_in(splits[7], 71), 0),
        "land_mask": touch_ends((jax.random.randint(splits[1], (LAT, LON), 0, 3) < 1).astype(jnp.int32), jax.random.fold_in(splits[1], 1), 0, 1),
        "land_vector": centred(splits[2], (C,), 1.0, 4.0, (), jnp.float32),
        "w_qkv": draw_w_qkv(jax.random.fold_in(splits[7], 71), 0),
        "w_proj": centred(splits[4], (BLOCKS, C, C), C ** -0.5, 0.4375, ((0, 8),)),
        "w_up": centred(splits[5], (BLOCKS, C, FF), C ** -0.5, 0.4375, ((0, 8),)),
        "w_down": centred(splits[6], (BLOCKS, FF, C), FF ** -0.5, 0.21875, ((0, 8),)),
    }


def normalize(values):
    center = values - lax.optimization_barrier(jnp.mean(values, axis=-1, keepdims=True))
    spread = lax.optimization_barrier(jnp.mean(center * center, axis=-1, keepdims=True))
    return center * lax.rsqrt(spread + 1e-05)

def region_ids(length, window, shifted):
    places = jnp.arange(length)
    labels = jnp.where(places < length - window, 0, jnp.where(places < length - window // 2, 1, 2))
    return labels * shifted

def window_attend(normed, weight_qkv, weight_proj, shifted):
    levels, rows, columns, width = normed.shape
    head_size = width // HEADS
    lev_blocks, lat_blocks, lon_blocks = (levels // WZ, rows // WLAT, columns // WLON)
    points = WZ * WLAT * WLON
    qkv = jnp.einsum('zlwc,cd->zlwd', normed.astype(jnp.float32), weight_qkv.astype(jnp.float32)).astype(jnp.bfloat16)
    parts = qkv.reshape(lev_blocks, WZ, lat_blocks, WLAT, lon_blocks, WLON, 3, HEADS, head_size)
    parts = parts.transpose(6, 0, 2, 4, 7, 1, 3, 5, 8).reshape(3, lev_blocks, lat_blocks, lon_blocks, HEADS, points, head_size)
    level_ids = region_ids(levels, WZ, shifted).reshape(lev_blocks, WZ)
    row_ids = region_ids(rows, WLAT, shifted).reshape(lat_blocks, WLAT)
    labels = level_ids[:, None, :, None] * 3 + row_ids[None, :, None, :]
    labels = jnp.broadcast_to(labels[..., None], (lev_blocks, lat_blocks, WZ, WLAT, WLON)).reshape(lev_blocks, lat_blocks, points)
    allowed = labels[:, :, None, None, :, None] == labels[:, :, None, None, None, :]
    scores = jnp.einsum('abcdqe,abcdke->abcdqk', parts[0].astype(jnp.float32), parts[1].astype(jnp.float32)) * head_size ** (-0.5)
    scores = jnp.where(allowed, scores, -1e+30)
    highest = lax.optimization_barrier(jnp.max(scores, axis=-1, keepdims=True))
    raised = jnp.exp(scores - highest)
    probs = (raised / lax.optimization_barrier(jnp.sum(raised, axis=-1, keepdims=True))).astype(jnp.bfloat16)
    attended = jnp.einsum('abcdqk,abcdke->abcdqe', probs.astype(jnp.float32), parts[2].astype(jnp.float32)).astype(jnp.bfloat16)
    attended = attended.reshape(lev_blocks, lat_blocks, lon_blocks, HEADS, WZ, WLAT, WLON, head_size)
    attended = attended.transpose(0, 4, 1, 5, 2, 6, 3, 7).reshape(levels, rows, columns, width)
    return jnp.einsum('zlwc,cd->zlwd', attended.astype(jnp.float32), weight_proj.astype(jnp.float32))

def run_block(tokens, weight_qkv, weight_proj, weight_up, weight_down, shifted):
    moves = (WZ // 2 * shifted, WLAT // 2 * shifted, WLON // 2 * shifted)
    values = tokens.astype(jnp.float32)
    rolled = jnp.roll(values, (-moves[0], -moves[1], -moves[2]), (0, 1, 2))
    normed = normalize(rolled).astype(jnp.bfloat16)
    projected = window_attend(normed, weight_qkv, weight_proj, shifted)
    projected = jnp.roll(projected, (moves[0], moves[1], moves[2]), (0, 1, 2))
    residual = values + projected
    normed_two = normalize(residual).astype(jnp.bfloat16)
    hidden = jax.nn.gelu(jnp.einsum('zlwc,cf->zlwf', normed_two.astype(jnp.float32), weight_up.astype(jnp.float32)), approximate=False).astype(jnp.bfloat16)
    output = residual + jnp.einsum('zlwf,fc->zlwc', hidden.astype(jnp.float32), weight_down.astype(jnp.float32))
    return output.astype(jnp.bfloat16)

def reference(fields, land_mask, land_vector, w_qkv, w_proj, w_up, w_down):
    inputs_grid = fields.astype(jnp.float32).reshape(MICRO, Z, LAT, LON, C)
    inputs_grid = inputs_grid + land_mask.astype(jnp.float32)[None, None, :, :, None] * land_vector.astype(jnp.float32)
    stream = inputs_grid.astype(jnp.bfloat16)
    results = []
    for block_index in range(BLOCKS):
        shifted = block_index % 2

        def apply_block(tokens, block_index=block_index, shifted=shifted):
            return run_block(tokens, w_qkv[block_index], w_proj[block_index], w_up[block_index], w_down[block_index], shifted)
        stream = lax.map(apply_block, stream)
        results.append(stream.reshape(MICRO, Z, LAT, LON * C))
    return jnp.stack(results)
```

```python
import functools

import jax
import jax.numpy as jnp
import numpy as np
from jax import lax
from jax.experimental import pallas as pl
from jax.experimental.pallas import tpu as pltpu
from jax.sharding import PartitionSpec as P

HEADS = 6
WZ = 2
WLAT = 6
WLON = 12
HALF = WLON // 2
LOG2E = 1.4426950408889634


def normalize(values):
    center = values - jnp.mean(values, axis=-1, keepdims=True)
    spread = jnp.mean(center * center, axis=-1, keepdims=True)
    return center * lax.rsqrt(spread + 1e-05)


def window_bias(levels, rows):
    lat_blocks = rows // WLAT
    index = np.arange(WLAT * levels * HALF)
    row, level = index // (levels * HALF), index // HALF % levels
    row = row[None] + WLAT * np.arange(lat_blocks)[:, None]

    def label(place, length, window):
        return np.where(place < length - window, 0, np.where(place < length - window // 2, 1, 2))

    labels = label(level, levels, WZ)[None] * 3 + label(row, rows, WLAT)
    keys = np.concatenate([labels, labels], 1)
    return np.where(labels[:, :, None] == keys[:, None, :], 0.0, -1e30).astype(np.float32)


def block_kernel(shifted, own_ref, par_ref, wqkv_ref, wproj_ref, wup_ref, wdown_ref, bias_ref, out_ref):
    tokens, width = own_ref.shape
    head_size = width // HEADS
    piece = bias_ref.shape[1]
    move = piece // 2
    x = own_ref[...].astype(jnp.float32)
    y = par_ref[...].astype(jnp.float32)
    if shifted:
        x = pltpu.roll(x, tokens - move, 0)
        y = pltpu.roll(y, tokens - move, 0)
    nx = normalize(x).astype(jnp.bfloat16)
    ny = normalize(y).astype(jnp.bfloat16)
    f32 = jnp.float32
    qkv = jnp.dot(nx, wqkv_ref[...], preferred_element_type=f32)
    kv = jnp.dot(ny, wqkv_ref[:, 256:], preferred_element_type=f32)
    channel_head = lax.broadcasted_iota(jnp.int32, (1, width), 1) // head_size
    attended = []
    scale = head_size ** (-0.5) * LOG2E
    for w in range(tokens // piece):
        at = slice(w * piece, (w + 1) * piece)
        q = qkv[at, :width]
        qm = jnp.concatenate([jnp.where(channel_head == h, q, 0.0) for h in range(HEADS)], 0).astype(jnp.bfloat16)
        k = jnp.concatenate([qkv[at, 256 : 256 + width], kv[at, :width]], 0).astype(jnp.bfloat16)
        v = jnp.concatenate([qkv[at, 512 : 512 + width], kv[at, 256 : 256 + width]], 0).astype(jnp.bfloat16)
        s = lax.dot_general(qm, k, (((1,), (1,)), ((), ())), preferred_element_type=f32)
        s = s * scale
        if shifted:
            s = (s.reshape(HEADS, piece, 2 * piece) + bias_ref[w][None]).reshape(HEADS * piece, 2 * piece)
        e = jnp.exp2(s - jnp.max(s, axis=-1, keepdims=True))
        r = 1.0 / jnp.sum(e, axis=-1, keepdims=True)
        o = jnp.dot(e.astype(jnp.bfloat16), v, preferred_element_type=f32) * r
        total = jnp.zeros((piece, width), f32)
        for h in range(HEADS):
            total = jnp.where(channel_head == h, o[h * piece : (h + 1) * piece], total)
        attended.append(total)
    a = jnp.concatenate(attended, 0).astype(jnp.bfloat16)
    residual = x + jnp.dot(a, wproj_ref[...], preferred_element_type=f32)
    n2 = normalize(residual).astype(jnp.bfloat16)
    u = jnp.dot(n2, wup_ref[...], preferred_element_type=f32)
    hidden = (0.5 * u * (1.0 + lax.erf(u * (0.5**0.5)))).astype(jnp.bfloat16)
    result = residual + jnp.dot(hidden, wdown_ref[...], preferred_element_type=f32)
    if shifted:
        result = pltpu.roll(result, move, 0)
    out_ref[...] = result.astype(jnp.bfloat16)


def run_block(own, partner, weights, bias, shifted, interpret=False):
    return pl.pallas_call(
        functools.partial(block_kernel, shifted),
        out_shape=jax.ShapeDtypeStruct(own.shape, jnp.bfloat16),
        compiler_params=pltpu.CompilerParams(vmem_limit_bytes=40 * 2**20),
        interpret=interpret,
        name="odd_block" if shifted else "even_block",
    )(own, partner, *weights, bias)


def on_device(fields, land_mask, land_vector, w_qkv, w_proj, w_up, w_down):
    micro_count, levels, rows, flat_width = fields.shape
    width = land_vector.shape[0]
    tile_count, section_count = lax.axis_size("tile"), lax.axis_size("section")
    section = lax.axis_index("section")
    core, chip = section % 2, section // 2
    chips = section_count // 2
    tokens = rows * levels * HALF

    mates = [(s, s ^ 1) for s in range(section_count)]
    onward = [(s, s + 2) for s in range(section_count - 2)]
    across = []
    for t in range(tile_count):
        for c in range(chips):
            west, east = t * section_count + 2 * c + 1, (t + 1) % tile_count * section_count + 2 * c
            across += [(west, east), (east, west)]

    pack = jnp.concatenate([jnp.concatenate([w_qkv[0], w_proj[0]], 1), w_up[0], w_down[0].T], 0)
    other = lax.ppermute(pack, "section", mates)

    def unpack(p):
        qkvp, up, down = p[:width], p[width : 2 * width], p[2 * width :].T
        parts = [jnp.pad(qkvp[:, i * width : (i + 1) * width], ((0, 0), (0, 256 - width))) for i in range(3)]
        return jnp.concatenate(parts, 1), qkvp[:, 3 * width :], up, down

    even_weights = unpack(jnp.where(core == 0, pack, other))
    odd_weights = unpack(jnp.where(core == 0, other, pack))
    bias = jnp.asarray(window_bias(levels, rows))

    grid = fields.reshape(micro_count, levels, rows, WLON, width).astype(jnp.float32)
    grid = grid + land_mask.astype(jnp.float32)[None, None, :, :, None] * land_vector
    grid = grid.astype(jnp.bfloat16).reshape(micro_count, levels, rows, 2, HALF, width)
    grid = grid.transpose(0, 3, 2, 1, 4, 5).reshape(micro_count, 2, tokens, width)
    start_own = jnp.where(core == 0, grid[:, 0], grid[:, 1])
    start_partner = jnp.where(core == 0, grid[:, 1], grid[:, 0])

    evens, odds = [], []
    own, partner = start_own[0], start_partner[0]
    for tick in range(micro_count + chips - 1):
        even = run_block(own, partner, even_weights, bias, False)
        odd = run_block(even, lax.ppermute(even, ("tile", "section"), across), odd_weights, bias, True)
        evens.append(even)
        odds.append(odd)
        if tick == micro_count + chips - 2:
            break
        own = lax.ppermute(odd, "section", onward)
        partner = lax.ppermute(own, "section", mates)
        if tick + 1 < micro_count:
            own = jnp.where(chip == 0, start_own[tick + 1], own)
            partner = jnp.where(chip == 0, start_partner[tick + 1], partner)

    evens = lax.dynamic_slice_in_dim(jnp.stack(evens), chip, micro_count, 0)
    odds = lax.dynamic_slice_in_dim(jnp.stack(odds), chip, micro_count, 0)
    mine = jnp.where(core == 0, evens, odds)
    theirs = lax.ppermute(jnp.where(core == 0, odds, evens), "section", mates)
    halves = jnp.stack([jnp.where(core == 0, mine, theirs), jnp.where(core == 0, theirs, mine)], 1)
    out = halves.reshape(micro_count, 2, rows, levels, HALF, width).transpose(0, 3, 2, 1, 4, 5)
    return out.reshape(1, micro_count, levels, rows, flat_width)


def solution(mesh):
    in_specs = (
        P(None, None, None, "tile"),
        P(None, "tile"),
        P(),
        P("section", None, None),
        P("section", None, None),
        P("section", None, None),
        P("section", None, None),
    )
    out_specs = P("section", None, None, None, "tile")
    return jax.shard_map(on_device, mesh=mesh, in_specs=in_specs, out_specs=out_specs, check_vma=False)
```

```python
import functools

import jax
import jax.numpy as jnp
import numpy as np
from jax import lax
from jax.experimental import pallas as pl
from jax.experimental.pallas import tpu as pltpu
from jax.sharding import PartitionSpec as P

HEADS = 6
WZ = 2
WLAT = 6
WLON = 12
HALF = WLON // 2
STAGE = 4
REACH = 2
LOG2E = 1.4426950408889634
LANES = 128
VMEM_LIMIT = 56 * 2**20


def normalize(values):
    center = values - jnp.mean(values, axis=-1, keepdims=True)
    spread = jnp.mean(center * center, axis=-1, keepdims=True)
    return center * lax.rsqrt(spread + 1e-05)


def window_bias(levels, rows):
    lat_blocks = rows // WLAT
    index = np.arange(WLAT * levels * HALF)
    row, level = index // (levels * HALF), index // HALF % levels
    row = row[None] + WLAT * np.arange(lat_blocks)[:, None]

    def label(place, length, window):
        return np.where(place < length - window, 0, np.where(place < length - window // 2, 1, 2))

    labels = label(level, levels, WZ)[None] * 3 + label(row, rows, WLAT)
    keys = np.concatenate([labels, labels], 1)
    return np.where(labels[:, :, None] == keys[:, None, :], 0.0, -1e30).astype(np.float32)


def pack_tile(west, east):
    return jnp.concatenate(
        [west[:, :LANES], east[:, :LANES], jnp.concatenate([west[:, LANES:], east[:, LANES:]], 1)], 0
    )


def unpack_tile(packed):
    tokens = packed.shape[0] // 3
    last = packed[2 * tokens :]
    side = last.shape[1] // 2
    west = jnp.concatenate([packed[:tokens], last[:, :side]], 1)
    east = jnp.concatenate([packed[tokens : 2 * tokens], last[:, side:]], 1)
    return west, east


def prepare_kernel(micro_ref, fields_ref, mask_ref, vector_ref, wqkv_ref, wproj_ref, wup_ref, wdown_ref,
                   tile_ref, pack_ref, grid_ref):
    _, levels, rows, _ = fields_ref.shape
    width = vector_ref.shape[1]
    mask = mask_ref[...].astype(jnp.float32)
    vector = vector_ref[...]
    step = levels * HALF
    for level in range(levels):
        for column in range(WLON):
            piece = fields_ref[0, level, :, column * width : (column + 1) * width].astype(jnp.float32)
            piece = piece + mask[:, column : column + 1] * vector
            half, inside = divmod(column, HALF)
            at = pl.ds(level * HALF + inside, rows, stride=step)
            grid_ref[2 * half, at, :] = piece[:, :LANES]
            grid_ref[2 * half + 1, at, :] = jnp.concatenate([piece[:, LANES:]] * 2, 1)
    tokens, side = rows * step, width - LANES
    tile_ref[:tokens] = grid_ref[0].astype(jnp.bfloat16)
    tile_ref[tokens : 2 * tokens] = grid_ref[2].astype(jnp.bfloat16)
    lane = lax.broadcasted_iota(jnp.int32, (1, LANES), 1)
    tile_ref[2 * tokens :] = jnp.where(lane < side, grid_ref[1], grid_ref[3]).astype(jnp.bfloat16)
    side = 256 - width
    for i in range(3):
        pack_ref[:, 256 * i : 256 * i + 256] = jnp.concatenate(
            [wqkv_ref[0, :, i * width : (i + 1) * width], wproj_ref[0, :, i * side : (i + 1) * side]], 1
        )
    hidden = wup_ref.shape[2]
    pack_ref[:, 768 : 768 + hidden] = wup_ref[0]
    at = 768 + hidden
    for i in range(hidden // width):
        pack_ref[:, at + LANES * i : at + LANES * (i + 1)] = wdown_ref[0, i * width : (i + 1) * width, :LANES]
    at += hidden // width * LANES
    for i in range(0, hidden // width, 2):
        pack_ref[:, at + side * i : at + side * (i + 2)] = jnp.concatenate(
            [wdown_ref[0, (i + j) * width : (i + j + 1) * width, LANES:] for j in range(2)], 1
        )


def prepare(micro, fields, land_mask, land_vector, weights):
    _, levels, rows, flat = fields.shape
    width = land_vector.shape[1]
    tokens = rows * levels * HALF
    whole = lambda a: pl.BlockSpec(a.shape, lambda i, m: (0,) * a.ndim)
    return pl.pallas_call(
        prepare_kernel,
        out_shape=(
            jax.ShapeDtypeStruct((3 * tokens, LANES), jnp.bfloat16),
            jax.ShapeDtypeStruct((width, 2304), jnp.bfloat16),
        ),
        grid_spec=pltpu.PrefetchScalarGridSpec(
            num_scalar_prefetch=1,
            grid=(1,),
            in_specs=[pl.BlockSpec((1, levels, rows, flat), lambda i, m: (m[0], 0, 0, 0))]
            + [whole(a) for a in (land_mask, land_vector, *weights)],
            out_specs=(
                pl.BlockSpec((3 * tokens, LANES), lambda i, m: (0, 0)),
                pl.BlockSpec((width, 2304), lambda i, m: (0, 0)),
            ),
            scratch_shapes=[pltpu.VMEM((4, tokens, LANES), jnp.float32)],
        ),
        compiler_params=pltpu.CompilerParams(vmem_limit_bytes=VMEM_LIMIT),
        name="prepare",
    )(micro, fields, land_mask, land_vector, *weights)


def stage_kernel(place_ref, t0, t1, t2, t3, t4, w0, w1, w2, w3, bias_ref, last_ref, outs_ref,
                 xa, xb, q_ref, k_ref, v_ref, wqkv_ref, wproj_ref, wup_ref, wdown_ref):
    f32, bf16 = jnp.float32, jnp.bfloat16
    halves, tokens, width = xa.shape
    head_size = width // HEADS
    windows, piece, _ = bias_ref.shape
    move = piece // 2
    place = place_ref[0]
    side = 256 - width
    hidden = wup_ref.shape[2]

    for i, ref in enumerate((t0, t1, t2, t3, t4)):
        west, east = unpack_tile(ref[...].astype(f32))
        xa[2 * i] = west.astype(bf16)
        xa[2 * i + 1] = east.astype(bf16)
    for i, ref in enumerate((w0, w1, w2, w3)):
        at = place ^ i
        wqkv_ref[at] = ref[:, :768]
        wproj_ref[at] = jnp.concatenate([ref[:, 256 * j + width : 256 * j + 256] for j in range(3)], 1)
        wup_ref[at] = ref[:, 768 : 768 + hidden]
        base = 768 + hidden
        rest = base + hidden // width * LANES
        for j in range(hidden // width):
            wdown_ref[at, j * width : (j + 1) * width, :] = jnp.concatenate(
                [ref[:, base + LANES * j : base + LANES * (j + 1)], ref[:, rest + side * j : rest + side * (j + 1)]], 1
            )

    channel_head = lax.broadcasted_iota(jnp.int32, (1, width), 1) // head_size
    scale = head_size ** (-0.5) * LOG2E
    ones = jnp.ones((2 * piece, side), f32)

    for b in range(STAGE):
        shifted = b % 2 == 1
        source, target = (xa, xb) if b % 2 == 0 else (xb, xa)

        def load(h, source=source, shifted=shifted):
            x = source[h].astype(f32)
            return pltpu.roll(x, tokens - move, 0) if shifted else x

        def pair(i, carry, b=b, load=load):
            kv = []
            for j in range(2):
                h = b + 2 * i + j
                qkv = jnp.dot(normalize(load(h)).astype(bf16), wqkv_ref[b], preferred_element_type=f32)
                q_ref[h] = qkv[:, :width] * scale
                kv.append((qkv[:, 256 : 256 + width], qkv[:, 512 : 512 + width]))
            for w in range(windows):
                at = slice(w * piece, (w + 1) * piece)
                k_ref[i, w] = jnp.concatenate([kv[0][0][at], kv[1][0][at]], 0).astype(bf16)
                v = jnp.concatenate([kv[0][1][at], kv[1][1][at]], 0)
                v_ref[i, w] = jnp.concatenate([v, ones], 1).astype(bf16)
            return carry

        def attend(h, carry, b=b, load=load, target=target, shifted=shifted):
            i = (h - b) // 2
            x = load(h)
            attended = []
            for w in range(windows):
                q = q_ref[h, w * piece : (w + 1) * piece, :]
                qm = jnp.concatenate([jnp.where(channel_head == n, q, 0.0) for n in range(HEADS)], 0).astype(bf16)
                s = lax.dot_general(qm, k_ref[i, w], (((1,), (1,)), ((), ())), preferred_element_type=f32)
                if shifted:
                    s = (s.reshape(HEADS, piece, 2 * piece) + bias_ref[w][None]).reshape(HEADS * piece, 2 * piece)
                e = jnp.exp2(s - jnp.max(s, axis=-1, keepdims=True)).astype(bf16)
                o = jnp.dot(e, v_ref[i, w], preferred_element_type=f32)
                o = o[:, :width] * (1.0 / o[:, width : width + 1])
                total = o[:piece]
                for n in range(1, HEADS):
                    total = jnp.where(channel_head == n, o[n * piece : (n + 1) * piece], total)
                attended.append(total)
            a = jnp.concatenate(attended, 0).astype(bf16)
            residual = x + jnp.dot(a, wproj_ref[b], preferred_element_type=f32)
            n2 = normalize(residual).astype(bf16)
            u = jnp.dot(n2, wup_ref[b], preferred_element_type=f32)
            g = (0.5 * u * (1.0 + lax.erf(u * (0.5**0.5)))).astype(bf16)
            y = residual + jnp.dot(g, wdown_ref[b], preferred_element_type=f32)
            if shifted:
                y = pltpu.roll(y, move, 0)
            target[h] = y.astype(bf16)
            return carry

        lax.fori_loop(0, halves // 2 - b, pair, 0)
        lax.fori_loop(1 + b, halves - 1 - b, attend, 0)
        west, east = target[halves // 2 - 1].astype(f32), target[halves // 2].astype(f32)
        packed = pack_tile(west, east).astype(bf16)
        outs_ref[place ^ b] = packed
        if b == STAGE - 1:
            last_ref[...] = packed


def run_stage(place, tiles, weights, bias):
    packed_tokens = tiles[0].shape[0]
    tokens = packed_tokens // 3
    width = weights[0].shape[0]
    halves = 2 * len(tiles)
    windows, piece, _ = bias.shape
    vmem = pl.BlockSpec(memory_space=pltpu.VMEM)
    bf16, f32 = jnp.bfloat16, jnp.float32
    return pl.pallas_call(
        stage_kernel,
        out_shape=(
            jax.ShapeDtypeStruct((packed_tokens, LANES), bf16),
            jax.ShapeDtypeStruct((STAGE, packed_tokens, LANES), bf16),
        ),
        in_specs=[pl.BlockSpec(memory_space=pltpu.SMEM)] + [vmem] * (len(tiles) + len(weights) + 1),
        out_specs=(vmem, vmem),
        scratch_shapes=[
            pltpu.VMEM((halves, tokens, width), bf16),
            pltpu.VMEM((halves, tokens, width), bf16),
            pltpu.VMEM((halves, tokens, width), f32),
            pltpu.VMEM((halves // 2, windows, 2 * piece, width), bf16),
            pltpu.VMEM((halves // 2, windows, 2 * piece, 256), bf16),
            pltpu.VMEM((STAGE, width, 768), bf16),
            pltpu.VMEM((STAGE, width, width), bf16),
            pltpu.VMEM((STAGE, width, 768), bf16),
            pltpu.VMEM((STAGE, 768, width), bf16),
        ],
        compiler_params=pltpu.CompilerParams(vmem_limit_bytes=VMEM_LIMIT),
        name="stage",
    )(place, *tiles, *weights, bias)


def finish_kernel(place_ref, o0, o1, o2, o3, out_ref, grid_ref):
    _, _, levels, rows, _ = out_ref.shape
    tokens = grid_ref.shape[1]
    step = levels * HALF
    width = out_ref.shape[4] // WLON
    side = width - LANES
    for i, ref in enumerate((o0, o1, o2, o3)):
        packed = ref[...].astype(jnp.float32)
        for part in range(3):
            grid_ref[part] = packed[part * tokens : (part + 1) * tokens]
        micro = place_ref[0] ^ i
        for level in range(levels):
            for column in range(WLON):
                half, inside = divmod(column, HALF)
                at = pl.ds(level * HALF + inside, rows, stride=step)
                rest = grid_ref[2, at, :][:, half * side : (half + 1) * side]
                piece = jnp.concatenate([grid_ref[half, at, :], rest], 1)
                out_ref[0, micro, level, :, column * width : (column + 1) * width] = piece.astype(jnp.bfloat16)


def finish(place, pieces, shape):
    tokens = pieces[0].shape[0] // 3
    vmem = pl.BlockSpec(memory_space=pltpu.VMEM)
    return pl.pallas_call(
        finish_kernel,
        out_shape=jax.ShapeDtypeStruct(shape, jnp.bfloat16),
        in_specs=[pl.BlockSpec(memory_space=pltpu.SMEM)] + [vmem] * len(pieces),
        out_specs=vmem,
        scratch_shapes=[pltpu.VMEM((3, tokens, LANES), jnp.float32)],
        compiler_params=pltpu.CompilerParams(vmem_limit_bytes=VMEM_LIMIT),
        name="finish",
    )(place, *pieces)


def on_device(fields, land_mask, land_vector, w_qkv, w_proj, w_up, w_down):
    micro_count, levels, rows, flat_width = fields.shape
    width = land_vector.shape[0]
    tile_count, section_count = lax.axis_size("tile"), lax.axis_size("section")
    section = lax.axis_index("section")
    place = (section % STAGE).astype(jnp.int32).reshape(1)
    axes = ("tile", "section")

    def exchange(value, bit):
        return lax.ppermute(value, "section", [(s, s ^ bit) for s in range(section_count)])

    def shift(value, tiles, stages):
        pairs = [
            (t * section_count + s, (t + tiles) % tile_count * section_count + s + stages * STAGE)
            for t in range(tile_count)
            for s in range(STAGE)
        ]
        return lax.ppermute(value, axes, pairs)

    tile, pack = prepare(place, fields, land_mask, land_vector.reshape(1, width), (w_qkv, w_proj, w_up, w_down))
    bias = jnp.asarray(window_bias(levels, rows))

    far = exchange(pack, 2)
    offsets = range(-REACH, REACH + 1)
    tiles = [tile if d == 0 else shift(tile, -d, 0) for d in offsets]
    weights = (pack, exchange(pack, 1), far, exchange(far, 1))

    last, early = run_stage(place, tiles, weights, bias)
    tiles = [shift(last, -d, 1) for d in offsets]
    _, late = run_stage(place, tiles, weights, bias)
    outs = jnp.where(section < STAGE, early, late)

    pieces = [outs[0]] + [exchange(outs[i], i) for i in range(1, STAGE)]
    return finish(place, pieces, (1, micro_count, levels, rows, flat_width))


def solution(mesh):
    in_specs = (
        P(None, None, None, "tile"),
        P(None, "tile"),
        P(),
        P("section", None, None),
        P("section", None, None),
        P("section", None, None),
        P("section", None, None),
    )
    out_specs = P("section", None, None, None, "tile")
    return jax.shard_map(on_device, mesh=mesh, in_specs=in_specs, out_specs=out_specs, check_vma=False)
```

```python
import functools

import jax
import jax.numpy as jnp
import numpy as np
from jax import lax
from jax.experimental import pallas as pl
from jax.experimental.pallas import tpu as pltpu
from jax.sharding import PartitionSpec as P

HEADS = 6
WZ = 2
WLAT = 6
WLON = 12
HALF = WLON // 2
STAGE = 4
REACH = 2
LOG2E = 1.4426950408889634
LANES = 128
VMEM_LIMIT = 56 * 2**20


def normalize(values):
    center = values - jnp.mean(values, axis=-1, keepdims=True)
    spread = jnp.mean(center * center, axis=-1, keepdims=True)
    return center * lax.rsqrt(spread + 1e-05)


def window_bias(levels, rows):
    lat_blocks = rows // WLAT
    index = np.arange(WLAT * levels * HALF)
    row, level = index // (levels * HALF), index // HALF % levels
    row = row[None] + WLAT * np.arange(lat_blocks)[:, None]

    def label(place, length, window):
        return np.where(place < length - window, 0, np.where(place < length - window // 2, 1, 2))

    labels = label(level, levels, WZ)[None] * 3 + label(row, rows, WLAT)
    keys = np.concatenate([labels, labels], 1)
    return np.where(labels[:, :, None] == keys[:, None, :], 0.0, -1e30).astype(np.float32)


def pack_tile(west, east):
    return jnp.concatenate(
        [west[:, :LANES], east[:, :LANES], jnp.concatenate([west[:, LANES:], east[:, LANES:]], 1)], 0
    )


def unpack_tile(packed):
    tokens = packed.shape[0] // 3
    last = packed[2 * tokens :]
    side = last.shape[1] // 2
    west = jnp.concatenate([packed[:tokens], last[:, :side]], 1)
    east = jnp.concatenate([packed[tokens : 2 * tokens], last[:, side:]], 1)
    return west, east


def prepare_kernel(micro_ref, fields_ref, mask_ref, vector_ref, wqkv_ref, wproj_ref, wup_ref, wdown_ref,
                   tile_ref, pack_ref, grid_ref):
    _, levels, rows, _ = fields_ref.shape
    width = vector_ref.shape[1]
    mask = mask_ref[...].astype(jnp.float32)
    vector = vector_ref[...]
    step = levels * HALF
    for level in range(levels):
        for column in range(WLON):
            piece = fields_ref[0, level, :, column * width : (column + 1) * width].astype(jnp.float32)
            piece = piece + mask[:, column : column + 1] * vector
            half, inside = divmod(column, HALF)
            at = pl.ds(level * HALF + inside, rows, stride=step)
            grid_ref[2 * half, at, :] = piece[:, :LANES]
            grid_ref[2 * half + 1, at, :] = jnp.concatenate([piece[:, LANES:]] * 2, 1)
    tokens, side = rows * step, width - LANES
    tile_ref[:tokens] = grid_ref[0].astype(jnp.bfloat16)
    tile_ref[tokens : 2 * tokens] = grid_ref[2].astype(jnp.bfloat16)
    lane = lax.broadcasted_iota(jnp.int32, (1, LANES), 1)
    tile_ref[2 * tokens :] = jnp.where(lane < side, grid_ref[1], grid_ref[3]).astype(jnp.bfloat16)
    side = 256 - width
    for i in range(3):
        pack_ref[:, 256 * i : 256 * i + 256] = jnp.concatenate(
            [wqkv_ref[0, :, i * width : (i + 1) * width], wproj_ref[0, :, i * side : (i + 1) * side]], 1
        )
    hidden = wup_ref.shape[2]
    pack_ref[:, 768 : 768 + hidden] = wup_ref[0]
    pack_ref[:, 768 + hidden :] = wdown_ref[0]


def prepare(micro, fields, land_mask, land_vector, weights):
    _, levels, rows, flat = fields.shape
    width = land_vector.shape[1]
    tokens = rows * levels * HALF
    whole = lambda a: pl.BlockSpec(a.shape, lambda i, m: (0,) * a.ndim)
    return pl.pallas_call(
        prepare_kernel,
        out_shape=(
            jax.ShapeDtypeStruct((3 * tokens, LANES), jnp.bfloat16),
            jax.ShapeDtypeStruct((width, 2304), jnp.bfloat16),
        ),
        grid_spec=pltpu.PrefetchScalarGridSpec(
            num_scalar_prefetch=1,
            grid=(1,),
            in_specs=[pl.BlockSpec((1, levels, rows, flat), lambda i, m: (m[0], 0, 0, 0))]
            + [whole(a) for a in (land_mask, land_vector, *weights)],
            out_specs=(
                pl.BlockSpec((3 * tokens, LANES), lambda i, m: (0, 0)),
                pl.BlockSpec((width, 2304), lambda i, m: (0, 0)),
            ),
            scratch_shapes=[pltpu.VMEM((4, tokens, LANES), jnp.float32)],
        ),
        compiler_params=pltpu.CompilerParams(vmem_limit_bytes=VMEM_LIMIT),
        name="prepare",
    )(micro, fields, land_mask, land_vector, *weights)


def stage_kernel(place_ref, t0, t1, t2, t3, t4, w0, w1, w2, w3, bias_ref, last_ref, outs_ref,
                 xa, xb, q_ref, k_ref, v_ref, w_ref, wproj_ref, low_ref, high_ref):
    f32, bf16 = jnp.float32, jnp.bfloat16
    halves, tokens, width = xa.shape
    head_size = width // HEADS
    windows, piece, _ = bias_ref.shape
    move = piece // 2
    place = place_ref[0]
    side = 256 - width
    hidden = (w_ref.shape[2] - 768) // 2

    for i, ref in enumerate((w0, w1, w2, w3)):
        at = place ^ i
        w_ref[at] = ref[...]
        wproj_ref[at] = jnp.concatenate([ref[:, 256 * j + width : 256 * j + 256] for j in range(3)], 1)

    channel_head = lax.broadcasted_iota(jnp.int32, (1, width), 1) // head_size
    scale = head_size ** (-0.5) * LOG2E
    ones = jnp.ones((2 * piece, 256 - width), f32)

    def load_tiles():
        for i, ref in enumerate((t0, t1, t2, t3, t4)):
            west, east = unpack_tile(ref[...].astype(f32))
            xa[2 * i] = west.astype(bf16)
            xa[2 * i + 1] = east.astype(bf16)

    def select_heads(parts, first, lanes):
        total = parts[0]
        for n in range(1, len(parts)):
            total = jnp.where(channel_head[:, first : first + lanes] == first // head_size + n, parts[n], total)
        return total

    def window_attention(h, i, w, shifted, exact):
        q = q_ref[h, w * piece : (w + 1) * piece, :]
        qm = jnp.concatenate([jnp.where(channel_head == n, q, 0.0) for n in range(HEADS)], 0).astype(bf16)
        s = lax.dot_general(qm, k_ref[i, w], (((1,), (1,)), ((), ())), preferred_element_type=f32)
        if shifted:
            s = (s.reshape(HEADS, piece, 2 * piece) + bias_ref[w][None]).reshape(HEADS * piece, 2 * piece)
        if exact:
            s = s - jnp.max(s, axis=-1, keepdims=True)
        o = jnp.dot(jnp.exp2(s).astype(bf16), v_ref[i, w], preferred_element_type=f32)
        heads = [o[n * piece : (n + 1) * piece] for n in range(HEADS)]
        full = LANES // head_size
        tops = [select_heads([x[:, :LANES] for x in heads[:full]], 0, LANES),
                select_heads([x[:, LANES:width] for x in heads[full:]], LANES, width - LANES)]
        side = 256 - width
        ends = [x[:, LANES:] for x in heads]
        odd = channel_head[:, :LANES] % 2 == 1
        couples = [jnp.where(odd, ends[n + 1], ends[n]) for n in range(0, HEADS, 2)]
        lane = lax.broadcasted_iota(jnp.int32, (1, LANES), 1)
        sums = [jnp.where(lane < side, pltpu.roll(couples[0], side, 1), couples[1]),
                pltpu.roll(couples[2], side, 1)[:, :side]]
        if not exact:
            low_ref[...] = jnp.minimum(low_ref[...], jnp.min(sums[0].reshape(-1, 8, LANES), axis=0))
            high_ref[...] = jnp.maximum(high_ref[...], jnp.max(sums[0].reshape(-1, 8, LANES), axis=0))
            rest = slice(0, width - LANES)
            low_ref[:, rest] = jnp.minimum(low_ref[:, rest], jnp.min(sums[1].reshape(-1, 8, width - LANES), axis=0))
            high_ref[:, rest] = jnp.maximum(high_ref[:, rest], jnp.max(sums[1].reshape(-1, 8, width - LANES), axis=0))
        return jnp.concatenate([top / total for top, total in zip(tops, sums)], 1)

    def block(b, shifted, exact, together):
        source, target = (xb, xa) if shifted else (xa, xb)

        def load(h):
            x = source[h].astype(f32)
            return pltpu.roll(x, tokens - move, 0) if shifted else x

        def pair(i, carry):
            kv = []
            for j in range(2):
                h = b + 2 * i + j
                qkv = jnp.dot(normalize(load(h)).astype(bf16), w_ref[b, :, :768], preferred_element_type=f32)
                q_ref[h] = qkv[:, :width] * scale
                kv.append((qkv[:, 256 : 256 + width], qkv[:, 512 : 512 + width]))
            for w in range(windows):
                at = slice(w * piece, (w + 1) * piece)
                k_ref[i, w] = jnp.concatenate([kv[0][0][at], kv[1][0][at]], 0).astype(bf16)
                v = jnp.concatenate([kv[0][1][at], kv[1][1][at]], 0)
                v_ref[i, w] = jnp.concatenate([v, ones], 1).astype(bf16)
            return carry

        def attend(c, carry):
            own = [1 + b + together * c + j for j in range(together)]
            x = jnp.concatenate([load(h) for h in own], 0)
            a = jnp.concatenate(
                [window_attention(h, (h - b) // 2, w, shifted, exact) for h in own for w in range(windows)], 0
            ).astype(bf16)
            residual = x + jnp.dot(a, wproj_ref[b], preferred_element_type=f32)
            n2 = normalize(residual).astype(bf16)
            u = jnp.dot(n2, w_ref[b, :, 768 : 768 + hidden], preferred_element_type=f32)
            g = (0.5 * u * (1.0 + lax.erf(u * (0.5**0.5)))).astype(bf16)
            y = residual + lax.dot_general(
                g, w_ref[b, :, 768 + hidden :], (((1,), (1,)), ((), ())), preferred_element_type=f32
            )
            for j, h in enumerate(own):
                part = y[j * tokens : (j + 1) * tokens]
                if shifted:
                    part = pltpu.roll(part, move, 0)
                target[h] = part.astype(bf16)
            return carry

        lax.fori_loop(0, halves // 2 - b, pair, 0)
        lax.fori_loop(0, (halves - 2 - 2 * b) // together, attend, 0)
        west, east = target[halves // 2 - 1].astype(f32), target[halves // 2].astype(f32)
        outs_ref[place ^ b] = pack_tile(west, east).astype(bf16)

    def compute(exact, together):
        load_tiles()

        def two_blocks(n, carry):
            block(2 * n, False, exact, together)
            block(2 * n + 1, True, exact, together)
            return carry

        lax.fori_loop(0, STAGE // 2, two_blocks, 0)

    low_ref[...] = jnp.ones_like(low_ref)
    high_ref[...] = jnp.ones_like(high_ref)
    compute(False, 2)
    safe = (jnp.min(low_ref[...]) >= 2.0**-90) & (jnp.max(high_ref[...]) <= 2.0**90)

    @pl.when(jnp.logical_not(safe))
    def _():
        compute(True, 1)

    last_ref[...] = outs_ref[place ^ (STAGE - 1)]


def run_stage(place, tiles, weights, bias):
    packed_tokens = tiles[0].shape[0]
    tokens = packed_tokens // 3
    width = weights[0].shape[0]
    halves = 2 * len(tiles)
    windows, piece, _ = bias.shape
    vmem = pl.BlockSpec(memory_space=pltpu.VMEM)
    bf16, f32 = jnp.bfloat16, jnp.float32
    return pl.pallas_call(
        stage_kernel,
        out_shape=(
            jax.ShapeDtypeStruct((packed_tokens, LANES), bf16),
            jax.ShapeDtypeStruct((STAGE, packed_tokens, LANES), bf16),
        ),
        in_specs=[pl.BlockSpec(memory_space=pltpu.SMEM)] + [vmem] * (len(tiles) + len(weights) + 1),
        out_specs=(vmem, vmem),
        scratch_shapes=[
            pltpu.VMEM((halves, tokens, width), bf16),
            pltpu.VMEM((halves, tokens, width), bf16),
            pltpu.VMEM((halves, tokens, width), f32),
            pltpu.VMEM((halves // 2, windows, 2 * piece, width), bf16),
            pltpu.VMEM((halves // 2, windows, 2 * piece, 256), bf16),
            pltpu.VMEM((STAGE,) + weights[0].shape, bf16),
            pltpu.VMEM((STAGE, width, width), bf16),
            pltpu.VMEM((8, LANES), f32),
            pltpu.VMEM((8, LANES), f32),
        ],
        compiler_params=pltpu.CompilerParams(vmem_limit_bytes=VMEM_LIMIT),
        name="stage",
    )(place, *tiles, *weights, bias)


def finish_kernel(place_ref, o0, o1, o2, o3, out_ref, grid_ref):
    _, _, levels, rows, _ = out_ref.shape
    tokens = grid_ref.shape[1]
    step = levels * HALF
    width = out_ref.shape[4] // WLON
    side = width - LANES
    for i, ref in enumerate((o0, o1, o2, o3)):
        packed = ref[...].astype(jnp.float32)
        for part in range(3):
            grid_ref[part] = packed[part * tokens : (part + 1) * tokens]
        micro = place_ref[0] ^ i
        for level in range(levels):
            for column in range(WLON):
                half, inside = divmod(column, HALF)
                at = pl.ds(level * HALF + inside, rows, stride=step)
                rest = grid_ref[2, at, :][:, half * side : (half + 1) * side]
                piece = jnp.concatenate([grid_ref[half, at, :], rest], 1)
                out_ref[0, micro, level, :, column * width : (column + 1) * width] = piece.astype(jnp.bfloat16)


def finish(place, pieces, shape):
    tokens = pieces[0].shape[0] // 3
    vmem = pl.BlockSpec(memory_space=pltpu.VMEM)
    return pl.pallas_call(
        finish_kernel,
        out_shape=jax.ShapeDtypeStruct(shape, jnp.bfloat16),
        in_specs=[pl.BlockSpec(memory_space=pltpu.SMEM)] + [vmem] * len(pieces),
        out_specs=vmem,
        scratch_shapes=[pltpu.VMEM((3, tokens, LANES), jnp.float32)],
        compiler_params=pltpu.CompilerParams(vmem_limit_bytes=VMEM_LIMIT),
        name="finish",
    )(place, *pieces)


def on_device(fields, land_mask, land_vector, w_qkv, w_proj, w_up, w_down):
    micro_count, levels, rows, flat_width = fields.shape
    width = land_vector.shape[0]
    tile_count, section_count = lax.axis_size("tile"), lax.axis_size("section")
    section = lax.axis_index("section")
    place = (section % STAGE).astype(jnp.int32).reshape(1)
    axes = ("tile", "section")

    def exchange(value, bit):
        return lax.ppermute(value, "section", [(s, s ^ bit) for s in range(section_count)])

    def shift(value, tiles, stages):
        pairs = [
            (t * section_count + s, (t + tiles) % tile_count * section_count + s + stages * STAGE)
            for t in range(tile_count)
            for s in range(STAGE)
        ]
        return lax.ppermute(value, axes, pairs)

    tile, pack = prepare(place, fields, land_mask, land_vector.reshape(1, width), (w_qkv, w_proj, w_up, w_down.transpose(0, 2, 1)))
    bias = jnp.asarray(window_bias(levels, rows))

    offsets = range(-REACH, REACH + 1)
    tiles = [tile if d == 0 else shift(tile, -d, 0) for d in offsets]
    weights = [pack] + [exchange(pack, i) for i in range(1, STAGE)]

    last, early = run_stage(place, tiles, weights, bias)
    tiles = [shift(last, -d, 1) for d in offsets]
    _, late = run_stage(place, tiles, weights, bias)
    outs = jnp.where(section < STAGE, early, late)

    pieces = [outs[0]] + [exchange(outs[i], i) for i in range(1, STAGE)]
    return finish(place, pieces, (1, micro_count, levels, rows, flat_width))


def solution(mesh):
    in_specs = (
        P(None, None, None, "tile"),
        P(None, "tile"),
        P(),
        P("section", None, None),
        P("section", None, None),
        P("section", None, None),
        P("section", None, None),
    )
    out_specs = P("section", None, None, None, "tile")
    return jax.shard_map(on_device, mesh=mesh, in_specs=in_specs, out_specs=out_specs, check_vma=False)
```

```python
import functools

import jax
import jax.numpy as jnp
import numpy as np
from jax import lax
from jax.experimental import pallas as pl
from jax.experimental.pallas import tpu as pltpu
from jax.sharding import PartitionSpec as P

HEADS = 6
WZ = 2
WLAT = 6
WLON = 12
HALF = WLON // 2
STAGE = 4
REACH = 2
LOG2E = 1.4426950408889634
LANES = 128
VMEM_LIMIT = 56 * 2**20


def normalize(values):
    center = values - jnp.mean(values, axis=-1, keepdims=True)
    spread = jnp.mean(center * center, axis=-1, keepdims=True)
    return center * lax.rsqrt(spread + 1e-05)


def window_bias(levels, rows):
    lat_blocks = rows // WLAT
    index = np.arange(WLAT * levels * HALF)
    row, level = index // (levels * HALF), index // HALF % levels
    row = row[None] + WLAT * np.arange(lat_blocks)[:, None]

    def label(place, length, window):
        return np.where(place < length - window, 0, np.where(place < length - window // 2, 1, 2))

    labels = label(level, levels, WZ)[None] * 3 + label(row, rows, WLAT)
    keys = np.concatenate([labels, labels], 1)
    return np.where(labels[:, :, None] == keys[:, None, :], 0.0, -1e30).astype(np.float32)


def pack_tile(west, east):
    return jnp.concatenate(
        [west[:, :LANES], jnp.concatenate([west[:, LANES:], east[:, LANES:]], 1), east[:, :LANES]], 0
    )


def west_of(packed, tokens):
    return jnp.concatenate([packed[:tokens], packed[tokens : 2 * tokens, : LANES // 2]], 1)


def east_of(packed, tokens):
    end = packed.shape[0]
    return jnp.concatenate([packed[end - tokens :], packed[end - 2 * tokens : end - tokens, LANES // 2 :]], 1)


def prepare_kernel(micro_ref, fields_ref, mask_ref, vector_ref, wqkv_ref, wproj_ref, wup_ref, wdown_ref,
                   tile_ref, pack_ref, grid_ref):
    _, levels, rows, _ = fields_ref.shape
    width = vector_ref.shape[1]
    mask = mask_ref[...].astype(jnp.float32)
    vector = vector_ref[...]
    step = levels * HALF
    for level in range(levels):
        for column in range(WLON):
            piece = fields_ref[0, level, :, column * width : (column + 1) * width].astype(jnp.float32)
            piece = piece + mask[:, column : column + 1] * vector
            half, inside = divmod(column, HALF)
            at = pl.ds(level * HALF + inside, rows, stride=step)
            grid_ref[2 * half, at, :] = piece[:, :LANES]
            grid_ref[2 * half + 1, at, :] = jnp.concatenate([piece[:, LANES:]] * 2, 1)
    tokens, side = rows * step, width - LANES
    tile_ref[:tokens] = grid_ref[0].astype(jnp.bfloat16)
    tile_ref[2 * tokens :] = grid_ref[2].astype(jnp.bfloat16)
    lane = lax.broadcasted_iota(jnp.int32, (1, LANES), 1)
    tile_ref[tokens : 2 * tokens] = jnp.where(lane < side, grid_ref[1], grid_ref[3]).astype(jnp.bfloat16)
    side = 256 - width
    for i in range(3):
        pack_ref[:, 256 * i : 256 * i + 256] = jnp.concatenate(
            [wqkv_ref[0, :, i * width : (i + 1) * width], wproj_ref[0, :, i * side : (i + 1) * side]], 1
        )
    hidden = wup_ref.shape[2]
    pack_ref[:, 768 : 768 + hidden] = wup_ref[0]
    pack_ref[:, 768 + hidden :] = wdown_ref[0]


def prepare(micro, fields, land_mask, land_vector, weights):
    _, levels, rows, flat = fields.shape
    width = land_vector.shape[1]
    tokens = rows * levels * HALF
    whole = lambda a: pl.BlockSpec(a.shape, lambda i, m: (0,) * a.ndim)
    return pl.pallas_call(
        prepare_kernel,
        out_shape=(
            jax.ShapeDtypeStruct((3 * tokens, LANES), jnp.bfloat16),
            jax.ShapeDtypeStruct((width, 2304), jnp.bfloat16),
        ),
        grid_spec=pltpu.PrefetchScalarGridSpec(
            num_scalar_prefetch=1,
            grid=(1,),
            in_specs=[pl.BlockSpec((1, levels, rows, flat), lambda i, m: (m[0], 0, 0, 0))]
            + [whole(a) for a in (land_mask, land_vector, *weights)],
            out_specs=(
                pl.BlockSpec((3 * tokens, LANES), lambda i, m: (0, 0)),
                pl.BlockSpec((width, 2304), lambda i, m: (0, 0)),
            ),
            scratch_shapes=[pltpu.VMEM((4, tokens, LANES), jnp.float32)],
        ),
        compiler_params=pltpu.CompilerParams(vmem_limit_bytes=VMEM_LIMIT),
        name="prepare",
    )(micro, fields, land_mask, land_vector, *weights)


def compute_stage(mode, tile_refs, bias_ref, w_ref, wproj_ref, store, scratch):
    xa, xb, q_ref, k_ref, v_ref, low_ref, high_ref = scratch
    f32, bf16 = jnp.float32, jnp.bfloat16
    halves, tokens, width = xa.shape
    head_size = width // HEADS
    windows, piece, _ = bias_ref.shape
    move = piece // 2
    hidden = (w_ref.shape[2] - 768) // 2
    middle = halves // 2

    channel_head = lax.broadcasted_iota(jnp.int32, (1, width), 1) // head_size
    scale = head_size ** (-0.5) * LOG2E
    ones = jnp.ones((2 * piece, 256 - width), f32)

    def load_tiles():
        into = xb if mode == "rest" else xa
        first = middle - len(tile_refs)
        for i, ref in enumerate(tile_refs):
            packed = ref[...].astype(f32)
            for j, part in enumerate((west_of, east_of)):
                h = first + 2 * i + j
                if mode != "rest" or 0 < h < halves - 1:
                    into[h] = part(packed, tokens).astype(bf16)

    def select_heads(parts, first, lanes):
        total = parts[0]
        for n in range(1, len(parts)):
            total = jnp.where(channel_head[:, first : first + lanes] == first // head_size + n, parts[n], total)
        return total

    def window_attention(h, i, w, shifted, exact):
        q = q_ref[h, w * piece : (w + 1) * piece, :]
        qm = jnp.concatenate([jnp.where(channel_head == n, q, 0.0) for n in range(HEADS)], 0).astype(bf16)
        s = lax.dot_general(qm, k_ref[i, w], (((1,), (1,)), ((), ())), preferred_element_type=f32)
        if shifted:
            s = (s.reshape(HEADS, piece, 2 * piece) + bias_ref[w][None]).reshape(HEADS * piece, 2 * piece)
        if exact:
            s = s - jnp.max(s, axis=-1, keepdims=True)
        o = jnp.dot(jnp.exp2(s).astype(bf16), v_ref[i, w], preferred_element_type=f32)
        heads = [o[n * piece : (n + 1) * piece] for n in range(HEADS)]
        full = LANES // head_size
        tops = [select_heads([x[:, :LANES] for x in heads[:full]], 0, LANES),
                select_heads([x[:, LANES:width] for x in heads[full:]], LANES, width - LANES)]
        side = 256 - width
        ends = [x[:, LANES:] for x in heads]
        odd = channel_head[:, :LANES] % 2 == 1
        couples = [jnp.where(odd, ends[n + 1], ends[n]) for n in range(0, HEADS, 2)]
        lane = lax.broadcasted_iota(jnp.int32, (1, LANES), 1)
        sums = [jnp.where(lane < side, pltpu.roll(couples[0], side, 1), couples[1]),
                pltpu.roll(couples[2], side, 1)[:, :side]]
        if not exact:
            low_ref[...] = jnp.minimum(low_ref[...], jnp.min(sums[0].reshape(-1, 8, LANES), axis=0))
            high_ref[...] = jnp.maximum(high_ref[...], jnp.max(sums[0].reshape(-1, 8, LANES), axis=0))
            rest = slice(0, width - LANES)
            low_ref[:, rest] = jnp.minimum(low_ref[:, rest], jnp.min(sums[1].reshape(-1, 8, width - LANES), axis=0))
            high_ref[:, rest] = jnp.maximum(high_ref[:, rest], jnp.max(sums[1].reshape(-1, 8, width - LANES), axis=0))
        return jnp.concatenate([top / total for top, total in zip(tops, sums)], 1)

    def block(b, shifted, exact, together, alone=False):
        source, target = (xb, xa) if shifted else (xa, xb)

        def load(h):
            x = source[h].astype(f32)
            return pltpu.roll(x, tokens - move, 0) if shifted else x

        def pair(i, carry):
            kv = []
            for j in range(2):
                h = b + 2 * i + j
                qkv = jnp.dot(normalize(load(h)).astype(bf16), w_ref[b, :, :768], preferred_element_type=f32)
                q_ref[h] = qkv[:, :width] * scale
                kv.append((qkv[:, 256 : 256 + width], qkv[:, 512 : 512 + width]))
            for w in range(windows):
                at = slice(w * piece, (w + 1) * piece)
                k_ref[i, w] = jnp.concatenate([kv[0][0][at], kv[1][0][at]], 0).astype(bf16)
                v = jnp.concatenate([kv[0][1][at], kv[1][1][at]], 0)
                v_ref[i, w] = jnp.concatenate([v, ones], 1).astype(bf16)
            return carry

        def attend(c, carry):
            own = [(middle - 1 if alone else 1 + b) + together * c + j for j in range(together)]
            x = jnp.concatenate([load(h) for h in own], 0)
            a = jnp.concatenate(
                [window_attention(h, (h - b) // 2, w, shifted, exact) for h in own for w in range(windows)], 0
            ).astype(bf16)
            residual = x + jnp.dot(a, wproj_ref[b], preferred_element_type=f32)
            n2 = normalize(residual).astype(bf16)
            u = jnp.dot(n2, w_ref[b, :, 768 : 768 + hidden], preferred_element_type=f32)
            g = (0.5 * u * (1.0 + lax.erf(u * (0.5**0.5)))).astype(bf16)
            y = residual + lax.dot_general(
                g, w_ref[b, :, 768 + hidden :], (((1,), (1,)), ((), ())), preferred_element_type=f32
            )
            for j, h in enumerate(own):
                part = y[j * tokens : (j + 1) * tokens]
                if shifted:
                    part = pltpu.roll(part, move, 0)
                target[h] = part.astype(bf16)
            return carry

        if alone:
            pair(middle // 2, 0)
            lax.fori_loop(0, 2 // together, attend, 0)
        else:
            lax.fori_loop(0, middle - b, pair, 0)
            lax.fori_loop(0, (halves - 2 - 2 * b) // together, attend, 0)
        store(b, pack_tile(target[middle - 1].astype(f32), target[middle].astype(f32)).astype(bf16))

    def compute(exact, together):
        load_tiles()

        def two_blocks(n, carry):
            block(2 * n, False, exact, together)
            block(2 * n + 1, True, exact, together)
            return carry

        if mode == "whole":
            lax.fori_loop(0, STAGE // 2, two_blocks, 0)
        elif mode == "first":
            block(0, False, exact, together, True)
        else:
            for b in range(1, STAGE):
                block(b, b % 2 == 1, exact, together)

    low_ref[...] = jnp.ones_like(low_ref)
    high_ref[...] = jnp.ones_like(high_ref)
    compute(False, 2)
    safe = (jnp.min(low_ref[...]) >= 2.0**-90) & (jnp.max(high_ref[...]) <= 2.0**90)

    @pl.when(jnp.logical_not(safe))
    def _():
        compute(True, 1)


def unpack_projection(ref, width):
    return jnp.concatenate([ref[:, 256 * j + width : 256 * j + 256] for j in range(3)], 1)


def gather_weights(place, refs, w_ref, wproj_ref):
    for i, ref in enumerate(refs):
        w_ref[place ^ i] = ref[...]
        wproj_ref[place ^ i] = unpack_projection(ref, wproj_ref.shape[1])


def whole_kernel(place_ref, t0, t1, t2, t3, t4, w0, w1, w2, w3, bias_ref, last_ref, outs_ref,
                 w_ref, wproj_ref, *scratch):
    place = place_ref[0]
    gather_weights(place, (w0, w1, w2, w3), w_ref, wproj_ref)

    def store(b, packed):
        outs_ref[place ^ b] = packed

    compute_stage("whole", (t0, t1, t2, t3, t4), bias_ref, w_ref, wproj_ref, store, scratch)
    last_ref[...] = outs_ref[place ^ (STAGE - 1)]


def first_kernel(tile_in, w_in, bias_ref, tile_ref, west_ref, east_ref, w_ref, wproj_ref, *scratch):
    w_ref[0] = w_in[...]
    wproj_ref[0] = unpack_projection(w_in, wproj_ref.shape[1])

    def store(b, packed):
        tile_ref[...] = packed

    compute_stage("first", (tile_in,), bias_ref, w_ref, wproj_ref, store, scratch)
    west_ref[...] = tile_ref[: west_ref.shape[0]]
    east_ref[...] = tile_ref[tile_ref.shape[0] - east_ref.shape[0] :]


def rest_kernel(place_ref, t0, t1, t2, t3, t4, w0, w1, w2, w3, bias_ref, early_ref, o0, o1, o2, o3,
                outs_ref, w_ref, wproj_ref, *scratch):
    place = place_ref[0]
    late = place_ref[1] == 1

    @pl.when(late)
    def _():
        gather_weights(place, (w0, w1, w2, w3), w_ref, wproj_ref)

        def store(b, packed):
            outs_ref[place ^ b] = packed

        store(0, t2[...])
        compute_stage("rest", (t0, t1, t2, t3, t4), bias_ref, w_ref, wproj_ref, store, scratch)
        for i, ref in enumerate((o0, o1, o2, o3)):
            ref[...] = outs_ref[i]

    @pl.when(jnp.logical_not(late))
    def _():
        for i, ref in enumerate((o0, o1, o2, o3)):
            ref[...] = early_ref[i]


def run_stage(kernel, place, operands, outs, extra, blocks, tokens, width, bias_shape):
    halves = 2 * (2 * REACH + 1)
    windows, piece, _ = bias_shape
    vmem = pl.BlockSpec(memory_space=pltpu.VMEM)
    bf16, f32 = jnp.bfloat16, jnp.float32
    places = [] if place is None else [place]
    return pl.pallas_call(
        kernel,
        out_shape=tuple(jax.ShapeDtypeStruct(shape, bf16) for shape in outs),
        in_specs=[pl.BlockSpec(memory_space=pltpu.SMEM)] * len(places) + [vmem] * len(operands),
        out_specs=(vmem,) * len(outs),
        scratch_shapes=[pltpu.VMEM(shape, bf16) for shape in extra]
        + [
            pltpu.VMEM((blocks, width, 2304), bf16),
            pltpu.VMEM((blocks, width, width), bf16),
            pltpu.VMEM((halves, tokens, width), bf16),
            pltpu.VMEM((halves, tokens, width), bf16),
            pltpu.VMEM((halves, tokens, width), f32),
            pltpu.VMEM((halves // 2, windows, 2 * piece, width), bf16),
            pltpu.VMEM((halves // 2, windows, 2 * piece, 256), bf16),
            pltpu.VMEM((8, LANES), f32),
            pltpu.VMEM((8, LANES), f32),
        ],
        compiler_params=pltpu.CompilerParams(vmem_limit_bytes=VMEM_LIMIT),
        name=kernel.__name__,
    )(*places, *operands)


def finish_kernel(place_ref, o0, o1, o2, o3, out_ref, grid_ref):
    _, _, levels, rows, _ = out_ref.shape
    tokens = grid_ref.shape[1]
    step = levels * HALF
    width = out_ref.shape[4] // WLON
    side = width - LANES
    for i, ref in enumerate((o0, o1, o2, o3)):
        packed = ref[...].astype(jnp.float32)
        for part in range(3):
            grid_ref[part] = packed[part * tokens : (part + 1) * tokens]
        micro = place_ref[0] ^ i
        for level in range(levels):
            for column in range(WLON):
                half, inside = divmod(column, HALF)
                at = pl.ds(level * HALF + inside, rows, stride=step)
                rest = grid_ref[1, at, :][:, half * side : (half + 1) * side]
                piece = jnp.concatenate([grid_ref[2 * half, at, :], rest], 1)
                out_ref[0, micro, level, :, column * width : (column + 1) * width] = piece.astype(jnp.bfloat16)


def finish(place, pieces, shape):
    tokens = pieces[0].shape[0] // 3
    vmem = pl.BlockSpec(memory_space=pltpu.VMEM)
    return pl.pallas_call(
        finish_kernel,
        out_shape=jax.ShapeDtypeStruct(shape, jnp.bfloat16),
        in_specs=[pl.BlockSpec(memory_space=pltpu.SMEM)] + [vmem] * len(pieces),
        out_specs=vmem,
        scratch_shapes=[pltpu.VMEM((3, tokens, LANES), jnp.float32)],
        compiler_params=pltpu.CompilerParams(vmem_limit_bytes=VMEM_LIMIT),
        name="finish",
    )(place, *pieces)


def on_device(fields, land_mask, land_vector, w_qkv, w_proj, w_up, w_down):
    micro_count, levels, rows, flat_width = fields.shape
    width = land_vector.shape[0]
    tile_count, section_count = lax.axis_size("tile"), lax.axis_size("section")
    section = lax.axis_index("section")
    place = jnp.stack([section % STAGE, section // STAGE]).astype(jnp.int32)
    axes = ("tile", "section")

    def exchange(value, bit):
        return lax.ppermute(value, "section", [(s, s ^ bit) for s in range(section_count)])

    def shift(value, tiles, first, stages=0):
        pairs = [
            (t * section_count + s, (t + tiles) % tile_count * section_count + s + stages * STAGE)
            for t in range(tile_count)
            for s in range(first, first + STAGE)
        ]
        return lax.ppermute(value, axes, pairs)

    tokens = rows * levels * HALF
    tile_shape, half_shape = (3 * tokens, LANES), (2 * tokens, LANES)
    bias = jnp.asarray(window_bias(levels, rows))
    sizes = (tokens, width, bias.shape)

    tile, pack = prepare(
        place, fields, land_mask, land_vector.reshape(1, width), (w_qkv, w_proj, w_up, w_down.transpose(0, 2, 1))
    )
    tiles = [tile if d == 0 else shift(tile, -d, 0) for d in range(-REACH, REACH + 1)]
    near, far = exchange(pack, 1), exchange(pack, 2)
    far, tiles = lax.optimization_barrier((far, tiles))
    weights = [pack, near, far, exchange(far, 1)]

    last, early = run_stage(
        whole_kernel, place, (*tiles, *weights, bias), (tile_shape, (STAGE,) + tile_shape), (), STAGE, *sizes
    )
    own = shift(last, 0, 0, 1)
    first = lax.select_n(place[0], *weights)
    own, west, east = run_stage(first_kernel, None, (own, first, bias), (tile_shape, half_shape, half_shape), (), 1, *sizes)
    tiles = [shift(east, 2, STAGE), shift(own, 1, STAGE), own, shift(own, -1, STAGE), shift(west, -2, STAGE)]
    outs = run_stage(
        rest_kernel, place, (*tiles, *weights, bias, early), (tile_shape,) * STAGE, ((STAGE,) + tile_shape,), STAGE, *sizes
    )

    pieces = [outs[0]] + [exchange(outs[i], i) for i in range(1, STAGE)]
    return finish(place, pieces, (1, micro_count, levels, rows, flat_width))


def solution(mesh):
    in_specs = (
        P(None, None, None, "tile"),
        P(None, "tile"),
        P(),
        P("section", None, None),
        P("section", None, None),
        P("section", None, None),
        P("section", None, None),
    )
    out_specs = P("section", None, None, None, "tile")
    return jax.shard_map(on_device, mesh=mesh, in_specs=in_specs, out_specs=out_specs, check_vma=False)
```

```python
import functools

import jax
import jax.numpy as jnp
import numpy as np
from jax import lax
from jax.experimental import pallas as pl
from jax.experimental.pallas import tpu as pltpu
from jax.sharding import PartitionSpec as P

HEADS = 6
WZ = 2
WLAT = 6
WLON = 12
HALF = WLON // 2
STAGE = 4
REACH = 2
LOG2E = 1.4426950408889634
LANES = 128
VMEM_LIMIT = 56 * 2**20


def normalize(values):
    center = values - jnp.mean(values, axis=-1, keepdims=True)
    spread = jnp.mean(center * center, axis=-1, keepdims=True)
    return center * lax.rsqrt(spread + 1e-05)


def window_bias(levels, rows):
    lat_blocks = rows // WLAT
    index = np.arange(WLAT * levels * HALF)
    row, level = index // (levels * HALF), index // HALF % levels
    row = row[None] + WLAT * np.arange(lat_blocks)[:, None]

    def label(place, length, window):
        return np.where(place < length - window, 0, np.where(place < length - window // 2, 1, 2))

    labels = label(level, levels, WZ)[None] * 3 + label(row, rows, WLAT)
    keys = np.concatenate([labels, labels], 1)
    return np.where(labels[:, :, None] == keys[:, None, :], 0.0, -1e30).astype(np.float32)


def pack_tile(west, east):
    return jnp.concatenate(
        [west[:, :LANES], jnp.concatenate([west[:, LANES:], east[:, LANES:]], 1), east[:, :LANES]], 0
    )


def west_of(packed, tokens):
    return jnp.concatenate([packed[:tokens], packed[tokens : 2 * tokens, : LANES // 2]], 1)


def east_of(packed, tokens):
    end = packed.shape[0]
    return jnp.concatenate([packed[end - tokens :], packed[end - 2 * tokens : end - tokens, LANES // 2 :]], 1)


def embed_kernel(micro_ref, fields_ref, mask_ref, vector_ref, tile_ref, grid_ref):
    _, levels, rows, _ = fields_ref.shape
    width = vector_ref.shape[1]
    mask = mask_ref[...].astype(jnp.float32)
    vector = vector_ref[...]
    step = levels * HALF
    for level in range(levels):
        for column in range(WLON):
            piece = fields_ref[0, level, :, column * width : (column + 1) * width].astype(jnp.float32)
            piece = piece + mask[:, column : column + 1] * vector
            half, inside = divmod(column, HALF)
            at = pl.ds(level * HALF + inside, rows, stride=step)
            grid_ref[2 * half, at, :] = piece[:, :LANES]
            grid_ref[2 * half + 1, at, :] = jnp.concatenate([piece[:, LANES:]] * 2, 1)
    tokens, side = rows * step, width - LANES
    tile_ref[:tokens] = grid_ref[0].astype(jnp.bfloat16)
    tile_ref[2 * tokens :] = grid_ref[2].astype(jnp.bfloat16)
    lane = lax.broadcasted_iota(jnp.int32, (1, LANES), 1)
    tile_ref[tokens : 2 * tokens] = jnp.where(lane < side, grid_ref[1], grid_ref[3]).astype(jnp.bfloat16)


def embed(micro, fields, land_mask, land_vector):
    _, levels, rows, flat = fields.shape
    tokens = rows * levels * HALF
    whole = lambda a: pl.BlockSpec(a.shape, lambda i, m: (0,) * a.ndim)
    return pl.pallas_call(
        embed_kernel,
        out_shape=jax.ShapeDtypeStruct((3 * tokens, LANES), jnp.bfloat16),
        grid_spec=pltpu.PrefetchScalarGridSpec(
            num_scalar_prefetch=1,
            grid=(1,),
            in_specs=[pl.BlockSpec((1, levels, rows, flat), lambda i, m: (m[0], 0, 0, 0)),
                      whole(land_mask), whole(land_vector)],
            out_specs=pl.BlockSpec((3 * tokens, LANES), lambda i, m: (0, 0)),
            scratch_shapes=[pltpu.VMEM((4, tokens, LANES), jnp.float32)],
        ),
        compiler_params=pltpu.CompilerParams(vmem_limit_bytes=VMEM_LIMIT),
        name="embed",
    )(micro, fields, land_mask, land_vector)


def pack_kernel(wqkv_ref, wproj_ref, wup_ref, wdown_ref, pack_ref):
    width = wproj_ref.shape[1]
    side = 256 - width
    for i in range(3):
        pack_ref[:, 256 * i : 256 * i + 256] = jnp.concatenate(
            [wqkv_ref[0, :, i * width : (i + 1) * width], wproj_ref[0, :, i * side : (i + 1) * side]], 1
        )
    hidden = wup_ref.shape[2]
    pack_ref[:, 768 : 768 + hidden] = wup_ref[0]
    pack_ref[:, 768 + hidden :] = wdown_ref[0]


def pack_weights(*weights):
    vmem = pl.BlockSpec(memory_space=pltpu.VMEM)
    width = weights[0].shape[1]
    return pl.pallas_call(
        pack_kernel,
        out_shape=jax.ShapeDtypeStruct((width, 2304), jnp.bfloat16),
        in_specs=[vmem] * len(weights),
        out_specs=vmem,
        compiler_params=pltpu.CompilerParams(vmem_limit_bytes=VMEM_LIMIT),
        name="pack_weights",
    )(*weights)


def compute_stage(mode, tile_refs, bias_ref, w_ref, wproj_ref, store, scratch):
    xa, xb, q_ref, k_ref, v_ref, low_ref, high_ref = scratch
    f32, bf16 = jnp.float32, jnp.bfloat16
    halves, tokens, width = xa.shape
    head_size = width // HEADS
    windows, piece, _ = bias_ref.shape
    move = piece // 2
    hidden = (w_ref.shape[2] - 768) // 2
    middle = halves // 2

    channel_head = lax.broadcasted_iota(jnp.int32, (1, width), 1) // head_size
    scale = head_size ** (-0.5) * LOG2E
    ones = jnp.ones((2 * piece, 256 - width), f32)

    def load_tiles():
        into = xb if mode == "rest" else xa
        first = middle - len(tile_refs)
        for i, ref in enumerate(tile_refs):
            packed = ref[...].astype(f32)
            for j, part in enumerate((west_of, east_of)):
                h = first + 2 * i + j
                if mode != "rest" or 0 < h < halves - 1:
                    into[h] = part(packed, tokens).astype(bf16)

    def select_heads(parts, first, lanes):
        total = parts[0]
        for n in range(1, len(parts)):
            total = jnp.where(channel_head[:, first : first + lanes] == first // head_size + n, parts[n], total)
        return total

    def window_attention(h, i, w, shifted, exact):
        q = q_ref[h, w * piece : (w + 1) * piece, :]
        qm = jnp.concatenate([jnp.where(channel_head == n, q, 0.0) for n in range(HEADS)], 0).astype(bf16)
        s = lax.dot_general(qm, k_ref[i, w], (((1,), (1,)), ((), ())), preferred_element_type=f32)
        if shifted:
            s = (s.reshape(HEADS, piece, 2 * piece) + bias_ref[w][None]).reshape(HEADS * piece, 2 * piece)
        if exact:
            s = s - jnp.max(s, axis=-1, keepdims=True)
        o = jnp.dot(jnp.exp2(s).astype(bf16), v_ref[i, w], preferred_element_type=f32)
        heads = [o[n * piece : (n + 1) * piece] for n in range(HEADS)]
        full = LANES // head_size
        tops = [select_heads([x[:, :LANES] for x in heads[:full]], 0, LANES),
                select_heads([x[:, LANES:width] for x in heads[full:]], LANES, width - LANES)]
        side = 256 - width
        ends = [x[:, LANES:] for x in heads]
        odd = channel_head[:, :LANES] % 2 == 1
        couples = [jnp.where(odd, ends[n + 1], ends[n]) for n in range(0, HEADS, 2)]
        lane = lax.broadcasted_iota(jnp.int32, (1, LANES), 1)
        sums = [jnp.where(lane < side, pltpu.roll(couples[0], side, 1), couples[1]),
                pltpu.roll(couples[2], side, 1)[:, :side]]
        if not exact:
            low_ref[...] = jnp.minimum(low_ref[...], jnp.min(sums[0].reshape(-1, 8, LANES), axis=0))
            high_ref[...] = jnp.maximum(high_ref[...], jnp.max(sums[0].reshape(-1, 8, LANES), axis=0))
            rest = slice(0, width - LANES)
            low_ref[:, rest] = jnp.minimum(low_ref[:, rest], jnp.min(sums[1].reshape(-1, 8, width - LANES), axis=0))
            high_ref[:, rest] = jnp.maximum(high_ref[:, rest], jnp.max(sums[1].reshape(-1, 8, width - LANES), axis=0))
        return jnp.concatenate([top / total for top, total in zip(tops, sums)], 1)

    def block(b, shifted, exact, together, alone=False):
        source, target = (xb, xa) if shifted else (xa, xb)

        def load(h):
            x = source[h].astype(f32)
            return pltpu.roll(x, tokens - move, 0) if shifted else x

        def pair(i, carry):
            kv = []
            for j in range(2):
                h = b + 2 * i + j
                qkv = jnp.dot(normalize(load(h)).astype(bf16), w_ref[b, :, :768], preferred_element_type=f32)
                q_ref[h] = qkv[:, :width] * scale
                kv.append((qkv[:, 256 : 256 + width], qkv[:, 512 : 512 + width]))
            for w in range(windows):
                at = slice(w * piece, (w + 1) * piece)
                k_ref[i, w] = jnp.concatenate([kv[0][0][at], kv[1][0][at]], 0).astype(bf16)
                v = jnp.concatenate([kv[0][1][at], kv[1][1][at]], 0)
                v_ref[i, w] = jnp.concatenate([v, ones], 1).astype(bf16)
            return carry

        def attend(c, carry):
            own = [(middle - 1 if alone else 1 + b) + together * c + j for j in range(together)]
            x = jnp.concatenate([load(h) for h in own], 0)
            a = jnp.concatenate(
                [window_attention(h, (h - b) // 2, w, shifted, exact) for h in own for w in range(windows)], 0
            ).astype(bf16)
            residual = x + jnp.dot(a, wproj_ref[b], preferred_element_type=f32)
            n2 = normalize(residual).astype(bf16)
            u = jnp.dot(n2, w_ref[b, :, 768 : 768 + hidden], preferred_element_type=f32)
            g = (0.5 * u * (1.0 + lax.erf(u * (0.5**0.5)))).astype(bf16)
            y = residual + lax.dot_general(
                g, w_ref[b, :, 768 + hidden :], (((1,), (1,)), ((), ())), preferred_element_type=f32
            )
            for j, h in enumerate(own):
                part = y[j * tokens : (j + 1) * tokens]
                if shifted:
                    part = pltpu.roll(part, move, 0)
                target[h] = part.astype(bf16)
            return carry

        if alone:
            pair(middle // 2, 0)
            lax.fori_loop(0, 2 // together, attend, 0)
        else:
            lax.fori_loop(0, middle - b, pair, 0)
            lax.fori_loop(0, (halves - 2 - 2 * b) // together, attend, 0)
        store(b, pack_tile(target[middle - 1].astype(f32), target[middle].astype(f32)).astype(bf16))

    def compute(exact, together):
        load_tiles()

        def two_blocks(n, carry):
            @pl.when(n > 0)
            def _():
                block(2 * n, False, exact, together)

            block(2 * n + 1, True, exact, together)
            return carry

        if mode == "first":
            block(0, False, exact, together, True)
        else:
            lax.fori_loop(0, STAGE // 2, two_blocks, 0)

    low_ref[...] = jnp.ones_like(low_ref)
    high_ref[...] = jnp.ones_like(high_ref)
    compute(False, 2)
    safe = (jnp.min(low_ref[...]) >= 2.0**-90) & (jnp.max(high_ref[...]) <= 2.0**90)

    @pl.when(jnp.logical_not(safe))
    def _():
        compute(True, 1)


def unpack_projection(ref, width):
    return jnp.concatenate([ref[:, 256 * j + width : 256 * j + 256] for j in range(3)], 1)


def gather_weights(place, refs, w_ref, wproj_ref):
    for i, ref in enumerate(refs):
        w_ref[place ^ i] = ref[...]
        wproj_ref[place ^ i] = unpack_projection(ref, wproj_ref.shape[1])


def first_kernel(place_ref, tile_in, w0, w1, w2, w3, bias_ref, tile_ref, west_ref, east_ref,
                 w_ref, wproj_ref, *scratch):
    for i, ref in enumerate((w0, w1, w2, w3)):

        @pl.when(place_ref[0] == i)
        def _(ref=ref):
            w_ref[0] = ref[...]
            wproj_ref[0] = unpack_projection(ref, wproj_ref.shape[1])

    def store(b, packed):
        tile_ref[...] = packed

    compute_stage("first", (tile_in,), bias_ref, w_ref, wproj_ref, store, scratch)
    west_ref[...] = tile_ref[: west_ref.shape[0]]
    east_ref[...] = tile_ref[tile_ref.shape[0] - east_ref.shape[0] :]


def compute_rest(place, tiles, weights, bias_ref, outs_ref, w_ref, wproj_ref, scratch):
    gather_weights(place, weights, w_ref, wproj_ref)

    def store(b, packed):
        outs_ref[place ^ b] = packed

    store(0, tiles[REACH][...])
    compute_stage("rest", tiles, bias_ref, w_ref, wproj_ref, store, scratch)


def early_kernel(place_ref, t0, t1, t2, t3, t4, w0, w1, w2, w3, bias_ref, last_ref, outs_ref,
                 w_ref, wproj_ref, *scratch):
    place = place_ref[0]
    compute_rest(place, (t0, t1, t2, t3, t4), (w0, w1, w2, w3), bias_ref, outs_ref, w_ref, wproj_ref, scratch)
    last_ref[...] = outs_ref[place ^ (STAGE - 1)]


def late_kernel(place_ref, t0, t1, t2, t3, t4, w0, w1, w2, w3, bias_ref, early_ref, o0, o1, o2, o3,
                outs_ref, w_ref, wproj_ref, *scratch):
    late = place_ref[1] == 1

    @pl.when(late)
    def _():
        compute_rest(
            place_ref[0], (t0, t1, t2, t3, t4), (w0, w1, w2, w3), bias_ref, outs_ref, w_ref, wproj_ref, scratch
        )
        for i, ref in enumerate((o0, o1, o2, o3)):
            ref[...] = outs_ref[i]

    @pl.when(jnp.logical_not(late))
    def _():
        for i, ref in enumerate((o0, o1, o2, o3)):
            ref[...] = early_ref[i]


def run_stage(kernel, place, operands, outs, extra, blocks, tokens, width, bias_shape):
    halves = 2 * (2 * REACH + 1)
    windows, piece, _ = bias_shape
    vmem = pl.BlockSpec(memory_space=pltpu.VMEM)
    bf16, f32 = jnp.bfloat16, jnp.float32
    return pl.pallas_call(
        kernel,
        out_shape=tuple(jax.ShapeDtypeStruct(shape, bf16) for shape in outs),
        in_specs=[pl.BlockSpec(memory_space=pltpu.SMEM)] + [vmem] * len(operands),
        out_specs=(vmem,) * len(outs),
        scratch_shapes=[pltpu.VMEM(shape, bf16) for shape in extra]
        + [
            pltpu.VMEM((blocks, width, 2304), bf16),
            pltpu.VMEM((blocks, width, width), bf16),
            pltpu.VMEM((halves, tokens, width), bf16),
            pltpu.VMEM((halves, tokens, width), bf16),
            pltpu.VMEM((halves, tokens, width), f32),
            pltpu.VMEM((halves // 2, windows, 2 * piece, width), bf16),
            pltpu.VMEM((halves // 2, windows, 2 * piece, 256), bf16),
            pltpu.VMEM((8, LANES), f32),
            pltpu.VMEM((8, LANES), f32),
        ],
        compiler_params=pltpu.CompilerParams(vmem_limit_bytes=VMEM_LIMIT),
        name=kernel.__name__,
    )(place, *operands)


def finish_kernel(place_ref, o0, o1, o2, o3, out_ref, grid_ref):
    _, _, levels, rows, _ = out_ref.shape
    tokens = grid_ref.shape[1]
    step = levels * HALF
    width = out_ref.shape[4] // WLON
    side = width - LANES
    for i, ref in enumerate((o0, o1, o2, o3)):
        packed = ref[...].astype(jnp.float32)
        for part in range(3):
            grid_ref[part] = packed[part * tokens : (part + 1) * tokens]
        micro = place_ref[0] ^ i
        for level in range(levels):
            for column in range(WLON):
                half, inside = divmod(column, HALF)
                at = pl.ds(level * HALF + inside, rows, stride=step)
                rest = grid_ref[1, at, :][:, half * side : (half + 1) * side]
                piece = jnp.concatenate([grid_ref[2 * half, at, :], rest], 1)
                out_ref[0, micro, level, :, column * width : (column + 1) * width] = piece.astype(jnp.bfloat16)


def finish(place, pieces, shape):
    tokens = pieces[0].shape[0] // 3
    vmem = pl.BlockSpec(memory_space=pltpu.VMEM)
    return pl.pallas_call(
        finish_kernel,
        out_shape=jax.ShapeDtypeStruct(shape, jnp.bfloat16),
        in_specs=[pl.BlockSpec(memory_space=pltpu.SMEM)] + [vmem] * len(pieces),
        out_specs=vmem,
        scratch_shapes=[pltpu.VMEM((3, tokens, LANES), jnp.float32)],
        compiler_params=pltpu.CompilerParams(vmem_limit_bytes=VMEM_LIMIT),
        name="finish",
    )(place, *pieces)


def on_device(fields, land_mask, land_vector, w_qkv, w_proj, w_up, w_down):
    micro_count, levels, rows, flat_width = fields.shape
    width = land_vector.shape[0]
    tile_count, section_count = lax.axis_size("tile"), lax.axis_size("section")
    section = lax.axis_index("section")
    place = jnp.stack([section % STAGE, section // STAGE]).astype(jnp.int32)
    axes = ("tile", "section")

    def exchange(value, bit):
        return lax.ppermute(value, "section", [(s, s ^ bit) for s in range(section_count)])

    def shift(value, tiles, first, stages=0):
        pairs = [
            (t * section_count + s, (t + tiles) % tile_count * section_count + s + stages * STAGE)
            for t in range(tile_count)
            for s in range(first, first + STAGE)
        ]
        return lax.ppermute(value, axes, pairs)

    tokens = rows * levels * HALF
    tile_shape, half_shape = (3 * tokens, LANES), (2 * tokens, LANES)
    bias = jnp.asarray(window_bias(levels, rows))
    sizes = (tokens, width, bias.shape)

    pack = pack_weights(w_qkv, w_proj, w_up, w_down.transpose(0, 2, 1))
    near, far = exchange(pack, 1), exchange(pack, 2)
    weights = (pack, near, far, exchange(far, 1))
    stack_shape = (STAGE,) + tile_shape

    def even_then_halo(tile, first_section):
        own, west, east = run_stage(
            first_kernel, place, (tile, *weights, bias), (tile_shape, half_shape, half_shape), (), 1, *sizes
        )
        move = functools.partial(shift, first=first_section)
        return move(east, 2), move(own, 1), own, move(own, -1), move(west, -2)

    tiles = even_then_halo(embed(place, fields, land_mask, land_vector.reshape(1, width)), 0)
    last, early = run_stage(
        early_kernel, place, (*tiles, *weights, bias), (tile_shape, stack_shape), (), STAGE, *sizes
    )
    tiles = even_then_halo(shift(last, 0, 0, 1), STAGE)
    outs = run_stage(
        late_kernel, place, (*tiles, *weights, bias, early), (tile_shape,) * STAGE, (stack_shape,), STAGE, *sizes
    )

    pieces = [outs[0]] + [exchange(outs[i], i) for i in range(1, STAGE)]
    return finish(place, pieces, (1, micro_count, levels, rows, flat_width))


def solution(mesh):
    in_specs = (
        P(None, None, None, "tile"),
        P(None, "tile"),
        P(),
        P("section", None, None),
        P("section", None, None),
        P("section", None, None),
        P("section", None, None),
    )
    out_specs = P("section", None, None, None, "tile")
    return jax.shard_map(on_device, mesh=mesh, in_specs=in_specs, out_specs=out_specs, check_vma=False)
```

```python
import functools

import jax
import jax.numpy as jnp
import numpy as np
from jax import lax
from jax.experimental import pallas as pl
from jax.experimental.pallas import tpu as pltpu
from jax.sharding import PartitionSpec as P

HEADS = 6
WZ = 2
WLAT = 6
WLON = 12
HALF = WLON // 2
STAGE = 4
REACH = 2
LOG2E = 1.4426950408889634
LANES = 128
VMEM_LIMIT = 56 * 2**20


def normalize(values):
    center = values - jnp.mean(values, axis=-1, keepdims=True)
    spread = jnp.mean(center * center, axis=-1, keepdims=True)
    return center * lax.rsqrt(spread + 1e-05)


def window_bias(levels, rows):
    lat_blocks = rows // WLAT
    index = np.arange(WLAT * levels * HALF)
    row, level = index // (levels * HALF), index // HALF % levels
    row = row[None] + WLAT * np.arange(lat_blocks)[:, None]

    def label(place, length, window):
        return np.where(place < length - window, 0, np.where(place < length - window // 2, 1, 2))

    labels = label(level, levels, WZ)[None] * 3 + label(row, rows, WLAT)
    keys = np.concatenate([labels, labels], 1)
    return np.where(labels[:, :, None] == keys[:, None, :], 0.0, -1e30).astype(np.float32)


def pack_tile(west, east):
    return jnp.concatenate(
        [west[:, :LANES], jnp.concatenate([west[:, LANES:], east[:, LANES:]], 1), east[:, :LANES]], 0
    )


def unpack_tile(packed, tokens):
    side = packed[tokens : 2 * tokens]
    middle = LANES // 2
    west = jnp.concatenate([packed[:tokens], side[:, :middle]], 1)
    return west, jnp.concatenate([packed[2 * tokens :], side[:, middle:]], 1)


def embed_kernel(micro_ref, fields_ref, mask_ref, vector_ref, tile_ref, grid_ref):
    _, levels, rows, _ = fields_ref.shape
    width = vector_ref.shape[1]
    mask = mask_ref[...].astype(jnp.float32)
    vector = vector_ref[...]
    step = levels * HALF
    for level in range(levels):
        for column in range(WLON):
            piece = fields_ref[0, level, :, column * width : (column + 1) * width].astype(jnp.float32)
            piece = piece + mask[:, column : column + 1] * vector
            half, inside = divmod(column, HALF)
            at = pl.ds(level * HALF + inside, rows, stride=step)
            grid_ref[2 * half, at, :] = piece[:, :LANES]
            grid_ref[2 * half + 1, at, :] = jnp.concatenate([piece[:, LANES:]] * 2, 1)
    tokens, side = rows * step, width - LANES
    tile_ref[:tokens] = grid_ref[0].astype(jnp.bfloat16)
    tile_ref[2 * tokens :] = grid_ref[2].astype(jnp.bfloat16)
    lane = lax.broadcasted_iota(jnp.int32, (1, LANES), 1)
    tile_ref[tokens : 2 * tokens] = jnp.where(lane < side, grid_ref[1], grid_ref[3]).astype(jnp.bfloat16)


def embed(micro, fields, land_mask, land_vector):
    _, levels, rows, flat = fields.shape
    tokens = rows * levels * HALF
    whole = lambda a: pl.BlockSpec(a.shape, lambda i, m: (0,) * a.ndim)
    return pl.pallas_call(
        embed_kernel,
        out_shape=jax.ShapeDtypeStruct((3 * tokens, LANES), jnp.bfloat16),
        grid_spec=pltpu.PrefetchScalarGridSpec(
            num_scalar_prefetch=1,
            grid=(1,),
            in_specs=[pl.BlockSpec((1, levels, rows, flat), lambda i, m: (m[0], 0, 0, 0)),
                      whole(land_mask), whole(land_vector)],
            out_specs=pl.BlockSpec((3 * tokens, LANES), lambda i, m: (0, 0)),
            scratch_shapes=[pltpu.VMEM((4, tokens, LANES), jnp.float32)],
        ),
        compiler_params=pltpu.CompilerParams(vmem_limit_bytes=VMEM_LIMIT),
        name="embed",
    )(micro, fields, land_mask, land_vector)


def pack_kernel(wqkv_ref, wproj_ref, wup_ref, wdown_ref, pack_ref):
    width = wproj_ref.shape[1]
    side = 256 - width
    for i in range(3):
        pack_ref[:, 256 * i : 256 * i + 256] = jnp.concatenate(
            [wqkv_ref[0, :, i * width : (i + 1) * width], wproj_ref[0, :, i * side : (i + 1) * side]], 1
        )
    hidden = wup_ref.shape[2]
    pack_ref[:, 768 : 768 + hidden] = wup_ref[0]
    pack_ref[:, 768 + hidden :] = wdown_ref[0]


def pack_weights(*weights):
    vmem = pl.BlockSpec(memory_space=pltpu.VMEM)
    width = weights[0].shape[1]
    return pl.pallas_call(
        pack_kernel,
        out_shape=jax.ShapeDtypeStruct((width, 2304), jnp.bfloat16),
        in_specs=[vmem] * len(weights),
        out_specs=vmem,
        compiler_params=pltpu.CompilerParams(vmem_limit_bytes=VMEM_LIMIT),
        name="pack_weights",
    )(*weights)


def compute_stage(mode, flags, tile_refs, bias_ref, w_ref, wproj_ref, store, scratch):
    xa, xb, q_ref, k_ref, v_ref, low_ref, high_ref = scratch
    f32, bf16 = jnp.float32, jnp.bfloat16
    halves, tokens, width = xa.shape
    head_size = width // HEADS
    windows, piece, _ = bias_ref.shape
    move = piece // 2
    hidden = (w_ref.shape[2] - 768) // 2
    middle = halves // 2

    channel_head = lax.broadcasted_iota(jnp.int32, (1, width), 1) // head_size
    scale = head_size ** (-0.5) * LOG2E
    ones = jnp.ones((2 * piece, 256 - width), f32)

    def load_tiles():
        into = xb if mode == "rest" else xa
        for i, ref in enumerate(tile_refs):
            distance = (0, 1, 1, 2, 2)[i]
            east = flags[i] if i else 0
            base = middle - 1 - 2 * distance + 4 * distance * east
            if mode == "rest" and distance == REACH:
                main, side = ref[:tokens].astype(f32), ref[tokens:].astype(f32)
                last = jnp.where(east == 1, side[:, : LANES // 2], side[:, LANES // 2 :])
                into[base + 1 - east] = jnp.concatenate([main, last], 1).astype(bf16)
            else:
                for j, part in enumerate(unpack_tile(ref[...].astype(f32), tokens)):
                    into[base + j] = part.astype(bf16)

    def select_heads(parts, first, lanes):
        total = parts[0]
        for n in range(1, len(parts)):
            total = jnp.where(channel_head[:, first : first + lanes] == first // head_size + n, parts[n], total)
        return total

    def window_attention(h, i, w, shifted, exact):
        q = q_ref[h, w * piece : (w + 1) * piece, :]
        qm = jnp.concatenate([jnp.where(channel_head == n, q, 0.0) for n in range(HEADS)], 0).astype(bf16)
        s = lax.dot_general(qm, k_ref[i, w], (((1,), (1,)), ((), ())), preferred_element_type=f32)
        if shifted:
            s = (s.reshape(HEADS, piece, 2 * piece) + bias_ref[w][None]).reshape(HEADS * piece, 2 * piece)
        if exact:
            s = s - jnp.max(s, axis=-1, keepdims=True)
        o = jnp.dot(jnp.exp2(s).astype(bf16), v_ref[i, w], preferred_element_type=f32)
        heads = [o[n * piece : (n + 1) * piece] for n in range(HEADS)]
        full = LANES // head_size
        tops = [select_heads([x[:, :LANES] for x in heads[:full]], 0, LANES),
                select_heads([x[:, LANES:width] for x in heads[full:]], LANES, width - LANES)]
        side = 256 - width
        ends = [x[:, LANES:] for x in heads]
        odd = channel_head[:, :LANES] % 2 == 1
        couples = [jnp.where(odd, ends[n + 1], ends[n]) for n in range(0, HEADS, 2)]
        lane = lax.broadcasted_iota(jnp.int32, (1, LANES), 1)
        sums = [jnp.where(lane < side, pltpu.roll(couples[0], side, 1), couples[1]),
                pltpu.roll(couples[2], side, 1)[:, :side]]
        if not exact:
            low_ref[...] = jnp.minimum(low_ref[...], jnp.min(sums[0].reshape(-1, 8, LANES), axis=0))
            high_ref[...] = jnp.maximum(high_ref[...], jnp.max(sums[0].reshape(-1, 8, LANES), axis=0))
            rest = slice(0, width - LANES)
            low_ref[:, rest] = jnp.minimum(low_ref[:, rest], jnp.min(sums[1].reshape(-1, 8, width - LANES), axis=0))
            high_ref[:, rest] = jnp.maximum(high_ref[:, rest], jnp.max(sums[1].reshape(-1, 8, width - LANES), axis=0))
        return jnp.concatenate([top / total for top, total in zip(tops, sums)], 1)

    def block(b, shifted, exact, together, alone=False):
        source, target = (xb, xa) if shifted else (xa, xb)

        def load(h):
            x = source[h].astype(f32)
            return pltpu.roll(x, tokens - move, 0) if shifted else x

        def pair(i, carry):
            kv = []
            for j in range(2):
                h = b + 2 * i + j
                qkv = jnp.dot(normalize(load(h)).astype(bf16), w_ref[b, :, :768], preferred_element_type=f32)
                q_ref[h] = qkv[:, :width] * scale
                kv.append((qkv[:, 256 : 256 + width], qkv[:, 512 : 512 + width]))
            for w in range(windows):
                at = slice(w * piece, (w + 1) * piece)
                k_ref[i, w] = jnp.concatenate([kv[0][0][at], kv[1][0][at]], 0).astype(bf16)
                v = jnp.concatenate([kv[0][1][at], kv[1][1][at]], 0)
                v_ref[i, w] = jnp.concatenate([v, ones], 1).astype(bf16)
            return carry

        def attend(c, carry):
            own = [(middle - 1 if alone else 1 + b) + together * c + j for j in range(together)]
            x = jnp.concatenate([load(h) for h in own], 0)
            a = jnp.concatenate(
                [window_attention(h, (h - b) // 2, w, shifted, exact) for h in own for w in range(windows)], 0
            ).astype(bf16)
            residual = x + jnp.dot(a, wproj_ref[b], preferred_element_type=f32)
            n2 = normalize(residual).astype(bf16)
            u = jnp.dot(n2, w_ref[b, :, 768 : 768 + hidden], preferred_element_type=f32)
            g = (0.5 * u * (1.0 + lax.erf(u * (0.5**0.5)))).astype(bf16)
            y = residual + lax.dot_general(
                g, w_ref[b, :, 768 + hidden :], (((1,), (1,)), ((), ())), preferred_element_type=f32
            )
            for j, h in enumerate(own):
                part = y[j * tokens : (j + 1) * tokens]
                if shifted:
                    part = pltpu.roll(part, move, 0)
                target[h] = part.astype(bf16)
            return carry

        if alone:
            pair(middle // 2, 0)
            lax.fori_loop(0, 2 // together, attend, 0)
        else:
            lax.fori_loop(0, middle - b, pair, 0)
            lax.fori_loop(0, (halves - 2 - 2 * b) // together, attend, 0)
        store(b, pack_tile(target[middle - 1].astype(f32), target[middle].astype(f32)).astype(bf16))

    def compute(exact, together):
        load_tiles()

        def two_blocks(n, carry):
            if mode == "whole":
                block(2 * n, False, exact, together)
            else:

                @pl.when(n > 0)
                def _():
                    block(2 * n, False, exact, together)

            block(2 * n + 1, True, exact, together)
            return carry

        if mode == "first":
            block(0, False, exact, together, True)
        else:
            lax.fori_loop(0, STAGE // 2, two_blocks, 0)

    low_ref[...] = jnp.ones_like(low_ref)
    high_ref[...] = jnp.ones_like(high_ref)
    compute(False, 2)
    safe = (jnp.min(low_ref[...]) >= 2.0**-90) & (jnp.max(high_ref[...]) <= 2.0**90)

    @pl.when(jnp.logical_not(safe))
    def _():
        compute(True, 1)


def unpack_projection(ref, width):
    return jnp.concatenate([ref[:, 256 * j + width : 256 * j + 256] for j in range(3)], 1)


def gather_weights(place, refs, w_ref, wproj_ref):
    for i, ref in enumerate(refs):
        w_ref[place ^ i] = ref[...]
        wproj_ref[place ^ i] = unpack_projection(ref, wproj_ref.shape[1])


def first_kernel(place_ref, tile_in, w0, w1, w2, w3, bias_ref, tile_ref, p_ref, q_ref, w_ref, wproj_ref, *scratch):
    for i, ref in enumerate((w0, w1, w2, w3)):

        @pl.when(place_ref[0] == i)
        def _(ref=ref):
            w_ref[0] = ref[...]
            wproj_ref[0] = unpack_projection(ref, wproj_ref.shape[1])

    def store(b, packed):
        tile_ref[...] = packed

    compute_stage("first", None, (tile_in,), bias_ref, w_ref, wproj_ref, store, scratch)
    tokens = tile_ref.shape[0] // 3
    for ref, flag in ((p_ref, place_ref[4]), (q_ref, place_ref[5])):
        ref[:tokens] = jnp.where(flag == 1, tile_ref[2 * tokens :].astype(jnp.float32),
                                 tile_ref[:tokens].astype(jnp.float32)).astype(jnp.bfloat16)
        ref[tokens:] = tile_ref[tokens : 2 * tokens]


def flags_of(place_ref):
    return (0,) + tuple(place_ref[2 + i] for i in range(4))


def whole_kernel(place_ref, t0, t1, t2, t3, t4, w0, w1, w2, w3, bias_ref, last_ref, outs_ref,
                 w_ref, wproj_ref, *scratch):
    place = place_ref[0]
    gather_weights(place, (w0, w1, w2, w3), w_ref, wproj_ref)

    def store(b, packed):
        outs_ref[place ^ b] = packed

    compute_stage("whole", flags_of(place_ref), (t0, t1, t2, t3, t4), bias_ref, w_ref, wproj_ref, store, scratch)
    last_ref[...] = outs_ref[place ^ (STAGE - 1)]


def rest_kernel(place_ref, t0, t1, t2, t3, t4, w0, w1, w2, w3, bias_ref, early_ref, o0, o1, o2, o3,
                outs_ref, w_ref, wproj_ref, *scratch):
    place = place_ref[0]
    late = place_ref[1] == 1

    @pl.when(late)
    def _():
        gather_weights(place, (w0, w1, w2, w3), w_ref, wproj_ref)

        def store(b, packed):
            outs_ref[place ^ b] = packed

        store(0, t0[...])
        compute_stage("rest", flags_of(place_ref), (t0, t1, t2, t3, t4), bias_ref, w_ref, wproj_ref, store, scratch)
        for i, ref in enumerate((o0, o1, o2, o3)):
            ref[...] = outs_ref[i]

    @pl.when(jnp.logical_not(late))
    def _():
        for i, ref in enumerate((o0, o1, o2, o3)):
            ref[...] = early_ref[i]


def run_stage(kernel, place, operands, outs, extra, blocks, tokens, width, bias_shape):
    halves = 2 * (2 * REACH + 1)
    windows, piece, _ = bias_shape
    vmem = pl.BlockSpec(memory_space=pltpu.VMEM)
    bf16, f32 = jnp.bfloat16, jnp.float32
    return pl.pallas_call(
        kernel,
        out_shape=tuple(jax.ShapeDtypeStruct(shape, bf16) for shape in outs),
        in_specs=[pl.BlockSpec(memory_space=pltpu.SMEM)] + [vmem] * len(operands),
        out_specs=(vmem,) * len(outs),
        scratch_shapes=[pltpu.VMEM(shape, bf16) for shape in extra]
        + [
            pltpu.VMEM((blocks, width, 2304), bf16),
            pltpu.VMEM((blocks, width, width), bf16),
            pltpu.VMEM((halves, tokens, width), bf16),
            pltpu.VMEM((halves, tokens, width), bf16),
            pltpu.VMEM((halves, tokens, width), f32),
            pltpu.VMEM((halves // 2, windows, 2 * piece, width), bf16),
            pltpu.VMEM((halves // 2, windows, 2 * piece, 256), bf16),
            pltpu.VMEM((8, LANES), f32),
            pltpu.VMEM((8, LANES), f32),
        ],
        compiler_params=pltpu.CompilerParams(vmem_limit_bytes=VMEM_LIMIT),
        name=kernel.__name__,
    )(place, *operands)


def finish_kernel(place_ref, o0, o1, o2, o3, out_ref, grid_ref):
    _, _, levels, rows, _ = out_ref.shape
    tokens = grid_ref.shape[1]
    step = levels * HALF
    width = out_ref.shape[4] // WLON
    side = width - LANES
    for i, ref in enumerate((o0, o1, o2, o3)):
        packed = ref[...].astype(jnp.float32)
        for part in range(3):
            grid_ref[part] = packed[part * tokens : (part + 1) * tokens]
        micro = place_ref[0] ^ i
        for level in range(levels):
            for column in range(WLON):
                half, inside = divmod(column, HALF)
                at = pl.ds(level * HALF + inside, rows, stride=step)
                rest = grid_ref[1, at, :][:, half * side : (half + 1) * side]
                piece = jnp.concatenate([grid_ref[2 * half, at, :], rest], 1)
                out_ref[0, micro, level, :, column * width : (column + 1) * width] = piece.astype(jnp.bfloat16)


def finish(place, pieces, shape):
    tokens = pieces[0].shape[0] // 3
    vmem = pl.BlockSpec(memory_space=pltpu.VMEM)
    return pl.pallas_call(
        finish_kernel,
        out_shape=jax.ShapeDtypeStruct(shape, jnp.bfloat16),
        in_specs=[pl.BlockSpec(memory_space=pltpu.SMEM)] + [vmem] * len(pieces),
        out_specs=vmem,
        scratch_shapes=[pltpu.VMEM((3, tokens, LANES), jnp.float32)],
        compiler_params=pltpu.CompilerParams(vmem_limit_bytes=VMEM_LIMIT),
        name="finish",
    )(place, *pieces)


def on_device(fields, land_mask, land_vector, w_qkv, w_proj, w_up, w_down):
    micro_count, levels, rows, flat_width = fields.shape
    width = land_vector.shape[0]
    tile_count, section_count = lax.axis_size("tile"), lax.axis_size("section")
    section = lax.axis_index("section")
    tile_index = lax.axis_index("tile")
    east_of_pair = tile_index % 2 == 0
    east_of_four = tile_index % 4 < 2
    place = jnp.stack(
        [section % STAGE, section // STAGE, ~east_of_pair, east_of_pair, ~east_of_four, east_of_four]
    ).astype(jnp.int32)
    axes = ("tile", "section")

    def exchange(value, bit):
        return lax.ppermute(value, "section", [(s, s ^ bit) for s in range(section_count)])

    def forward(value):
        return lax.ppermute(value, "section", [(s, s + STAGE) for s in range(STAGE)])

    def swap(values, first):
        received = []
        for value, distance, phase in zip(values, (1, 1, 2, 2), (1, 0, 1, 0)):
            pairs = []
            for t in range(tile_count):
                if t // distance % 2 == phase:
                    for s in range(first, first + STAGE):
                        here, there = t * section_count + s, (t + distance) % tile_count * section_count + s
                        pairs += [(here, there), (there, here)]
            received.append(lax.ppermute(value, axes, pairs))
        return received

    tokens = rows * levels * HALF
    tile_shape, half_shape = (3 * tokens, LANES), (2 * tokens, LANES)
    bias = jnp.asarray(window_bias(levels, rows))
    sizes = (tokens, width, bias.shape)

    pack = pack_weights(w_qkv, w_proj, w_up, w_down.transpose(0, 2, 1))
    near, far = exchange(pack, 1), exchange(pack, 2)
    tile = embed(place, fields, land_mask, land_vector.reshape(1, width))
    halo = swap((tile,) * 4, 0)
    far, halo = lax.optimization_barrier((far, halo))
    weights = (pack, near, far, exchange(far, 1))
    stack_shape = (STAGE,) + tile_shape

    last, early = run_stage(
        whole_kernel, place, (tile, *halo, *weights, bias), (tile_shape, stack_shape), (), STAGE, *sizes
    )
    tile, p, q = run_stage(
        first_kernel, place, (forward(last), *weights, bias), (tile_shape, half_shape, half_shape), (), 1, *sizes
    )
    halo = swap((tile, tile, p, q), STAGE)
    outs = run_stage(
        rest_kernel, place, (tile, *halo, *weights, bias, early), (tile_shape,) * STAGE, (stack_shape,), STAGE, *sizes
    )

    pieces = [outs[0]] + [exchange(outs[i], i) for i in range(1, STAGE)]
    return finish(place, pieces, (1, micro_count, levels, rows, flat_width))


def solution(mesh):
    in_specs = (
        P(None, None, None, "tile"),
        P(None, "tile"),
        P(),
        P("section", None, None),
        P("section", None, None),
        P("section", None, None),
        P("section", None, None),
    )
    out_specs = P("section", None, None, None, "tile")
    return jax.shard_map(on_device, mesh=mesh, in_specs=in_specs, out_specs=out_specs, check_vma=False)
```

```python
import functools

import jax
import jax.numpy as jnp
import numpy as np
from jax import lax
from jax.experimental import pallas as pl
from jax.experimental.pallas import tpu as pltpu
from jax.sharding import PartitionSpec as P

HEADS = 6
WZ = 2
WLAT = 6
WLON = 12
HALF = WLON // 2
STAGE = 4
LOG2E = 1.4426950408889634
LANES = 128
VMEM_LIMIT = 56 * 2**20


def normalize(values):
    center = values - jnp.mean(values, axis=-1, keepdims=True)
    spread = jnp.mean(center * center, axis=-1, keepdims=True)
    return center * lax.rsqrt(spread + 1e-05)


def window_bias(levels, rows):
    lat_blocks = rows // WLAT
    index = np.arange(WLAT * levels * HALF)
    row, level = index // (levels * HALF), index // HALF % levels
    row = row[None] + WLAT * np.arange(lat_blocks)[:, None]

    def label(place, length, window):
        return np.where(place < length - window, 0, np.where(place < length - window // 2, 1, 2))

    labels = label(level, levels, WZ)[None] * 3 + label(row, rows, WLAT)
    keys = np.concatenate([labels, labels], 1)
    return np.where(labels[:, :, None] == keys[:, None, :], 0.0, -1e30).astype(np.float32)


def pack_tile(west, east):
    return jnp.concatenate(
        [west[:, :LANES], jnp.concatenate([west[:, LANES:], east[:, LANES:]], 1), east[:, :LANES]], 0
    )


def unpack_tile(packed, tokens):
    side = packed[tokens : 2 * tokens]
    middle = LANES // 2
    west = jnp.concatenate([packed[:tokens], side[:, :middle]], 1)
    return west, jnp.concatenate([packed[2 * tokens :], side[:, middle:]], 1)


def embed_kernel(micro_ref, fields_ref, mask_ref, vector_ref, tile_ref, grid_ref):
    _, levels, rows, _ = fields_ref.shape
    width = vector_ref.shape[1]
    mask = mask_ref[...].astype(jnp.float32)
    vector = vector_ref[...]
    step = levels * HALF
    for level in range(levels):
        for column in range(WLON):
            piece = fields_ref[0, level, :, column * width : (column + 1) * width].astype(jnp.float32)
            piece = piece + mask[:, column : column + 1] * vector
            half, inside = divmod(column, HALF)
            at = pl.ds(level * HALF + inside, rows, stride=step)
            grid_ref[2 * half, at, :] = piece[:, :LANES]
            grid_ref[2 * half + 1, at, :] = jnp.concatenate([piece[:, LANES:]] * 2, 1)
    tokens, side = rows * step, width - LANES
    tile_ref[:tokens] = grid_ref[0].astype(jnp.bfloat16)
    tile_ref[2 * tokens :] = grid_ref[2].astype(jnp.bfloat16)
    lane = lax.broadcasted_iota(jnp.int32, (1, LANES), 1)
    tile_ref[tokens : 2 * tokens] = jnp.where(lane < side, grid_ref[1], grid_ref[3]).astype(jnp.bfloat16)


def embed(micro, fields, land_mask, land_vector):
    _, levels, rows, flat = fields.shape
    tokens = rows * levels * HALF
    whole = lambda a: pl.BlockSpec(a.shape, lambda i, m: (0,) * a.ndim)
    return pl.pallas_call(
        embed_kernel,
        out_shape=jax.ShapeDtypeStruct((3 * tokens, LANES), jnp.bfloat16),
        grid_spec=pltpu.PrefetchScalarGridSpec(
            num_scalar_prefetch=1,
            grid=(1,),
            in_specs=[pl.BlockSpec((1, levels, rows, flat), lambda i, m: (m[0], 0, 0, 0)),
                      whole(land_mask), whole(land_vector)],
            out_specs=pl.BlockSpec((3 * tokens, LANES), lambda i, m: (0, 0)),
            scratch_shapes=[pltpu.VMEM((4, tokens, LANES), jnp.float32)],
        ),
        compiler_params=pltpu.CompilerParams(vmem_limit_bytes=VMEM_LIMIT),
        name="embed",
    )(micro, fields, land_mask, land_vector)


def pack_kernel(wqkv_ref, wproj_ref, wup_ref, wdown_ref, pack_ref):
    width = wproj_ref.shape[1]
    side = 256 - width
    for i in range(3):
        pack_ref[:, 256 * i : 256 * i + 256] = jnp.concatenate(
            [wqkv_ref[0, :, i * width : (i + 1) * width], wproj_ref[0, :, i * side : (i + 1) * side]], 1
        )
    hidden = wup_ref.shape[2]
    pack_ref[:, 768 : 768 + hidden] = wup_ref[0]
    pack_ref[:, 768 + hidden :] = wdown_ref[0]


def pack_weights(*weights):
    vmem = pl.BlockSpec(memory_space=pltpu.VMEM)
    width = weights[0].shape[1]
    return pl.pallas_call(
        pack_kernel,
        out_shape=jax.ShapeDtypeStruct((width, 2304), jnp.bfloat16),
        in_specs=[vmem] * len(weights),
        out_specs=vmem,
        compiler_params=pltpu.CompilerParams(vmem_limit_bytes=VMEM_LIMIT),
        name="pack_weights",
    )(*weights)


def compute_blocks(mode, flags, tile_refs, bias_ref, w_ref, wproj_ref, store, scratch):
    xa, xb, q_ref, k_ref, v_ref, low_ref, high_ref = scratch
    f32, bf16 = jnp.float32, jnp.bfloat16
    halves, tokens, width = xa.shape
    head_size = width // HEADS
    windows, piece, _ = bias_ref.shape
    move = piece // 2
    hidden = (w_ref.shape[2] - 768) // 2
    channel_head = lax.broadcasted_iota(jnp.int32, (1, width), 1) // head_size
    scale = head_size ** (-0.5) * LOG2E
    ones = jnp.ones((2 * piece, 256 - width), f32)

    def load_tiles():
        into = xb if mode.startswith("odd") else xa
        for i, ref in enumerate(tile_refs):
            if ref.shape[0] == 3 * tokens:
                base = 4 * flags[i - 1] if i else 2
                for j, part in enumerate(unpack_tile(ref[...].astype(f32), tokens)):
                    into[base + j] = part.astype(bf16)
            else:
                east = flags[i - 1]
                main, side = ref[:tokens].astype(f32), ref[tokens:].astype(f32)
                last = jnp.where(east == 1, side[:, : LANES // 2], side[:, LANES // 2 :])
                into[1 + 3 * east] = jnp.concatenate([main, last], 1).astype(bf16)

    def select_heads(parts, first, lanes):
        total = parts[0]
        for n in range(1, len(parts)):
            total = jnp.where(channel_head[:, first : first + lanes] == first // head_size + n, parts[n], total)
        return total

    def window_attention(h, i, w, shifted, exact):
        q = q_ref[h, w * piece : (w + 1) * piece, :]
        qm = jnp.concatenate([jnp.where(channel_head == n, q, 0.0) for n in range(HEADS)], 0).astype(bf16)
        s = lax.dot_general(qm, k_ref[i, w], (((1,), (1,)), ((), ())), preferred_element_type=f32)
        if shifted:
            s = (s.reshape(HEADS, piece, 2 * piece) + bias_ref[w][None]).reshape(HEADS * piece, 2 * piece)
        if exact:
            s = s - jnp.max(s, axis=-1, keepdims=True)
        o = jnp.dot(jnp.exp2(s).astype(bf16), v_ref[i, w], preferred_element_type=f32)
        heads = [o[n * piece : (n + 1) * piece] for n in range(HEADS)]
        full = LANES // head_size
        tops = [select_heads([x[:, :LANES] for x in heads[:full]], 0, LANES),
                select_heads([x[:, LANES:width] for x in heads[full:]], LANES, width - LANES)]
        side = 256 - width
        ends = [x[:, LANES:] for x in heads]
        odd = channel_head[:, :LANES] % 2 == 1
        couples = [jnp.where(odd, ends[n + 1], ends[n]) for n in range(0, HEADS, 2)]
        lane = lax.broadcasted_iota(jnp.int32, (1, LANES), 1)
        sums = [jnp.where(lane < side, pltpu.roll(couples[0], side, 1), couples[1]),
                pltpu.roll(couples[2], side, 1)[:, :side]]
        if not exact:
            low_ref[...] = jnp.minimum(low_ref[...], jnp.min(sums[0].reshape(-1, 8, LANES), axis=0))
            high_ref[...] = jnp.maximum(high_ref[...], jnp.max(sums[0].reshape(-1, 8, LANES), axis=0))
            rest = slice(0, width - LANES)
            low_ref[:, rest] = jnp.minimum(low_ref[:, rest], jnp.min(sums[1].reshape(-1, 8, width - LANES), axis=0))
            high_ref[:, rest] = jnp.maximum(high_ref[:, rest], jnp.max(sums[1].reshape(-1, 8, width - LANES), axis=0))
        return jnp.concatenate([top / total for top, total in zip(tops, sums)], 1)

    def block(b, shifted, exact, together, first_pair, pairs, first_q, count):
        source, target = (xb, xa) if shifted else (xa, xb)

        def load(h):
            x = source[h].astype(f32)
            return pltpu.roll(x, tokens - move, 0) if shifted else x

        def pair(i, carry):
            kv = []
            for j in range(2):
                h = first_pair + 2 * i + j
                qkv = jnp.dot(normalize(load(h)).astype(bf16), w_ref[b, :, :768], preferred_element_type=f32)
                q_ref[h] = qkv[:, :width] * scale
                kv.append((qkv[:, 256 : 256 + width], qkv[:, 512 : 512 + width]))
            for w in range(windows):
                at = slice(w * piece, (w + 1) * piece)
                k_ref[i, w] = jnp.concatenate([kv[0][0][at], kv[1][0][at]], 0).astype(bf16)
                v = jnp.concatenate([kv[0][1][at], kv[1][1][at]], 0)
                v_ref[i, w] = jnp.concatenate([v, ones], 1).astype(bf16)
            return carry

        def attend(c, carry):
            own = [first_q + together * c + j for j in range(together)]
            x = jnp.concatenate([load(h) for h in own], 0)
            a = jnp.concatenate(
                [window_attention(h, (h - first_pair) // 2, w, shifted, exact) for h in own for w in range(windows)], 0
            ).astype(bf16)
            residual = x + jnp.dot(a, wproj_ref[b], preferred_element_type=f32)
            n2 = normalize(residual).astype(bf16)
            u = jnp.dot(n2, w_ref[b, :, 768 : 768 + hidden], preferred_element_type=f32)
            g = (0.5 * u * (1.0 + lax.erf(u * (0.5**0.5)))).astype(bf16)
            y = residual + lax.dot_general(
                g, w_ref[b, :, 768 + hidden :], (((1,), (1,)), ((), ())), preferred_element_type=f32
            )
            for j, h in enumerate(own):
                part = y[j * tokens : (j + 1) * tokens]
                if shifted:
                    part = pltpu.roll(part, move, 0)
                target[h] = part.astype(bf16)
            return carry

        lax.fori_loop(0, pairs, pair, 0)
        lax.fori_loop(0, count // together, attend, 0)
        store(b, pack_tile(target[2].astype(f32), target[3].astype(f32)).astype(bf16))

    def compute(exact, together):
        load_tiles()

        def odd(b):
            block(b, True, exact, together, 1, 2, 2, 2)

        def even(b):
            block(b, False, exact, together, 2, 1, 2, 2)

        def wide_even(n, carry):
            block(2 * n, False, exact, together, 2 * n, 3 - 2 * n, 1 + n, 4 - 2 * n)
            pl.when(n == 0)(lambda: odd(1))
            return carry

        if mode == "wide even":
            lax.fori_loop(0, 2, wide_even, 0)
        elif mode == "even":
            even(0)
        else:
            odd(0)
            if mode == "odd even":
                even(1)

    low_ref[...] = jnp.ones_like(low_ref)
    high_ref[...] = jnp.ones_like(high_ref)
    compute(False, 2)
    safe = (jnp.min(low_ref[...]) >= 2.0**-90) & (jnp.max(high_ref[...]) <= 2.0**90)

    @pl.when(jnp.logical_not(safe))
    def _():
        compute(True, 1)


def unpack_projection(ref, width):
    return jnp.concatenate([ref[:, 256 * j + width : 256 * j + 256] for j in range(3)], 1)


def gather_weights(place, refs, blocks, w_ref, wproj_ref):
    for i, ref in enumerate(refs):
        b = place ^ i

        @pl.when((b >= blocks[0]) & (b <= blocks[-1]))
        def _(ref=ref, slot=b - blocks[0]):
            w_ref[slot] = ref[...]
            wproj_ref[slot] = unpack_projection(ref, wproj_ref.shape[1])


def store_halves(place_ref, tile_ref, o_ref, e_ref):
    tokens = tile_ref.shape[0] // 3
    for ref, flag in ((o_ref, place_ref[2]), (e_ref, place_ref[3])):
        ref[:tokens] = jnp.where(flag == 1, tile_ref[2 * tokens :].astype(jnp.float32),
                                 tile_ref[:tokens].astype(jnp.float32)).astype(jnp.bfloat16)
        ref[tokens:] = tile_ref[tokens : 2 * tokens]


def part_kernel(mode, blocks, tile_count, place_ref, *refs):
    tiles, refs = refs[:tile_count], refs[tile_count:]
    weights, bias_ref, refs = refs[:STAGE], refs[STAGE], refs[STAGE + 1 :]
    outs, refs = refs[: len(blocks)], refs[len(blocks) :]
    halves = ()
    if mode != "odd":
        halves, refs = refs[:2], refs[2:]
    w_ref, wproj_ref, stage_ref, *scratch = refs
    gather_weights(place_ref[0], weights, blocks, w_ref, wproj_ref)

    def store(slot, packed):
        stage_ref[slot] = packed

    flags = (place_ref[2], place_ref[3])
    compute_blocks(mode, flags, tiles, bias_ref, w_ref, wproj_ref, store, scratch)
    for i, ref in enumerate(outs):
        ref[...] = stage_ref[i]
    if halves:
        store_halves(place_ref, outs[-1], *halves)


def last_kernel(place_ref, *refs):
    tiles, refs = refs[:3], refs[3:]
    weights, bias_ref, refs = refs[:STAGE], refs[STAGE], refs[STAGE + 1 :]
    early, late, refs = refs[:STAGE], refs[STAGE : 2 * STAGE - 1], refs[2 * STAGE - 1 :]
    outs, refs = refs[:STAGE], refs[STAGE:]
    w_ref, wproj_ref, stage_ref, *scratch = refs
    place = place_ref[0]

    def route(sources):
        for i, ref in enumerate(outs):
            for b, source in enumerate(sources):

                @pl.when((place ^ i) == b)
                def _(ref=ref, source=source):
                    ref[...] = source[...]

    @pl.when(place_ref[1] == 1)
    def _():
        gather_weights(place, weights, (STAGE - 1,), w_ref, wproj_ref)

        def store(slot, packed):
            stage_ref[slot] = packed

        flags = (place_ref[2], place_ref[3])
        compute_blocks("odd", flags, tiles, bias_ref, w_ref, wproj_ref, store, scratch)
        route((*late, stage_ref.at[0]))

    @pl.when(place_ref[1] == 0)
    def _():
        route(early)


def run_part(kernel, name, place, operands, outs, blocks, tokens, width, bias_shape):
    halves = 6
    windows, piece, _ = bias_shape
    vmem = pl.BlockSpec(memory_space=pltpu.VMEM)
    bf16, f32 = jnp.bfloat16, jnp.float32
    return pl.pallas_call(
        kernel,
        out_shape=tuple(jax.ShapeDtypeStruct(shape, bf16) for shape in outs),
        in_specs=[pl.BlockSpec(memory_space=pltpu.SMEM)] + [vmem] * len(operands),
        out_specs=(vmem,) * len(outs),
        scratch_shapes=[
            pltpu.VMEM((blocks, width, 2304), bf16),
            pltpu.VMEM((blocks, width, width), bf16),
            pltpu.VMEM((blocks, 3 * tokens, LANES), bf16),
            pltpu.VMEM((halves, tokens, width), bf16),
            pltpu.VMEM((halves, tokens, width), bf16),
            pltpu.VMEM((halves, tokens, width), f32),
            pltpu.VMEM((halves // 2, windows, 2 * piece, width), bf16),
            pltpu.VMEM((halves // 2, windows, 2 * piece, 256), bf16),
            pltpu.VMEM((8, LANES), f32),
            pltpu.VMEM((8, LANES), f32),
        ],
        compiler_params=pltpu.CompilerParams(vmem_limit_bytes=VMEM_LIMIT),
        name=name,
    )(place, *operands)


def finish_kernel(place_ref, o0, o1, o2, o3, out_ref, grid_ref):
    _, _, levels, rows, _ = out_ref.shape
    tokens = grid_ref.shape[1]
    step = levels * HALF
    width = out_ref.shape[4] // WLON
    side = width - LANES
    for i, ref in enumerate((o0, o1, o2, o3)):
        packed = ref[...].astype(jnp.float32)
        for part in range(3):
            grid_ref[part] = packed[part * tokens : (part + 1) * tokens]
        micro = place_ref[0] ^ i
        for level in range(levels):
            for column in range(WLON):
                half, inside = divmod(column, HALF)
                at = pl.ds(level * HALF + inside, rows, stride=step)
                rest = grid_ref[1, at, :][:, half * side : (half + 1) * side]
                piece = jnp.concatenate([grid_ref[2 * half, at, :], rest], 1)
                out_ref[0, micro, level, :, column * width : (column + 1) * width] = piece.astype(jnp.bfloat16)


def finish(place, pieces, shape):
    tokens = pieces[0].shape[0] // 3
    vmem = pl.BlockSpec(memory_space=pltpu.VMEM)
    return pl.pallas_call(
        finish_kernel,
        out_shape=jax.ShapeDtypeStruct(shape, jnp.bfloat16),
        in_specs=[pl.BlockSpec(memory_space=pltpu.SMEM)] + [vmem] * len(pieces),
        out_specs=vmem,
        scratch_shapes=[pltpu.VMEM((3, tokens, LANES), jnp.float32)],
        compiler_params=pltpu.CompilerParams(vmem_limit_bytes=VMEM_LIMIT),
        name="finish",
    )(place, *pieces)


def on_device(fields, land_mask, land_vector, w_qkv, w_proj, w_up, w_down):
    micro_count, levels, rows, flat_width = fields.shape
    width = land_vector.shape[0]
    tile_count, section_count = lax.axis_size("tile"), lax.axis_size("section")
    section = lax.axis_index("section")
    tile_index = lax.axis_index("tile")
    place = jnp.stack([section % STAGE, section // STAGE, tile_index % 2, 1 - tile_index % 2]).astype(jnp.int32)
    axes = ("tile", "section")

    def exchange(value, bit):
        return lax.ppermute(value, "section", [(s, s ^ bit) for s in range(section_count)])

    def forward(value):
        return lax.ppermute(value, "section", [(s, s + STAGE) for s in range(STAGE)])

    def swap(odd_value, even_value, first):
        received = []
        for value, phase in ((odd_value, 1), (even_value, 0)):
            pairs = []
            for t in range(phase, tile_count, 2):
                for s in range(first, first + STAGE):
                    here, there = t * section_count + s, (t + 1) % tile_count * section_count + s
                    pairs += [(here, there), (there, here)]
            received.append(lax.ppermute(value, axes, pairs))
        return received

    tokens = rows * levels * HALF
    tile_shape, half_shape = (3 * tokens, LANES), (2 * tokens, LANES)
    bias = jnp.asarray(window_bias(levels, rows))
    sizes = (tokens, width, bias.shape)

    pack = pack_weights(w_qkv, w_proj, w_up, w_down.transpose(0, 2, 1))
    near, far = exchange(pack, 1), exchange(pack, 2)
    tile = embed(place, fields, land_mask, land_vector.reshape(1, width))
    halo = swap(tile, tile, 0)
    far, halo = lax.optimization_barrier((far, halo))
    weights = (pack, near, far, exchange(far, 1))

    def part(mode, name, blocks, tiles):
        shapes = (tile_shape,) * len(blocks) + (() if mode == "odd" else (half_shape,) * 2)
        kernel = functools.partial(part_kernel, mode, blocks, len(tiles))
        return run_part(kernel, name, place, (*tiles, *weights, bias), shapes, len(blocks), *sizes)

    y0, y1, y2, o, e = part("wide even", "blocks_0_2", (0, 1, 2), (tile, *halo))
    (y3,) = part("odd", "block_3", (3,), (y2, *swap(o, e, 0)))
    y4, o, e = part("even", "block_4", (0,), (forward(y3),))
    y5, y6, o, e = part("odd even", "blocks_5_6", (1, 2), (y4, *swap(o, e, STAGE)))
    operands = (y6, *swap(o, e, STAGE), *weights, bias, y0, y1, y2, y3, y4, y5, y6)
    outs = run_part(last_kernel, "block_7", place, operands, (tile_shape,) * STAGE, 1, *sizes)

    pieces = [outs[0]] + [exchange(outs[i], i) for i in range(1, STAGE)]
    return finish(place, pieces, (1, micro_count, levels, rows, flat_width))


def solution(mesh):
    in_specs = (
        P(None, None, None, "tile"),
        P(None, "tile"),
        P(),
        P("section", None, None),
        P("section", None, None),
        P("section", None, None),
        P("section", None, None),
    )
    out_specs = P("section", None, None, None, "tile")
    return jax.shard_map(on_device, mesh=mesh, in_specs=in_specs, out_specs=out_specs, check_vma=False)
```

```python
import functools

import jax
import jax.numpy as jnp
import numpy as np
from jax import lax
from jax.experimental import pallas as pl
from jax.experimental.pallas import tpu as pltpu
from jax.sharding import PartitionSpec as P

HEADS = 6
WZ = 2
WLAT = 6
WLON = 12
HALF = WLON // 2
STAGE = 4
LOG2E = 1.4426950408889634
LANES = 128
VMEM_LIMIT = 36 * 2**20


def in_vmem(value):
    return pltpu.with_memory_space_constraint(value, pltpu.VMEM)


def normalize(values):
    center = values - jnp.mean(values, axis=-1, keepdims=True)
    spread = jnp.mean(center * center, axis=-1, keepdims=True)
    return center * lax.rsqrt(spread + 1e-05)


def window_bias(levels, rows):
    lat_blocks = rows // WLAT
    index = np.arange(WLAT * levels * HALF)
    row, level = index // (levels * HALF), index // HALF % levels
    row = row[None] + WLAT * np.arange(lat_blocks)[:, None]

    def label(place, length, window):
        return np.where(place < length - window, 0, np.where(place < length - window // 2, 1, 2))

    labels = label(level, levels, WZ)[None] * 3 + label(row, rows, WLAT)
    keys = np.concatenate([labels, labels], 1)
    return np.where(labels[:, :, None] == keys[:, None, :], 0.0, -1e30).astype(np.float32)


def pack_tile(west, east):
    return jnp.concatenate(
        [west[:, :LANES], jnp.concatenate([west[:, LANES:], east[:, LANES:]], 1), east[:, :LANES]], 0
    )


def unpack_tile(packed, tokens):
    side = packed[tokens : 2 * tokens]
    middle = LANES // 2
    west = jnp.concatenate([packed[:tokens], side[:, :middle]], 1)
    return west, jnp.concatenate([packed[2 * tokens :], side[:, middle:]], 1)


def embed_kernel(micro_ref, fields_ref, mask_ref, vector_ref, tile_ref, grid_ref):
    _, levels, rows, _ = fields_ref.shape
    width = vector_ref.shape[1]
    mask = mask_ref[...].astype(jnp.float32)
    vector = vector_ref[...]
    step = levels * HALF
    for level in range(levels):
        for column in range(WLON):
            piece = fields_ref[0, level, :, column * width : (column + 1) * width].astype(jnp.float32)
            piece = piece + mask[:, column : column + 1] * vector
            half, inside = divmod(column, HALF)
            at = pl.ds(level * HALF + inside, rows, stride=step)
            grid_ref[2 * half, at, :] = piece[:, :LANES]
            grid_ref[2 * half + 1, at, :] = jnp.concatenate([piece[:, LANES:]] * 2, 1)
    tokens, side = rows * step, width - LANES
    tile_ref[:tokens] = grid_ref[0].astype(jnp.bfloat16)
    tile_ref[2 * tokens :] = grid_ref[2].astype(jnp.bfloat16)
    lane = lax.broadcasted_iota(jnp.int32, (1, LANES), 1)
    tile_ref[tokens : 2 * tokens] = jnp.where(lane < side, grid_ref[1], grid_ref[3]).astype(jnp.bfloat16)


def embed(micro, fields, land_mask, land_vector):
    _, levels, rows, flat = fields.shape
    tokens = rows * levels * HALF
    whole = lambda a: pl.BlockSpec(a.shape, lambda i, m: (0,) * a.ndim)
    return pl.pallas_call(
        embed_kernel,
        out_shape=pltpu.VMEM((3 * tokens, LANES), jnp.bfloat16),
        grid_spec=pltpu.PrefetchScalarGridSpec(
            num_scalar_prefetch=1,
            grid=(1,),
            in_specs=[pl.BlockSpec((1, levels, rows, flat), lambda i, m: (m[0], 0, 0, 0)),
                      whole(land_mask), whole(land_vector)],
            out_specs=pl.BlockSpec((3 * tokens, LANES), lambda i, m: (0, 0)),
            scratch_shapes=[pltpu.VMEM((4, tokens, LANES), jnp.float32)],
        ),
        compiler_params=pltpu.CompilerParams(vmem_limit_bytes=VMEM_LIMIT),
        name="embed",
    )(micro, fields, land_mask, land_vector)


def pack_kernel(wqkv_ref, wproj_ref, wup_ref, wdown_ref, pack_ref):
    width = wproj_ref.shape[1]
    side = 256 - width
    for i in range(3):
        pack_ref[:, 256 * i : 256 * i + 256] = jnp.concatenate(
            [wqkv_ref[0, :, i * width : (i + 1) * width], wproj_ref[0, :, i * side : (i + 1) * side]], 1
        )
    hidden = wup_ref.shape[2]
    pack_ref[:, 768 : 768 + hidden] = wup_ref[0]
    pack_ref[:, 768 + hidden :] = wdown_ref[0]


def pack_weights(*weights):
    vmem = pl.BlockSpec(memory_space=pltpu.VMEM)
    width = weights[0].shape[1]
    return pl.pallas_call(
        pack_kernel,
        out_shape=pltpu.VMEM((width, 2304), jnp.bfloat16),
        in_specs=[vmem] * len(weights),
        out_specs=vmem,
        compiler_params=pltpu.CompilerParams(vmem_limit_bytes=VMEM_LIMIT),
        name="pack_weights",
    )(*weights)


def compute_blocks(mode, flags, tile_refs, bias_ref, w_ref, wproj_ref, store, scratch):
    xa, xb, q_ref, k_ref, v_ref, low_ref, high_ref = scratch
    f32, bf16 = jnp.float32, jnp.bfloat16
    halves, tokens, width = xa.shape
    head_size = width // HEADS
    windows, piece, _ = bias_ref.shape
    move = piece // 2
    hidden = (w_ref.shape[2] - 768) // 2
    channel_head = lax.broadcasted_iota(jnp.int32, (1, width), 1) // head_size
    scale = head_size ** (-0.5) * LOG2E
    ones = jnp.ones((2 * piece, 256 - width), f32)

    def load_tiles():
        into = xb if mode.startswith("odd") else xa
        for i, ref in enumerate(tile_refs):
            if ref.shape[0] == 3 * tokens:
                base = 4 * flags[i - 1] if i else 2
                for j, part in enumerate(unpack_tile(ref[...].astype(f32), tokens)):
                    into[base + j] = part.astype(bf16)
            else:
                east = flags[i - 1]
                main, side = ref[:tokens].astype(f32), ref[tokens:].astype(f32)
                last = jnp.where(east == 1, side[:, : LANES // 2], side[:, LANES // 2 :])
                into[1 + 3 * east] = jnp.concatenate([main, last], 1).astype(bf16)

    def select_heads(parts, first, lanes):
        total = parts[0]
        for n in range(1, len(parts)):
            total = jnp.where(channel_head[:, first : first + lanes] == first // head_size + n, parts[n], total)
        return total

    def rows_of(w):
        return pl.ds(w * piece if isinstance(w, int) else pl.multiple_of(w * piece, 8), piece)

    def window_attention(h, i, w, shifted, exact):
        q = q_ref[h, rows_of(w), :]
        qm = jnp.concatenate([jnp.where(channel_head == n, q, 0.0) for n in range(HEADS)], 0).astype(bf16)
        s = lax.dot_general(qm, k_ref[i, w], (((1,), (1,)), ((), ())), preferred_element_type=f32)
        if shifted:
            s = (s.reshape(HEADS, piece, 2 * piece) + bias_ref[w][None]).reshape(HEADS * piece, 2 * piece)
        if exact:
            s = s - jnp.max(s, axis=-1, keepdims=True)
        o = jnp.dot(jnp.exp2(s).astype(bf16), v_ref[i, w], preferred_element_type=f32)
        heads = [o[n * piece : (n + 1) * piece] for n in range(HEADS)]
        full = LANES // head_size
        tops = [select_heads([x[:, :LANES] for x in heads[:full]], 0, LANES),
                select_heads([x[:, LANES:width] for x in heads[full:]], LANES, width - LANES)]
        side = 256 - width
        ends = [x[:, LANES:] for x in heads]
        odd = channel_head[:, :LANES] % 2 == 1
        couples = [jnp.where(odd, ends[n + 1], ends[n]) for n in range(0, HEADS, 2)]
        lane = lax.broadcasted_iota(jnp.int32, (1, LANES), 1)
        sums = [jnp.where(lane < side, pltpu.roll(couples[0], side, 1), couples[1]),
                pltpu.roll(couples[2], side, 1)[:, :side]]
        if not exact:
            low_ref[...] = jnp.minimum(low_ref[...], jnp.min(sums[0].reshape(-1, 8, LANES), axis=0))
            high_ref[...] = jnp.maximum(high_ref[...], jnp.max(sums[0].reshape(-1, 8, LANES), axis=0))
            rest = slice(0, width - LANES)
            low_ref[:, rest] = jnp.minimum(low_ref[:, rest], jnp.min(sums[1].reshape(-1, 8, width - LANES), axis=0))
            high_ref[:, rest] = jnp.maximum(high_ref[:, rest], jnp.max(sums[1].reshape(-1, 8, width - LANES), axis=0))
        return jnp.concatenate([top / total for top, total in zip(tops, sums)], 1)

    def block(b, shifted, exact, together, first_pair, pairs, first_q, count):
        source, target = (xb, xa) if shifted else (xa, xb)

        def load(h):
            x = source[h].astype(f32)
            return pltpu.roll(x, tokens - move, 0) if shifted else x

        def pair(i, carry):
            kv = []
            for j in range(2):
                h = first_pair + 2 * i + j
                qkv = jnp.dot(normalize(load(h)).astype(bf16), w_ref[b, :, :768], preferred_element_type=f32)
                q_ref[h] = qkv[:, :width] * scale
                kv.append((qkv[:, 256 : 256 + width], qkv[:, 512 : 512 + width]))
            for w in range(windows):
                at = slice(w * piece, (w + 1) * piece)
                k_ref[i, w] = jnp.concatenate([kv[0][0][at], kv[1][0][at]], 0).astype(bf16)
                v = jnp.concatenate([kv[0][1][at], kv[1][1][at]], 0)
                v_ref[i, w] = jnp.concatenate([v, ones], 1).astype(bf16)
            return carry

        def attend(c, carry):
            own = [first_q + together * c + j for j in range(together)]
            x = jnp.concatenate([load(h) for h in own], 0)
            if exact:

                def one_window(w, carry):
                    for h in own:
                        q_ref[h, rows_of(w), :] = window_attention(h, (h - first_pair) // 2, w, shifted, exact)
                    return carry

                lax.fori_loop(0, windows, one_window, 0)
                a = jnp.concatenate([q_ref[h] for h in own], 0).astype(bf16)
            else:
                parts = [
                    window_attention(h, (h - first_pair) // 2, w, shifted, exact) for h in own for w in range(windows)
                ]
                a = jnp.concatenate(parts, 0).astype(bf16)
            residual = x + jnp.dot(a, wproj_ref[b], preferred_element_type=f32)
            n2 = normalize(residual).astype(bf16)
            u = jnp.dot(n2, w_ref[b, :, 768 : 768 + hidden], preferred_element_type=f32)
            g = (0.5 * u * (1.0 + lax.erf(u * (0.5**0.5)))).astype(bf16)
            y = residual + lax.dot_general(
                g, w_ref[b, :, 768 + hidden :], (((1,), (1,)), ((), ())), preferred_element_type=f32
            )
            for j, h in enumerate(own):
                part = y[j * tokens : (j + 1) * tokens]
                if shifted:
                    part = pltpu.roll(part, move, 0)
                target[h] = part.astype(bf16)
            return carry

        lax.fori_loop(0, pairs, pair, 0)
        lax.fori_loop(0, count // together, attend, 0)
        store(b, pack_tile(target[2].astype(f32), target[3].astype(f32)).astype(bf16))

    def compute(exact, together):
        load_tiles()

        def odd(b):
            block(b, True, exact, together, 1, 2, 2, 2)

        def even(b):
            block(b, False, exact, together, 2, 1, 2, 2)

        def wide_even(n, carry):
            block(2 * n, False, exact, together, 2 * n, 3 - 2 * n, 1 + n, 4 - 2 * n)
            pl.when(n == 0)(lambda: odd(1))
            return carry

        if mode == "wide even":
            lax.fori_loop(0, 2, wide_even, 0)
        elif mode == "even":
            even(0)
        else:
            odd(0)
            if mode == "odd even":
                even(1)

    low_ref[...] = jnp.ones_like(low_ref)
    high_ref[...] = jnp.ones_like(high_ref)
    compute(False, 2)
    safe = (jnp.min(low_ref[...]) >= 2.0**-90) & (jnp.max(high_ref[...]) <= 2.0**90)

    @pl.when(jnp.logical_not(safe))
    def _():
        compute(True, 1)


def unpack_projection(ref, width):
    return jnp.concatenate([ref[:, 256 * j + width : 256 * j + 256] for j in range(3)], 1)


def gather_weights(place, refs, blocks, w_ref, wproj_ref):
    for i, ref in enumerate(refs):
        b = place ^ i

        @pl.when((b >= blocks[0]) & (b <= blocks[-1]))
        def _(ref=ref, slot=b - blocks[0]):
            w_ref[slot] = ref[...]
            wproj_ref[slot] = unpack_projection(ref, wproj_ref.shape[1])


def store_halves(place_ref, tile_ref, o_ref, e_ref):
    tokens = tile_ref.shape[0] // 3
    for ref, flag in ((o_ref, place_ref[2]), (e_ref, place_ref[3])):
        ref[:tokens] = jnp.where(flag == 1, tile_ref[2 * tokens :].astype(jnp.float32),
                                 tile_ref[:tokens].astype(jnp.float32)).astype(jnp.bfloat16)
        ref[tokens:] = tile_ref[tokens : 2 * tokens]


def part_kernel(mode, blocks, tile_count, place_ref, *refs):
    tiles, refs = refs[:tile_count], refs[tile_count:]
    weights, bias_ref, refs = refs[:STAGE], refs[STAGE], refs[STAGE + 1 :]
    outs, refs = refs[: len(blocks)], refs[len(blocks) :]
    halves = ()
    if mode != "odd":
        halves, refs = refs[:2], refs[2:]
    w_ref, wproj_ref, stage_ref, *scratch = refs
    gather_weights(place_ref[0], weights, blocks, w_ref, wproj_ref)

    def store(slot, packed):
        stage_ref[slot] = packed

    flags = (place_ref[2], place_ref[3])
    compute_blocks(mode, flags, tiles, bias_ref, w_ref, wproj_ref, store, scratch)
    for i, ref in enumerate(outs):
        ref[...] = stage_ref[i]
    if halves:
        store_halves(place_ref, outs[-1], *halves)


def last_kernel(place_ref, *refs):
    tiles, refs = refs[:3], refs[3:]
    weights, bias_ref, refs = refs[:STAGE], refs[STAGE], refs[STAGE + 1 :]
    early, late, refs = refs[:STAGE], refs[STAGE : 2 * STAGE - 1], refs[2 * STAGE - 1 :]
    outs, refs = refs[:STAGE], refs[STAGE:]
    w_ref, wproj_ref, stage_ref, *scratch = refs
    place = place_ref[0]

    def route(sources):
        for i, ref in enumerate(outs):
            for b, source in enumerate(sources):

                @pl.when((place ^ i) == b)
                def _(ref=ref, source=source):
                    ref[...] = source[...]

    @pl.when(place_ref[1] == 1)
    def _():
        gather_weights(place, weights, (STAGE - 1,), w_ref, wproj_ref)

        def store(slot, packed):
            stage_ref[slot] = packed

        flags = (place_ref[2], place_ref[3])
        compute_blocks("odd", flags, tiles, bias_ref, w_ref, wproj_ref, store, scratch)
        route((*late, stage_ref.at[0]))

    @pl.when(place_ref[1] == 0)
    def _():
        route(early)


def run_part(kernel, name, place, operands, outs, blocks, tokens, width, bias_shape):
    halves = 6
    windows, piece, _ = bias_shape
    vmem = pl.BlockSpec(memory_space=pltpu.VMEM)
    bf16, f32 = jnp.bfloat16, jnp.float32
    return pl.pallas_call(
        kernel,
        out_shape=tuple(pltpu.VMEM(shape, bf16) for shape in outs),
        in_specs=[pl.BlockSpec(memory_space=pltpu.SMEM)] + [vmem] * len(operands),
        out_specs=(vmem,) * len(outs),
        scratch_shapes=[
            pltpu.VMEM((blocks, width, 2304), bf16),
            pltpu.VMEM((blocks, width, width), bf16),
            pltpu.VMEM((blocks, 3 * tokens, LANES), bf16),
            pltpu.VMEM((halves, tokens, width), bf16),
            pltpu.VMEM((halves, tokens, width), bf16),
            pltpu.VMEM((halves, tokens, width), f32),
            pltpu.VMEM((halves // 2, windows, 2 * piece, width), bf16),
            pltpu.VMEM((halves // 2, windows, 2 * piece, 256), bf16),
            pltpu.VMEM((8, LANES), f32),
            pltpu.VMEM((8, LANES), f32),
        ],
        compiler_params=pltpu.CompilerParams(vmem_limit_bytes=VMEM_LIMIT),
        name=name,
    )(place, *[in_vmem(x) for x in operands])


def finish_kernel(place_ref, o0, o1, o2, o3, out_ref, grid_ref):
    _, _, rows, levels, _ = out_ref.shape
    tokens = grid_ref.shape[1]
    step = levels * HALF
    width = out_ref.shape[4] // WLON
    side = width - LANES
    for i, ref in enumerate((o0, o1, o2, o3)):
        packed = ref[...].astype(jnp.float32)
        for part in range(3):
            grid_ref[part] = packed[part * tokens : (part + 1) * tokens]
        micro = place_ref[0] ^ i
        for column in range(WLON):
            half, inside = divmod(column, HALF)
            at = pl.ds(inside, rows * levels, stride=HALF)
            rest = grid_ref[1, at, :][:, half * side : (half + 1) * side]
            piece = jnp.concatenate([grid_ref[2 * half, at, :], rest], 1).reshape(rows, levels, width)
            out_ref[0, micro, :, :, column * width : (column + 1) * width] = piece.astype(jnp.bfloat16)


def finish(place, pieces, shape):
    tokens = pieces[0].shape[0] // 3
    vmem = pl.BlockSpec(memory_space=pltpu.VMEM)
    return pl.pallas_call(
        finish_kernel,
        out_shape=jax.ShapeDtypeStruct(shape, jnp.bfloat16),
        in_specs=[pl.BlockSpec(memory_space=pltpu.SMEM)] + [vmem] * len(pieces),
        out_specs=vmem,
        scratch_shapes=[pltpu.VMEM((3, tokens, LANES), jnp.float32)],
        compiler_params=pltpu.CompilerParams(vmem_limit_bytes=VMEM_LIMIT),
        name="finish",
    )(place, *[in_vmem(x) for x in pieces])


def on_device(fields, land_mask, land_vector, w_qkv, w_proj, w_up, w_down):
    micro_count, levels, rows, flat_width = fields.shape
    width = land_vector.shape[0]
    tile_count, section_count = lax.axis_size("tile"), lax.axis_size("section")
    section = lax.axis_index("section")
    tile_index = lax.axis_index("tile")
    place = jnp.stack([section % STAGE, section // STAGE, tile_index % 2, 1 - tile_index % 2]).astype(jnp.int32)
    axes = ("tile", "section")

    def exchange(value, bit):
        return lax.ppermute(value, "section", [(s, s ^ bit) for s in range(section_count)])

    def forward(value):
        return lax.ppermute(value, "section", [(s, s + STAGE) for s in range(STAGE)])

    def swap(odd_value, even_value, first):
        received = []
        for value, phase in ((odd_value, 1), (even_value, 0)):
            pairs = []
            for t in range(phase, tile_count, 2):
                for s in range(first, first + STAGE):
                    here, there = t * section_count + s, (t + 1) % tile_count * section_count + s
                    pairs += [(here, there), (there, here)]
            received.append(lax.ppermute(value, axes, pairs))
        return received

    tokens = rows * levels * HALF
    tile_shape, half_shape = (3 * tokens, LANES), (2 * tokens, LANES)
    bias = jnp.asarray(window_bias(levels, rows))
    sizes = (tokens, width, bias.shape)

    pack = pack_weights(w_qkv, w_proj, w_up, w_down.transpose(0, 2, 1))
    near, far = exchange(pack, 1), exchange(pack, 2)
    tile = embed(place, fields, land_mask, land_vector.reshape(1, width))
    halo = swap(tile, tile, 0)
    far, halo = lax.optimization_barrier((far, halo))
    weights = (pack, near, far, exchange(far, 1))

    def part(mode, name, blocks, tiles):
        shapes = (tile_shape,) * len(blocks) + (() if mode == "odd" else (half_shape,) * 2)
        kernel = functools.partial(part_kernel, mode, blocks, len(tiles))
        return run_part(kernel, name, place, (*tiles, *weights, bias), shapes, len(blocks), *sizes)

    y0, y1, y2, o, e = part("wide even", "blocks_0_2", (0, 1, 2), (tile, *halo))
    (y3,) = part("odd", "block_3", (3,), (y2, *swap(o, e, 0)))
    y4, o, e = part("even", "block_4", (0,), (forward(y3),))
    y5, y6, o, e = part("odd even", "blocks_5_6", (1, 2), (y4, *swap(o, e, STAGE)))
    operands = (y6, *swap(o, e, STAGE), *weights, bias, y0, y1, y2, y3, y4, y5, y6)
    outs = run_part(last_kernel, "block_7", place, operands, (tile_shape,) * STAGE, 1, *sizes)

    pieces = [outs[0]] + [exchange(outs[i], i) for i in range(1, STAGE)]
    return finish(place, pieces, (1, micro_count, rows, levels, flat_width)).transpose(0, 1, 3, 2, 4)


def solution(mesh):
    in_specs = (
        P(None, None, None, "tile"),
        P(None, "tile"),
        P(),
        P("section", None, None),
        P("section", None, None),
        P("section", None, None),
        P("section", None, None),
    )
    out_specs = P("section", None, None, None, "tile")
    return jax.shard_map(on_device, mesh=mesh, in_specs=in_specs, out_specs=out_specs, check_vma=False)
```

```python
import functools

import jax
import jax.numpy as jnp
import numpy as np
from jax import lax
from jax.experimental import pallas as pl
from jax.experimental.pallas import tpu as pltpu
from jax.sharding import PartitionSpec as P

HEADS = 6
WZ = 2
WLAT = 6
WLON = 12
HALF = WLON // 2
STAGE = 4
LOG2E = 1.4426950408889634
LANES = 128
VMEM_LIMIT = 36 * 2**20


def in_vmem(value):
    return pltpu.with_memory_space_constraint(value, pltpu.VMEM)


def normalize(values):
    center = values - jnp.mean(values, axis=-1, keepdims=True)
    spread = jnp.mean(center * center, axis=-1, keepdims=True)
    return center * lax.rsqrt(spread + 1e-05)


def window_bias(levels, rows):
    lat_blocks = rows // WLAT
    index = np.arange(WLAT * levels * HALF)
    row, level = index // (levels * HALF), index // HALF % levels
    row = row[None] + WLAT * np.arange(lat_blocks)[:, None]

    def label(place, length, window):
        return np.where(place < length - window, 0, np.where(place < length - window // 2, 1, 2))

    labels = label(level, levels, WZ)[None] * 3 + label(row, rows, WLAT)
    keys = np.concatenate([labels, labels], 1)
    return np.where(labels[:, :, None] == keys[:, None, :], 0.0, -1e30).astype(np.float32)


def pack_tile(west, east):
    return jnp.concatenate(
        [west[:, :LANES], jnp.concatenate([west[:, LANES:], east[:, LANES:]], 1), east[:, :LANES]], 0
    )


def unpack_tile(packed, tokens):
    side = packed[tokens : 2 * tokens]
    middle = LANES // 2
    west = jnp.concatenate([packed[:tokens], side[:, :middle]], 1)
    return west, jnp.concatenate([packed[2 * tokens :], side[:, middle:]], 1)


def embed_kernel(micro_ref, fields_ref, mask_ref, vector_ref, tile_ref, grid_ref):
    _, levels, rows, _ = fields_ref.shape
    width = vector_ref.shape[1]
    mask = mask_ref[...].astype(jnp.float32)
    vector = vector_ref[...]
    step = levels * HALF
    for level in range(levels):
        for column in range(WLON):
            piece = fields_ref[0, level, :, column * width : (column + 1) * width].astype(jnp.float32)
            piece = piece + mask[:, column : column + 1] * vector
            half, inside = divmod(column, HALF)
            at = pl.ds(level * HALF + inside, rows, stride=step)
            grid_ref[2 * half, at, :] = piece[:, :LANES]
            grid_ref[2 * half + 1, at, :] = jnp.concatenate([piece[:, LANES:]] * 2, 1)
    tokens, side = rows * step, width - LANES
    tile_ref[:tokens] = grid_ref[0].astype(jnp.bfloat16)
    tile_ref[2 * tokens :] = grid_ref[2].astype(jnp.bfloat16)
    lane = lax.broadcasted_iota(jnp.int32, (1, LANES), 1)
    tile_ref[tokens : 2 * tokens] = jnp.where(lane < side, grid_ref[1], grid_ref[3]).astype(jnp.bfloat16)


def embed(micro, fields, land_mask, land_vector):
    _, levels, rows, flat = fields.shape
    tokens = rows * levels * HALF
    whole = lambda a: pl.BlockSpec(a.shape, lambda i, m: (0,) * a.ndim)
    return pl.pallas_call(
        embed_kernel,
        out_shape=pltpu.VMEM((3 * tokens, LANES), jnp.bfloat16),
        grid_spec=pltpu.PrefetchScalarGridSpec(
            num_scalar_prefetch=1,
            grid=(1,),
            in_specs=[pl.BlockSpec((1, levels, rows, flat), lambda i, m: (m[0], 0, 0, 0)),
                      whole(land_mask), whole(land_vector)],
            out_specs=pl.BlockSpec((3 * tokens, LANES), lambda i, m: (0, 0)),
            scratch_shapes=[pltpu.VMEM((4, tokens, LANES), jnp.float32)],
        ),
        compiler_params=pltpu.CompilerParams(vmem_limit_bytes=VMEM_LIMIT),
        name="embed",
    )(micro, fields, land_mask, land_vector)


def pack_kernel(wqkv_ref, wproj_ref, wup_ref, wdown_ref, pack_ref):
    width = wproj_ref.shape[1]
    side = 256 - width
    for i in range(3):
        pack_ref[:, 256 * i : 256 * i + 256] = jnp.concatenate(
            [wqkv_ref[0, :, i * width : (i + 1) * width], wproj_ref[0, :, i * side : (i + 1) * side]], 1
        )
    hidden = wup_ref.shape[2]
    pack_ref[:, 768 : 768 + hidden] = wup_ref[0]
    pack_ref[:, 768 + hidden :] = wdown_ref[0]


def pack_weights(*weights):
    vmem = pl.BlockSpec(memory_space=pltpu.VMEM)
    width = weights[0].shape[1]
    return pl.pallas_call(
        pack_kernel,
        out_shape=pltpu.VMEM((width, 2304), jnp.bfloat16),
        in_specs=[vmem] * len(weights),
        out_specs=vmem,
        compiler_params=pltpu.CompilerParams(vmem_limit_bytes=VMEM_LIMIT),
        name="pack_weights",
    )(*[pltpu.with_memory_space_constraint(w, pltpu.HBM) for w in weights])


def compute_blocks(mode, flags, tile_refs, bias_ref, w_ref, wproj_ref, store, scratch):
    xa, xb, q_ref, k_ref, v_ref, low_ref, high_ref = scratch
    f32, bf16 = jnp.float32, jnp.bfloat16
    halves, tokens, width = xa.shape
    head_size = width // HEADS
    windows, piece, _ = bias_ref.shape
    move = piece // 2
    hidden = (w_ref.shape[2] - 768) // 2
    channel_head = lax.broadcasted_iota(jnp.int32, (1, width), 1) // head_size
    scale = head_size ** (-0.5) * LOG2E
    ones = jnp.ones((2 * piece, 256 - width), f32)

    def load_tiles():
        into = xb if mode.startswith("odd") else xa
        for i, ref in enumerate(tile_refs):
            if ref.shape[0] == 3 * tokens:
                base = 4 * flags[i - 1] if i else 2
                for j, part in enumerate(unpack_tile(ref[...].astype(f32), tokens)):
                    into[base + j] = part.astype(bf16)
            else:
                east = flags[i - 1]
                main, side = ref[:tokens].astype(f32), ref[tokens:].astype(f32)
                last = jnp.where(east == 1, side[:, : LANES // 2], side[:, LANES // 2 :])
                into[1 + 3 * east] = jnp.concatenate([main, last], 1).astype(bf16)

    def select_heads(parts, first, lanes):
        total = parts[0]
        for n in range(1, len(parts)):
            total = jnp.where(channel_head[:, first : first + lanes] == first // head_size + n, parts[n], total)
        return total

    def rows_of(w):
        return pl.ds(w * piece if isinstance(w, int) else pl.multiple_of(w * piece, 8), piece)

    def window_attention(h, i, w, shifted, exact):
        q = q_ref[h, rows_of(w), :]
        qm = jnp.concatenate([jnp.where(channel_head == n, q, 0.0) for n in range(HEADS)], 0).astype(bf16)
        s = lax.dot_general(qm, k_ref[i, w], (((1,), (1,)), ((), ())), preferred_element_type=f32)
        if shifted:
            s = (s.reshape(HEADS, piece, 2 * piece) + bias_ref[w][None]).reshape(HEADS * piece, 2 * piece)
        if exact:
            s = s - jnp.max(s, axis=-1, keepdims=True)
        o = jnp.dot(jnp.exp2(s).astype(bf16), v_ref[i, w], preferred_element_type=f32)
        heads = [o[n * piece : (n + 1) * piece] for n in range(HEADS)]
        full = LANES // head_size
        tops = [select_heads([x[:, :LANES] for x in heads[:full]], 0, LANES),
                select_heads([x[:, LANES:width] for x in heads[full:]], LANES, width - LANES)]
        side = 256 - width
        ends = [x[:, LANES:] for x in heads]
        odd = channel_head[:, :LANES] % 2 == 1
        couples = [jnp.where(odd, ends[n + 1], ends[n]) for n in range(0, HEADS, 2)]
        lane = lax.broadcasted_iota(jnp.int32, (1, LANES), 1)
        sums = [jnp.where(lane < side, pltpu.roll(couples[0], side, 1), couples[1]),
                pltpu.roll(couples[2], side, 1)[:, :side]]
        if not exact:
            low_ref[...] = jnp.minimum(low_ref[...], jnp.min(sums[0].reshape(-1, 8, LANES), axis=0))
            high_ref[...] = jnp.maximum(high_ref[...], jnp.max(sums[0].reshape(-1, 8, LANES), axis=0))
            rest = slice(0, width - LANES)
            low_ref[:, rest] = jnp.minimum(low_ref[:, rest], jnp.min(sums[1].reshape(-1, 8, width - LANES), axis=0))
            high_ref[:, rest] = jnp.maximum(high_ref[:, rest], jnp.max(sums[1].reshape(-1, 8, width - LANES), axis=0))
        return jnp.concatenate([top / total for top, total in zip(tops, sums)], 1)

    def block(b, shifted, exact, together, first_pair, pairs, first_q, count):
        source, target = (xb, xa) if shifted else (xa, xb)

        def load(h):
            x = source[h].astype(f32)
            return pltpu.roll(x, tokens - move, 0) if shifted else x

        def pair(i, carry):
            kv = []
            for j in range(2):
                h = first_pair + 2 * i + j
                qkv = jnp.dot(normalize(load(h)).astype(bf16), w_ref[b, :, :768], preferred_element_type=f32)
                q_ref[h] = qkv[:, :width] * scale
                kv.append((qkv[:, 256 : 256 + width], qkv[:, 512 : 512 + width]))
            for w in range(windows):
                at = slice(w * piece, (w + 1) * piece)
                k_ref[i, w] = jnp.concatenate([kv[0][0][at], kv[1][0][at]], 0).astype(bf16)
                v = jnp.concatenate([kv[0][1][at], kv[1][1][at]], 0)
                v_ref[i, w] = jnp.concatenate([v, ones], 1).astype(bf16)
            return carry

        def attend(c, carry):
            own = [first_q + together * c + j for j in range(together)]
            x = jnp.concatenate([load(h) for h in own], 0)
            if exact:

                def one_window(w, carry):
                    for h in own:
                        q_ref[h, rows_of(w), :] = window_attention(h, (h - first_pair) // 2, w, shifted, exact)
                    return carry

                lax.fori_loop(0, windows, one_window, 0)
                a = jnp.concatenate([q_ref[h] for h in own], 0).astype(bf16)
            else:
                parts = [
                    window_attention(h, (h - first_pair) // 2, w, shifted, exact) for h in own for w in range(windows)
                ]
                a = jnp.concatenate(parts, 0).astype(bf16)
            residual = x + jnp.dot(a, wproj_ref[b], preferred_element_type=f32)
            n2 = normalize(residual).astype(bf16)
            u = jnp.dot(n2, w_ref[b, :, 768 : 768 + hidden], preferred_element_type=f32)
            g = (0.5 * u * (1.0 + lax.erf(u * (0.5**0.5)))).astype(bf16)
            y = residual + lax.dot_general(
                g, w_ref[b, :, 768 + hidden :], (((1,), (1,)), ((), ())), preferred_element_type=f32
            )
            for j, h in enumerate(own):
                part = y[j * tokens : (j + 1) * tokens]
                if shifted:
                    part = pltpu.roll(part, move, 0)
                target[h] = part.astype(bf16)
            return carry

        lax.fori_loop(0, pairs, pair, 0)
        lax.fori_loop(0, count // together, attend, 0)
        store(b, pack_tile(target[2].astype(f32), target[3].astype(f32)).astype(bf16))

    def compute(exact, together):
        load_tiles()

        def odd(b):
            block(b, True, exact, together, 1, 2, 2, 2)

        def even(b):
            block(b, False, exact, together, 2, 1, 2, 2)

        def wide_even(n, carry):
            block(2 * n, False, exact, together, 2 * n, 3 - 2 * n, 1 + n, 4 - 2 * n)
            pl.when(n == 0)(lambda: odd(1))
            return carry

        if mode == "wide even":
            lax.fori_loop(0, 2, wide_even, 0)
        elif mode == "even":
            even(0)
        else:
            odd(0)
            if mode == "odd even":
                even(1)

    low_ref[...] = jnp.ones_like(low_ref)
    high_ref[...] = jnp.ones_like(high_ref)
    compute(False, 2)
    safe = (jnp.min(low_ref[...]) >= 2.0**-90) & (jnp.max(high_ref[...]) <= 2.0**90)

    @pl.when(jnp.logical_not(safe))
    def _():
        compute(True, 1)


def unpack_projection(ref, width):
    return jnp.concatenate([ref[:, 256 * j + width : 256 * j + 256] for j in range(3)], 1)


def gather_weights(place, refs, blocks, w_ref, wproj_ref):
    for i, ref in enumerate(refs):
        b = place ^ i

        @pl.when((b >= blocks[0]) & (b <= blocks[-1]))
        def _(ref=ref, slot=b - blocks[0]):
            w_ref[slot] = ref[...]
            wproj_ref[slot] = unpack_projection(ref, wproj_ref.shape[1])


def store_halves(place_ref, tile_ref, o_ref, e_ref):
    tokens = tile_ref.shape[0] // 3
    for ref, flag in ((o_ref, place_ref[2]), (e_ref, place_ref[3])):
        ref[:tokens] = jnp.where(flag == 1, tile_ref[2 * tokens :].astype(jnp.float32),
                                 tile_ref[:tokens].astype(jnp.float32)).astype(jnp.bfloat16)
        ref[tokens:] = tile_ref[tokens : 2 * tokens]


def part_kernel(mode, blocks, tile_count, place_ref, *refs):
    tiles, refs = refs[:tile_count], refs[tile_count:]
    weights, bias_ref, refs = refs[:STAGE], refs[STAGE], refs[STAGE + 1 :]
    outs, refs = refs[: len(blocks)], refs[len(blocks) :]
    halves = ()
    if mode != "odd":
        halves, refs = refs[:2], refs[2:]
    w_ref, wproj_ref, stage_ref, *scratch = refs
    gather_weights(place_ref[0], weights, blocks, w_ref, wproj_ref)

    def store(slot, packed):
        stage_ref[slot] = packed

    flags = (place_ref[2], place_ref[3])
    compute_blocks(mode, flags, tiles, bias_ref, w_ref, wproj_ref, store, scratch)
    for i, ref in enumerate(outs):
        ref[...] = stage_ref[i]
    if halves:
        store_halves(place_ref, outs[-1], *halves)


def last_kernel(place_ref, *refs):
    tiles, refs = refs[:3], refs[3:]
    weights, bias_ref, refs = refs[:STAGE], refs[STAGE], refs[STAGE + 1 :]
    early, late, refs = refs[:STAGE], refs[STAGE : 2 * STAGE - 1], refs[2 * STAGE - 1 :]
    outs, refs = refs[:STAGE], refs[STAGE:]
    w_ref, wproj_ref, stage_ref, *scratch = refs
    place = place_ref[0]

    def route(sources):
        for i, ref in enumerate(outs):
            for b, source in enumerate(sources):

                @pl.when((place ^ i) == b)
                def _(ref=ref, source=source):
                    ref[...] = source[...]

    @pl.when(place_ref[1] == 1)
    def _():
        gather_weights(place, weights, (STAGE - 1,), w_ref, wproj_ref)

        def store(slot, packed):
            stage_ref[slot] = packed

        flags = (place_ref[2], place_ref[3])
        compute_blocks("odd", flags, tiles, bias_ref, w_ref, wproj_ref, store, scratch)
        route((*late, stage_ref.at[0]))

    @pl.when(place_ref[1] == 0)
    def _():
        route(early)


def run_part(kernel, name, place, operands, outs, blocks, tokens, width, bias_shape):
    halves = 6
    windows, piece, _ = bias_shape
    vmem = pl.BlockSpec(memory_space=pltpu.VMEM)
    bf16, f32 = jnp.bfloat16, jnp.float32
    return pl.pallas_call(
        kernel,
        out_shape=tuple(pltpu.VMEM(shape, bf16) for shape in outs),
        in_specs=[pl.BlockSpec(memory_space=pltpu.SMEM)] + [vmem] * len(operands),
        out_specs=(vmem,) * len(outs),
        scratch_shapes=[
            pltpu.VMEM((blocks, width, 2304), bf16),
            pltpu.VMEM((blocks, width, width), bf16),
            pltpu.VMEM((blocks, 3 * tokens, LANES), bf16),
            pltpu.VMEM((halves, tokens, width), bf16),
            pltpu.VMEM((halves, tokens, width), bf16),
            pltpu.VMEM((halves, tokens, width), f32),
            pltpu.VMEM((halves // 2, windows, 2 * piece, width), bf16),
            pltpu.VMEM((halves // 2, windows, 2 * piece, 256), bf16),
            pltpu.VMEM((8, LANES), f32),
            pltpu.VMEM((8, LANES), f32),
        ],
        compiler_params=pltpu.CompilerParams(vmem_limit_bytes=VMEM_LIMIT),
        name=name,
    )(place, *[in_vmem(x) for x in operands])


def finish_kernel(count, place_ref, *refs):
    out_ref, grid_ref = refs[-2:]
    _, _, rows, levels, _ = out_ref.shape
    tokens = grid_ref.shape[1]
    width = out_ref.shape[4] // WLON
    side = width - LANES
    for i, ref in enumerate(refs[:count]):

        @pl.when(pl.program_id(0) == i)
        def _(ref=ref):
            packed = ref[...].astype(jnp.float32)
            for part in range(3):
                grid_ref[part] = packed[part * tokens : (part + 1) * tokens]
            for column in range(WLON):
                half, inside = divmod(column, HALF)
                at = pl.ds(inside, rows * levels, stride=HALF)
                rest = grid_ref[1, at, :][:, half * side : (half + 1) * side]
                piece = jnp.concatenate([grid_ref[2 * half, at, :], rest], 1).reshape(rows, levels, width)
                out_ref[0, 0, :, :, column * width : (column + 1) * width] = piece.astype(jnp.bfloat16)


def finish(place, pieces, first, shape, buffer=None):
    tokens = pieces[0].shape[0] // 3
    count = len(pieces)
    vmem = pl.BlockSpec(memory_space=pltpu.VMEM)
    more = [] if buffer is None else [buffer]
    return pl.pallas_call(
        functools.partial(finish_kernel, count),
        out_shape=jax.ShapeDtypeStruct(shape, jnp.bfloat16),
        grid_spec=pltpu.PrefetchScalarGridSpec(
            num_scalar_prefetch=1,
            grid=(count,),
            in_specs=[vmem] * count + [pl.BlockSpec(memory_space=pl.ANY)] * len(more),
            out_specs=pl.BlockSpec((1, 1) + shape[2:], lambda i, m: (0, m[0] ^ (first + i), 0, 0, 0)),
            scratch_shapes=[pltpu.VMEM((3, tokens, LANES), jnp.float32)],
        ),
        input_output_aliases={1 + count: 0} if more else {},
        compiler_params=pltpu.CompilerParams(vmem_limit_bytes=VMEM_LIMIT),
        name="finish",
    )(place, *[in_vmem(x) for x in pieces], *more)


def on_device(fields, land_mask, land_vector, w_qkv, w_proj, w_up, w_down):
    micro_count, levels, rows, flat_width = fields.shape
    width = land_vector.shape[0]
    tile_count, section_count = lax.axis_size("tile"), lax.axis_size("section")
    section = lax.axis_index("section")
    tile_index = lax.axis_index("tile")
    place = jnp.stack([section % STAGE, section // STAGE, tile_index % 2, 1 - tile_index % 2]).astype(jnp.int32)
    axes = ("tile", "section")

    def exchange(value, bit):
        return lax.ppermute(value, "section", [(s, s ^ bit) for s in range(section_count)])

    def forward(value):
        return lax.ppermute(value, "section", [(s, s + STAGE) for s in range(STAGE)])

    def swap(odd_value, even_value, first):
        received = []
        for value, phase in ((odd_value, 1), (even_value, 0)):
            pairs = []
            for t in range(phase, tile_count, 2):
                for s in range(first, first + STAGE):
                    here, there = t * section_count + s, (t + 1) % tile_count * section_count + s
                    pairs += [(here, there), (there, here)]
            received.append(lax.ppermute(value, axes, pairs))
        return received

    tokens = rows * levels * HALF
    tile_shape, half_shape = (3 * tokens, LANES), (2 * tokens, LANES)
    bias = jnp.asarray(window_bias(levels, rows))
    sizes = (tokens, width, bias.shape)

    pack = pack_weights(w_qkv, w_proj, w_up, w_down.transpose(0, 2, 1))
    near, far = exchange(pack, 1), exchange(pack, 2)
    tile = embed(place, fields, land_mask, land_vector.reshape(1, width))
    halo = swap(tile, tile, 0)
    far, halo = lax.optimization_barrier((far, halo))
    weights = (pack, near, far, exchange(far, 1))

    def part(mode, name, blocks, tiles):
        shapes = (tile_shape,) * len(blocks) + (() if mode == "odd" else (half_shape,) * 2)
        kernel = functools.partial(part_kernel, mode, blocks, len(tiles))
        return run_part(kernel, name, place, (*tiles, *weights, bias), shapes, len(blocks), *sizes)

    y0, y1, y2, o, e = part("wide even", "blocks_0_2", (0, 1, 2), (tile, *halo))
    (y3,) = part("odd", "block_3", (3,), (y2, *swap(o, e, 0)))
    y4, o, e = part("even", "block_4", (0,), (forward(y3),))
    y5, y6, o, e = part("odd even", "blocks_5_6", (1, 2), (y4, *swap(o, e, STAGE)))
    operands = (y6, *swap(o, e, STAGE), *weights, bias, y0, y1, y2, y3, y4, y5, y6)
    outs = run_part(last_kernel, "block_7", place, operands, (tile_shape,) * STAGE, 1, *sizes)

    across = [exchange(outs[i], i) for i in (2, 3)]
    mate = exchange(outs[1], 1)
    shape = (1, micro_count, rows, levels, flat_width)
    result = finish(place, [outs[0], mate], 0, shape)
    return finish(place, across, 2, shape, result).transpose(0, 1, 3, 2, 4)


def solution(mesh):
    in_specs = (
        P(None, None, None, "tile"),
        P(None, "tile"),
        P(),
        P("section", None, None),
        P("section", None, None),
        P("section", None, None),
        P("section", None, None),
    )
    out_specs = P("section", None, None, None, "tile")
    return jax.shard_map(on_device, mesh=mesh, in_specs=in_specs, out_specs=out_specs, check_vma=False)
```

```python
import functools

import jax
import jax.numpy as jnp
import numpy as np
from jax import lax
from jax.experimental import pallas as pl
from jax.experimental.pallas import tpu as pltpu
from jax.sharding import PartitionSpec as P

HEADS = 6
WZ = 2
WLAT = 6
WLON = 12
HALF = WLON // 2
STAGE = 4
LOG2E = 1.4426950408889634
LANES = 128
VMEM_LIMIT = 36 * 2**20


def in_vmem(value):
    return pltpu.with_memory_space_constraint(value, pltpu.VMEM)


def normalize(values):
    center = values - jnp.mean(values, axis=-1, keepdims=True)
    spread = jnp.mean(center * center, axis=-1, keepdims=True)
    return center * lax.rsqrt(spread + 1e-05)


def window_bias(levels, rows):
    lat_blocks = rows // WLAT
    index = np.arange(WLAT * levels * HALF)
    row, level = index // (levels * HALF), index // HALF % levels
    row = row[None] + WLAT * np.arange(lat_blocks)[:, None]

    def label(place, length, window):
        return np.where(place < length - window, 0, np.where(place < length - window // 2, 1, 2))

    labels = label(level, levels, WZ)[None] * 3 + label(row, rows, WLAT)
    keys = np.concatenate([labels, labels], 1)
    return np.where(labels[:, :, None] == keys[:, None, :], 0.0, -1e30).astype(np.float32)


def pack_tile(west, east):
    return jnp.concatenate(
        [west[:, :LANES], jnp.concatenate([west[:, LANES:], east[:, LANES:]], 1), east[:, :LANES]], 0
    )


def unpack_tile(packed, tokens):
    side = packed[tokens : 2 * tokens]
    middle = LANES // 2
    west = jnp.concatenate([packed[:tokens], side[:, :middle]], 1)
    return west, jnp.concatenate([packed[2 * tokens :], side[:, middle:]], 1)


def embed_kernel(micro_ref, fields_ref, mask_ref, vector_ref, tile_ref, grid_ref):
    _, levels, rows, _ = fields_ref.shape
    width = vector_ref.shape[1]
    mask = mask_ref[...].astype(jnp.float32)
    vector = vector_ref[...]
    step = levels * HALF
    for level in range(levels):
        for column in range(WLON):
            piece = fields_ref[0, level, :, column * width : (column + 1) * width].astype(jnp.float32)
            piece = piece + mask[:, column : column + 1] * vector
            half, inside = divmod(column, HALF)
            at = pl.ds(level * HALF + inside, rows, stride=step)
            grid_ref[2 * half, at, :] = piece[:, :LANES]
            grid_ref[2 * half + 1, at, :] = jnp.concatenate([piece[:, LANES:]] * 2, 1)
    tokens, side = rows * step, width - LANES
    tile_ref[:tokens] = grid_ref[0].astype(jnp.bfloat16)
    tile_ref[2 * tokens :] = grid_ref[2].astype(jnp.bfloat16)
    lane = lax.broadcasted_iota(jnp.int32, (1, LANES), 1)
    tile_ref[tokens : 2 * tokens] = jnp.where(lane < side, grid_ref[1], grid_ref[3]).astype(jnp.bfloat16)


def embed(micro, fields, land_mask, land_vector):
    _, levels, rows, flat = fields.shape
    tokens = rows * levels * HALF
    whole = lambda a: pl.BlockSpec(a.shape, lambda i, m: (0,) * a.ndim)
    return pl.pallas_call(
        embed_kernel,
        out_shape=pltpu.VMEM((3 * tokens, LANES), jnp.bfloat16),
        grid_spec=pltpu.PrefetchScalarGridSpec(
            num_scalar_prefetch=1,
            grid=(1,),
            in_specs=[pl.BlockSpec((1, levels, rows, flat), lambda i, m: (m[0], 0, 0, 0)),
                      whole(land_mask), whole(land_vector)],
            out_specs=pl.BlockSpec((3 * tokens, LANES), lambda i, m: (0, 0)),
            scratch_shapes=[pltpu.VMEM((4, tokens, LANES), jnp.float32)],
        ),
        compiler_params=pltpu.CompilerParams(vmem_limit_bytes=VMEM_LIMIT),
        name="embed",
    )(micro, fields, land_mask, land_vector)


def pack_kernel(wqkv_ref, wproj_ref, wup_ref, wdown_ref, pack_ref):
    width = wproj_ref.shape[1]
    side = 256 - width
    for i in range(3):
        pack_ref[:, 256 * i : 256 * i + 256] = jnp.concatenate(
            [wqkv_ref[0, :, i * width : (i + 1) * width], wproj_ref[0, :, i * side : (i + 1) * side]], 1
        )
    hidden = wup_ref.shape[2]
    pack_ref[:, 768 : 768 + hidden] = wup_ref[0]
    pack_ref[:, 768 + hidden :] = wdown_ref[0]


def pack_weights(*weights):
    vmem = pl.BlockSpec(memory_space=pltpu.VMEM)
    width = weights[0].shape[1]
    return pl.pallas_call(
        pack_kernel,
        out_shape=pltpu.VMEM((width, 2304), jnp.bfloat16),
        in_specs=[vmem] * len(weights),
        out_specs=vmem,
        compiler_params=pltpu.CompilerParams(vmem_limit_bytes=VMEM_LIMIT),
        name="pack_weights",
    )(*[pltpu.with_memory_space_constraint(w, pltpu.HBM) for w in weights])


def compute_blocks(mode, flags, tile_refs, bias_ref, w_ref, wproj_ref, store, scratch):
    xa, xb, q_ref, k_ref, v_ref, low_ref, high_ref = scratch
    f32, bf16 = jnp.float32, jnp.bfloat16
    halves, tokens, width = xa.shape
    head_size = width // HEADS
    windows, piece, _ = bias_ref.shape
    move = piece // 2
    hidden = (w_ref.shape[2] - 768) // 2
    channel_head = lax.broadcasted_iota(jnp.int32, (1, width), 1) // head_size
    scale = head_size ** (-0.5) * LOG2E
    ones = jnp.ones((2 * piece, 256 - width), f32)

    def load_tiles():
        into = xb if mode.startswith("odd") else xa
        for i, ref in enumerate(tile_refs):
            if ref.shape[0] == 3 * tokens:
                base = 4 * flags[i - 1] if i else 2
                for j, part in enumerate(unpack_tile(ref[...].astype(f32), tokens)):
                    into[base + j] = part.astype(bf16)
            else:
                east = flags[i - 1]
                main, side = ref[:tokens].astype(f32), ref[tokens:].astype(f32)
                last = jnp.where(east == 1, side[:, : LANES // 2], side[:, LANES // 2 :])
                into[1 + 3 * east] = jnp.concatenate([main, last], 1).astype(bf16)

    def select_heads(parts, first, lanes):
        total = parts[0]
        for n in range(1, len(parts)):
            total = jnp.where(channel_head[:, first : first + lanes] == first // head_size + n, parts[n], total)
        return total

    def rows_of(w):
        return pl.ds(w * piece if isinstance(w, int) else pl.multiple_of(w * piece, 8), piece)

    def window_attention(h, i, w, shifted, exact):
        q = q_ref[h, rows_of(w), :]
        qm = jnp.concatenate([jnp.where(channel_head == n, q, 0.0) for n in range(HEADS)], 0).astype(bf16)
        s = lax.dot_general(qm, k_ref[i, w], (((1,), (1,)), ((), ())), preferred_element_type=f32)
        if shifted:
            s = (s.reshape(HEADS, piece, 2 * piece) + bias_ref[w][None]).reshape(HEADS * piece, 2 * piece)
        if exact:
            s = s - jnp.max(s, axis=-1, keepdims=True)
        o = jnp.dot(jnp.exp2(s).astype(bf16), v_ref[i, w], preferred_element_type=f32)
        heads = [o[n * piece : (n + 1) * piece] for n in range(HEADS)]
        full = LANES // head_size
        tops = [select_heads([x[:, :LANES] for x in heads[:full]], 0, LANES),
                select_heads([x[:, LANES:width] for x in heads[full:]], LANES, width - LANES)]
        side = 256 - width
        ends = [x[:, LANES:] for x in heads]
        odd = channel_head[:, :LANES] % 2 == 1
        couples = [jnp.where(odd, ends[n + 1], ends[n]) for n in range(0, HEADS, 2)]
        lane = lax.broadcasted_iota(jnp.int32, (1, LANES), 1)
        sums = [jnp.where(lane < side, pltpu.roll(couples[0], side, 1), couples[1]),
                pltpu.roll(couples[2], side, 1)[:, :side]]
        if not exact:
            low_ref[...] = jnp.minimum(low_ref[...], jnp.min(sums[0].reshape(-1, 8, LANES), axis=0))
            high_ref[...] = jnp.maximum(high_ref[...], jnp.max(sums[0].reshape(-1, 8, LANES), axis=0))
            rest = slice(0, width - LANES)
            low_ref[:, rest] = jnp.minimum(low_ref[:, rest], jnp.min(sums[1].reshape(-1, 8, width - LANES), axis=0))
            high_ref[:, rest] = jnp.maximum(high_ref[:, rest], jnp.max(sums[1].reshape(-1, 8, width - LANES), axis=0))
        return jnp.concatenate([top / total for top, total in zip(tops, sums)], 1)

    def block(b, shifted, exact, together, first_pair, pairs, first_q, count):
        source, target = (xb, xa) if shifted else (xa, xb)

        def load(h):
            x = source[h].astype(f32)
            return pltpu.roll(x, tokens - move, 0) if shifted else x

        def pair(i, carry):
            kv = []
            for j in range(2):
                h = first_pair + 2 * i + j
                qkv = jnp.dot(normalize(load(h)).astype(bf16), w_ref[b, :, :768], preferred_element_type=f32)
                q_ref[h] = qkv[:, :width] * scale
                kv.append((qkv[:, 256 : 256 + width], qkv[:, 512 : 512 + width]))
            for w in range(windows):
                at = slice(w * piece, (w + 1) * piece)
                k_ref[i, w] = jnp.concatenate([kv[0][0][at], kv[1][0][at]], 0).astype(bf16)
                v = jnp.concatenate([kv[0][1][at], kv[1][1][at]], 0)
                v_ref[i, w] = jnp.concatenate([v, ones], 1).astype(bf16)
            return carry

        def attend(c, carry):
            own = [first_q + together * c + j for j in range(together)]
            x = jnp.concatenate([load(h) for h in own], 0)
            if exact:

                def one_window(w, carry):
                    for h in own:
                        q_ref[h, rows_of(w), :] = window_attention(h, (h - first_pair) // 2, w, shifted, exact)
                    return carry

                lax.fori_loop(0, windows, one_window, 0)
                a = jnp.concatenate([q_ref[h] for h in own], 0).astype(bf16)
            else:
                parts = [
                    window_attention(h, (h - first_pair) // 2, w, shifted, exact) for h in own for w in range(windows)
                ]
                a = jnp.concatenate(parts, 0).astype(bf16)
            residual = x + jnp.dot(a, wproj_ref[b], preferred_element_type=f32)
            n2 = normalize(residual).astype(bf16)
            u = jnp.dot(n2, w_ref[b, :, 768 : 768 + hidden], preferred_element_type=f32)
            g = (0.5 * u * (1.0 + lax.erf(u * (0.5**0.5)))).astype(bf16)
            y = residual + lax.dot_general(
                g, w_ref[b, :, 768 + hidden :], (((1,), (1,)), ((), ())), preferred_element_type=f32
            )
            for j, h in enumerate(own):
                part = y[j * tokens : (j + 1) * tokens]
                if shifted:
                    part = pltpu.roll(part, move, 0)
                target[h] = part.astype(bf16)
            return carry

        lax.fori_loop(0, pairs, pair, 0)
        lax.fori_loop(0, count // together, attend, 0)
        store(b, pack_tile(target[2].astype(f32), target[3].astype(f32)).astype(bf16))

    def compute(exact, together):
        load_tiles()

        def odd(b):
            block(b, True, exact, together, 1, 2, 2, 2)

        def even(b):
            block(b, False, exact, together, 2, 1, 2, 2)

        def wide_even(n, carry):
            block(2 * n, False, exact, together, 2 * n, 3 - 2 * n, 1 + n, 4 - 2 * n)
            pl.when(n == 0)(lambda: odd(1))
            return carry

        if mode == "wide even":
            lax.fori_loop(0, 2, wide_even, 0)
        elif mode == "even":
            even(0)
        else:
            odd(0)
            if mode == "odd even":
                even(1)

    low_ref[...] = jnp.ones_like(low_ref)
    high_ref[...] = jnp.ones_like(high_ref)
    compute(False, 2)
    safe = (jnp.min(low_ref[...]) >= 2.0**-90) & (jnp.max(high_ref[...]) <= 2.0**90)

    @pl.when(jnp.logical_not(safe))
    def _():
        compute(True, 1)


def unpack_projection(ref, width):
    return jnp.concatenate([ref[:, 256 * j + width : 256 * j + 256] for j in range(3)], 1)


def gather_weights(place, refs, blocks, w_ref, wproj_ref):
    for i, ref in enumerate(refs):
        b = place ^ i

        @pl.when((b >= blocks[0]) & (b <= blocks[-1]))
        def _(ref=ref, slot=b - blocks[0]):
            w_ref[slot] = ref[...]
            wproj_ref[slot] = unpack_projection(ref, wproj_ref.shape[1])


def store_halves(place_ref, tile_ref, o_ref, e_ref):
    tokens = tile_ref.shape[0] // 3
    for ref, flag in ((o_ref, place_ref[2]), (e_ref, place_ref[3])):
        ref[:tokens] = jnp.where(flag == 1, tile_ref[2 * tokens :].astype(jnp.float32),
                                 tile_ref[:tokens].astype(jnp.float32)).astype(jnp.bfloat16)
        ref[tokens:] = tile_ref[tokens : 2 * tokens]


def part_kernel(mode, blocks, tile_count, place_ref, *refs):
    tiles, refs = refs[:tile_count], refs[tile_count:]
    weights, bias_ref, refs = refs[:STAGE], refs[STAGE], refs[STAGE + 1 :]
    outs, refs = refs[: len(blocks)], refs[len(blocks) :]
    halves = ()
    if mode != "odd":
        halves, refs = refs[:2], refs[2:]
    w_ref, wproj_ref, stage_ref, *scratch = refs
    gather_weights(place_ref[0], weights, blocks, w_ref, wproj_ref)

    def store(slot, packed):
        stage_ref[slot] = packed

    flags = (place_ref[3], place_ref[2])
    compute_blocks(mode, flags, tiles, bias_ref, w_ref, wproj_ref, store, scratch)
    for i, ref in enumerate(outs):
        ref[...] = stage_ref[i]
    if halves:
        store_halves(place_ref, outs[-1], *halves)


def last_kernel(place_ref, *refs):
    tiles, refs = refs[:3], refs[3:]
    weights, bias_ref, refs = refs[:STAGE], refs[STAGE], refs[STAGE + 1 :]
    early, late, refs = refs[:STAGE], refs[STAGE : 2 * STAGE - 1], refs[2 * STAGE - 1 :]
    outs, refs = refs[:STAGE], refs[STAGE:]
    w_ref, wproj_ref, stage_ref, *scratch = refs
    place = place_ref[0]

    def route(sources):
        for i, ref in enumerate(outs):
            for b, source in enumerate(sources):

                @pl.when((place ^ i) == b)
                def _(ref=ref, source=source):
                    ref[...] = source[...]

    @pl.when(place_ref[1] == 1)
    def _():
        gather_weights(place, weights, (STAGE - 1,), w_ref, wproj_ref)

        def store(slot, packed):
            stage_ref[slot] = packed

        flags = (place_ref[3], place_ref[2])
        compute_blocks("odd", flags, tiles, bias_ref, w_ref, wproj_ref, store, scratch)
        route((*late, stage_ref.at[0]))

    @pl.when(place_ref[1] == 0)
    def _():
        route(early)


def run_part(kernel, name, place, operands, outs, blocks, tokens, width, bias_shape):
    halves = 6
    windows, piece, _ = bias_shape
    vmem = pl.BlockSpec(memory_space=pltpu.VMEM)
    bf16, f32 = jnp.bfloat16, jnp.float32
    return pl.pallas_call(
        kernel,
        out_shape=tuple(pltpu.VMEM(shape, bf16) for shape in outs),
        in_specs=[pl.BlockSpec(memory_space=pltpu.SMEM)] + [vmem] * len(operands),
        out_specs=(vmem,) * len(outs),
        scratch_shapes=[
            pltpu.VMEM((blocks, width, 2304), bf16),
            pltpu.VMEM((blocks, width, width), bf16),
            pltpu.VMEM((blocks, 3 * tokens, LANES), bf16),
            pltpu.VMEM((halves, tokens, width), bf16),
            pltpu.VMEM((halves, tokens, width), bf16),
            pltpu.VMEM((halves, tokens, width), f32),
            pltpu.VMEM((halves // 2, windows, 2 * piece, width), bf16),
            pltpu.VMEM((halves // 2, windows, 2 * piece, 256), bf16),
            pltpu.VMEM((8, LANES), f32),
            pltpu.VMEM((8, LANES), f32),
        ],
        compiler_params=pltpu.CompilerParams(vmem_limit_bytes=VMEM_LIMIT),
        name=name,
    )(place, *[in_vmem(x) for x in operands])


def finish_kernel(count, place_ref, *refs):
    out_ref, grid_ref = refs[-2:]
    _, _, rows, levels, _ = out_ref.shape
    tokens = grid_ref.shape[1]
    width = out_ref.shape[4] // WLON
    side = width - LANES
    for i, ref in enumerate(refs[:count]):

        @pl.when(pl.program_id(0) == i)
        def _(ref=ref):
            packed = ref[...].astype(jnp.float32)
            for part in range(3):
                grid_ref[part] = packed[part * tokens : (part + 1) * tokens]
            for column in range(WLON):
                half, inside = divmod(column, HALF)
                at = pl.ds(inside, rows * levels, stride=HALF)
                rest = grid_ref[1, at, :][:, half * side : (half + 1) * side]
                piece = jnp.concatenate([grid_ref[2 * half, at, :], rest], 1).reshape(rows, levels, width)
                out_ref[0, 0, :, :, column * width : (column + 1) * width] = piece.astype(jnp.bfloat16)


def finish(place, pieces, first, step, shape, buffer=None):
    tokens = pieces[0].shape[0] // 3
    count = len(pieces)
    vmem = pl.BlockSpec(memory_space=pltpu.VMEM)
    more = [] if buffer is None else [buffer]
    return pl.pallas_call(
        functools.partial(finish_kernel, count),
        out_shape=jax.ShapeDtypeStruct(shape, jnp.bfloat16),
        grid_spec=pltpu.PrefetchScalarGridSpec(
            num_scalar_prefetch=1,
            grid=(count,),
            in_specs=[vmem] * count + [pl.BlockSpec(memory_space=pl.ANY)] * len(more),
            out_specs=pl.BlockSpec((1, 1) + shape[2:], lambda i, m: (0, m[0] ^ (first + i * step), 0, 0, 0)),
            scratch_shapes=[pltpu.VMEM((3, tokens, LANES), jnp.float32)],
        ),
        input_output_aliases={1 + count: 0} if more else {},
        compiler_params=pltpu.CompilerParams(vmem_limit_bytes=VMEM_LIMIT),
        name="finish",
    )(place, *[in_vmem(x) for x in pieces], *more)


def on_device(fields, land_mask, land_vector, w_qkv, w_proj, w_up, w_down):
    micro_count, levels, rows, flat_width = fields.shape
    width = land_vector.shape[0]
    tile_count, section_count = lax.axis_size("tile"), lax.axis_size("section")
    section = lax.axis_index("section")
    tile_index = lax.axis_index("tile")
    place = jnp.stack([section % STAGE, section // STAGE, tile_index % 2, 1 - tile_index % 2]).astype(jnp.int32)
    axes = ("tile", "section")

    def exchange(value, bit):
        return lax.ppermute(value, "section", [(s, s ^ bit) for s in range(section_count)])

    def forward(value):
        return lax.ppermute(value, "section", [(s, s + STAGE) for s in range(STAGE)])

    def swap(odd_value, even_value, first, fields_first=False):
        received = {}
        for value, phase in ((odd_value, 1), (even_value, 0))[:: 1 if fields_first else -1]:
            pairs = []
            for t in range(phase, tile_count, 2):
                for s in range(first, first + STAGE):
                    here, there = t * section_count + s, (t + 1) % tile_count * section_count + s
                    pairs += [(here, there), (there, here)]
            received[phase] = lax.ppermute(value, axes, pairs)
        return received[0], received[1]

    tokens = rows * levels * HALF
    tile_shape, half_shape = (3 * tokens, LANES), (2 * tokens, LANES)
    bias = jnp.asarray(window_bias(levels, rows))
    sizes = (tokens, width, bias.shape)

    pack = pack_weights(w_qkv, w_proj, w_up, w_down.transpose(0, 2, 1))
    near, far = exchange(pack, 1), exchange(pack, 2)
    tile = embed(place, fields, land_mask, land_vector.reshape(1, width))
    halo = swap(tile, tile, 0, True)
    far, halo = lax.optimization_barrier((far, halo))
    weights = (pack, near, far, exchange(far, 1))

    def part(mode, name, blocks, tiles):
        shapes = (tile_shape,) * len(blocks) + (() if mode == "odd" else (half_shape,) * 2)
        kernel = functools.partial(part_kernel, mode, blocks, len(tiles))
        return run_part(kernel, name, place, (*tiles, *weights, bias), shapes, len(blocks), *sizes)

    y0, y1, y2, o, e = part("wide even", "blocks_0_2", (0, 1, 2), (tile, *halo))
    (y3,) = part("odd", "block_3", (3,), (y2, *swap(o, e, 0)))
    y4, o, e = part("even", "block_4", (0,), (forward(y3),))
    y5, y6, o, e = part("odd even", "blocks_5_6", (1, 2), (y4, *swap(o, e, STAGE)))
    operands = (y6, *swap(o, e, STAGE), *weights, bias, y0, y1, y2, y3, y4, y5, y6)
    outs = run_part(last_kernel, "block_7", place, operands, (tile_shape,) * STAGE, 1, *sizes)

    diagonal, far_piece, mate = (exchange(outs[i], i) for i in (3, 2, 1))
    shape = (1, micro_count, rows, levels, flat_width)
    result = finish(place, [outs[0], diagonal], 0, 3, shape)
    return finish(place, [mate, far_piece], 1, 1, shape, result).transpose(0, 1, 3, 2, 4)


def solution(mesh):
    in_specs = (
        P(None, None, None, "tile"),
        P(None, "tile"),
        P(),
        P("section", None, None),
        P("section", None, None),
        P("section", None, None),
        P("section", None, None),
    )
    out_specs = P("section", None, None, None, "tile")
    return jax.shard_map(on_device, mesh=mesh, in_specs=in_specs, out_specs=out_specs, check_vma=False)
```

```python
import functools

import jax
import jax.numpy as jnp
import numpy as np
from jax import lax
from jax.experimental import pallas as pl
from jax.experimental.pallas import tpu as pltpu
from jax.sharding import PartitionSpec as P

HEADS = 6
WZ = 2
WLAT = 6
WLON = 12
HALF = WLON // 2
STAGE = 4
LOG2E = 1.4426950408889634
LANES = 128
VMEM_LIMIT = 36 * 2**20


def in_vmem(value):
    return pltpu.with_memory_space_constraint(value, pltpu.VMEM)


def normalize(values):
    center = values - jnp.mean(values, axis=-1, keepdims=True)
    spread = jnp.mean(center * center, axis=-1, keepdims=True)
    return center * lax.rsqrt(spread + 1e-05)


def window_bias(levels, rows):
    lat_blocks = rows // WLAT
    index = np.arange(WLAT * levels * HALF)
    row, level = index // (levels * HALF), index // HALF % levels
    row = row[None] + WLAT * np.arange(lat_blocks)[:, None]

    def label(place, length, window):
        return np.where(place < length - window, 0, np.where(place < length - window // 2, 1, 2))

    labels = label(level, levels, WZ)[None] * 3 + label(row, rows, WLAT)
    keys = np.concatenate([labels, labels], 1)
    return np.where(labels[:, :, None] == keys[:, None, :], 0.0, -1e30).astype(np.float32)


def pack_tile(west, east):
    return jnp.concatenate(
        [west[:, :LANES], jnp.concatenate([west[:, LANES:], east[:, LANES:]], 1), east[:, :LANES]], 0
    )


def unpack_tile(packed, tokens):
    side = packed[tokens : 2 * tokens]
    middle = LANES // 2
    west = jnp.concatenate([packed[:tokens], side[:, :middle]], 1)
    return west, jnp.concatenate([packed[2 * tokens :], side[:, middle:]], 1)


def embed_kernel(micro_ref, fields_ref, mask_ref, vector_ref, tile_ref, grid_ref):
    _, levels, rows, _ = fields_ref.shape
    width = vector_ref.shape[1]
    mask = mask_ref[...].astype(jnp.float32)
    vector = vector_ref[...]
    step = levels * HALF
    for level in range(levels):
        for column in range(WLON):
            piece = fields_ref[0, level, :, column * width : (column + 1) * width].astype(jnp.float32)
            piece = piece + mask[:, column : column + 1] * vector
            half, inside = divmod(column, HALF)
            at = pl.ds(level * HALF + inside, rows, stride=step)
            grid_ref[2 * half, at, :] = piece[:, :LANES]
            grid_ref[2 * half + 1, at, :] = jnp.concatenate([piece[:, LANES:]] * 2, 1)
    tokens, side = rows * step, width - LANES
    tile_ref[:tokens] = grid_ref[0].astype(jnp.bfloat16)
    tile_ref[2 * tokens :] = grid_ref[2].astype(jnp.bfloat16)
    lane = lax.broadcasted_iota(jnp.int32, (1, LANES), 1)
    tile_ref[tokens : 2 * tokens] = jnp.where(lane < side, grid_ref[1], grid_ref[3]).astype(jnp.bfloat16)


def embed(micro, fields, land_mask, land_vector):
    _, levels, rows, flat = fields.shape
    tokens = rows * levels * HALF
    whole = lambda a: pl.BlockSpec(a.shape, lambda i, m: (0,) * a.ndim)
    return pl.pallas_call(
        embed_kernel,
        out_shape=pltpu.VMEM((3 * tokens, LANES), jnp.bfloat16),
        grid_spec=pltpu.PrefetchScalarGridSpec(
            num_scalar_prefetch=1,
            grid=(1,),
            in_specs=[pl.BlockSpec((1, levels, rows, flat), lambda i, m: (m[0], 0, 0, 0)),
                      whole(land_mask), whole(land_vector)],
            out_specs=pl.BlockSpec((3 * tokens, LANES), lambda i, m: (0, 0)),
            scratch_shapes=[pltpu.VMEM((4, tokens, LANES), jnp.float32)],
        ),
        compiler_params=pltpu.CompilerParams(vmem_limit_bytes=VMEM_LIMIT),
        name="embed",
    )(micro, fields, land_mask, land_vector)


def pack_kernel(wqkv_ref, wproj_ref, wup_ref, wdown_ref, pack_ref):
    width = wproj_ref.shape[1]
    side = 256 - width
    for i in range(3):
        pack_ref[:, 256 * i : 256 * i + 256] = jnp.concatenate(
            [wqkv_ref[0, :, i * width : (i + 1) * width], wproj_ref[0, :, i * side : (i + 1) * side]], 1
        )
    hidden = wup_ref.shape[2]
    pack_ref[:, 768 : 768 + hidden] = wup_ref[0]
    pack_ref[:, 768 + hidden :] = wdown_ref[0]


def pack_weights(*weights):
    vmem = pl.BlockSpec(memory_space=pltpu.VMEM)
    width = weights[0].shape[1]
    return pl.pallas_call(
        pack_kernel,
        out_shape=pltpu.VMEM((width, 2304), jnp.bfloat16),
        in_specs=[vmem] * len(weights),
        out_specs=vmem,
        compiler_params=pltpu.CompilerParams(vmem_limit_bytes=VMEM_LIMIT),
        name="pack_weights",
    )(*[pltpu.with_memory_space_constraint(w, pltpu.HBM) for w in weights])


def compute_blocks(mode, flags, tile_refs, bias_ref, w_ref, wproj_ref, store, scratch):
    xa, xb, q_ref, k_ref, v_ref, low_ref, high_ref = scratch
    f32, bf16 = jnp.float32, jnp.bfloat16
    halves, tokens, width = xa.shape
    head_size = width // HEADS
    windows, piece, _ = bias_ref.shape
    move = piece // 2
    hidden = (w_ref.shape[2] - 768) // 2
    channel_head = lax.broadcasted_iota(jnp.int32, (1, width), 1) // head_size
    scale = head_size ** (-0.5) * LOG2E
    ones = jnp.ones((2 * piece, 256 - width), f32)

    def load_tiles():
        into = xb if mode.startswith("odd") else xa
        for i, ref in enumerate(tile_refs):
            if ref.shape[0] == 3 * tokens:
                base = 4 * flags[i - 1] if i else 2
                for j, part in enumerate(unpack_tile(ref[...].astype(f32), tokens)):
                    into[base + j] = part.astype(bf16)
            else:
                east = flags[i - 1]
                main, side = ref[:tokens].astype(f32), ref[tokens:].astype(f32)
                last = jnp.where(east == 1, side[:, : LANES // 2], side[:, LANES // 2 :])
                into[1 + 3 * east] = jnp.concatenate([main, last], 1).astype(bf16)

    def select_heads(parts, first, lanes):
        total = parts[0]
        for n in range(1, len(parts)):
            total = jnp.where(channel_head[:, first : first + lanes] == first // head_size + n, parts[n], total)
        return total

    def rows_of(w):
        return pl.ds(w * piece if isinstance(w, int) else pl.multiple_of(w * piece, 8), piece)

    def window_attention(h, i, w, shifted, exact):
        q = q_ref[h, rows_of(w), :]
        qm = jnp.concatenate([jnp.where(channel_head == n, q, 0.0) for n in range(HEADS)], 0).astype(bf16)
        s = lax.dot_general(qm, k_ref[i, w], (((1,), (1,)), ((), ())), preferred_element_type=f32)
        if shifted:
            s = (s.reshape(HEADS, piece, 2 * piece) + bias_ref[w][None]).reshape(HEADS * piece, 2 * piece)
        if exact:
            s = s - jnp.max(s, axis=-1, keepdims=True)
        o = jnp.dot(jnp.exp2(s).astype(bf16), v_ref[i, w], preferred_element_type=f32)
        heads = [o[n * piece : (n + 1) * piece] for n in range(HEADS)]
        full = LANES // head_size
        tops = [select_heads([x[:, :LANES] for x in heads[:full]], 0, LANES),
                select_heads([x[:, LANES:width] for x in heads[full:]], LANES, width - LANES)]
        side = 256 - width
        ends = [x[:, LANES:] for x in heads]
        odd = channel_head[:, :LANES] % 2 == 1
        couples = [jnp.where(odd, ends[n + 1], ends[n]) for n in range(0, HEADS, 2)]
        lane = lax.broadcasted_iota(jnp.int32, (1, LANES), 1)
        sums = [jnp.where(lane < side, pltpu.roll(couples[0], side, 1), couples[1]),
                pltpu.roll(couples[2], side, 1)[:, :side]]
        if not exact:
            low_ref[...] = jnp.minimum(low_ref[...], jnp.min(sums[0].reshape(-1, 8, LANES), axis=0))
            high_ref[...] = jnp.maximum(high_ref[...], jnp.max(sums[0].reshape(-1, 8, LANES), axis=0))
            rest = slice(0, width - LANES)
            low_ref[:, rest] = jnp.minimum(low_ref[:, rest], jnp.min(sums[1].reshape(-1, 8, width - LANES), axis=0))
            high_ref[:, rest] = jnp.maximum(high_ref[:, rest], jnp.max(sums[1].reshape(-1, 8, width - LANES), axis=0))
        return jnp.concatenate([top / total for top, total in zip(tops, sums)], 1)

    def block(b, shifted, exact, together, first_pair, pairs, first_q, count):
        source, target = (xb, xa) if shifted else (xa, xb)

        def load(h):
            x = source[h].astype(f32)
            return pltpu.roll(x, tokens - move, 0) if shifted else x

        def pair(i, carry):
            kv = []
            for j in range(2):
                h = first_pair + 2 * i + j
                qkv = jnp.dot(normalize(load(h)).astype(bf16), w_ref[b, :, :768], preferred_element_type=f32)
                q_ref[h] = qkv[:, :width] * scale
                kv.append((qkv[:, 256 : 256 + width], qkv[:, 512 : 512 + width]))
            for w in range(windows):
                at = slice(w * piece, (w + 1) * piece)
                k_ref[i, w] = jnp.concatenate([kv[0][0][at], kv[1][0][at]], 0).astype(bf16)
                v = jnp.concatenate([kv[0][1][at], kv[1][1][at]], 0)
                v_ref[i, w] = jnp.concatenate([v, ones], 1).astype(bf16)
            return carry

        def attend(c, carry):
            own = [first_q + together * c + j for j in range(together)]
            x = jnp.concatenate([load(h) for h in own], 0)
            if exact:

                def one_window(w, carry):
                    for h in own:
                        q_ref[h, rows_of(w), :] = window_attention(h, (h - first_pair) // 2, w, shifted, exact)
                    return carry

                lax.fori_loop(0, windows, one_window, 0)
                a = jnp.concatenate([q_ref[h] for h in own], 0).astype(bf16)
            else:
                parts = [
                    window_attention(h, (h - first_pair) // 2, w, shifted, exact) for h in own for w in range(windows)
                ]
                a = jnp.concatenate(parts, 0).astype(bf16)
            residual = x + jnp.dot(a, wproj_ref[b], preferred_element_type=f32)
            n2 = normalize(residual).astype(bf16)
            u = jnp.dot(n2, w_ref[b, :, 768 : 768 + hidden], preferred_element_type=f32)
            g = (0.5 * u * (1.0 + lax.erf(u * (0.5**0.5)))).astype(bf16)
            y = residual + lax.dot_general(
                g, w_ref[b, :, 768 + hidden :], (((1,), (1,)), ((), ())), preferred_element_type=f32
            )
            for j, h in enumerate(own):
                part = y[j * tokens : (j + 1) * tokens]
                if shifted:
                    part = pltpu.roll(part, move, 0)
                target[h] = part.astype(bf16)
            return carry

        lax.fori_loop(0, pairs, pair, 0)
        lax.fori_loop(0, count // together, attend, 0)
        store(b, pack_tile(target[2].astype(f32), target[3].astype(f32)).astype(bf16))

    def compute(exact, together):
        load_tiles()

        def odd(b):
            block(b, True, exact, together, 1, 2, 2, 2)

        def even(b):
            block(b, False, exact, together, 2, 1, 2, 2)

        def wide_even(n, carry):
            block(2 * n, False, exact, together, 2 * n, 3 - 2 * n, 1 + n, 4 - 2 * n)
            pl.when(n == 0)(lambda: odd(1))
            return carry

        if mode == "wide even":
            lax.fori_loop(0, 2, wide_even, 0)
        elif mode == "even":
            even(0)
        else:
            odd(0)
            if mode == "odd even":
                even(1)

    low_ref[...] = jnp.ones_like(low_ref)
    high_ref[...] = jnp.ones_like(high_ref)
    compute(False, 2)
    safe = (jnp.min(low_ref[...]) >= 2.0**-90) & (jnp.max(high_ref[...]) <= 2.0**90)

    @pl.when(jnp.logical_not(safe))
    def _():
        compute(True, 1)


def unpack_projection(ref, width):
    return jnp.concatenate([ref[:, 256 * j + width : 256 * j + 256] for j in range(3)], 1)


def gather_weights(place, refs, blocks, w_ref, wproj_ref):
    for i, ref in enumerate(refs):
        b = place ^ i

        @pl.when((b >= blocks[0]) & (b <= blocks[-1]))
        def _(ref=ref, slot=b - blocks[0]):
            w_ref[slot] = ref[...]
            wproj_ref[slot] = unpack_projection(ref, wproj_ref.shape[1])


def store_halves(place_ref, tile_ref, o_ref, e_ref):
    tokens = tile_ref.shape[0] // 3
    for ref, flag in ((o_ref, place_ref[2]), (e_ref, place_ref[3])):
        ref[:tokens] = jnp.where(flag == 1, tile_ref[2 * tokens :].astype(jnp.float32),
                                 tile_ref[:tokens].astype(jnp.float32)).astype(jnp.bfloat16)
        ref[tokens:] = tile_ref[tokens : 2 * tokens]


def part_kernel(mode, blocks, tile_count, place_ref, *refs):
    tiles, refs = refs[:tile_count], refs[tile_count:]
    weights, bias_ref, refs = refs[:STAGE], refs[STAGE], refs[STAGE + 1 :]
    outs, refs = refs[: len(blocks)], refs[len(blocks) :]
    halves = ()
    if mode != "odd":
        halves, refs = refs[:2], refs[2:]
    w_ref, wproj_ref, stage_ref, *scratch = refs
    gather_weights(place_ref[0], weights, blocks, w_ref, wproj_ref)

    def store(slot, packed):
        stage_ref[slot] = packed

    flags = (place_ref[2], place_ref[3])
    compute_blocks(mode, flags, tiles, bias_ref, w_ref, wproj_ref, store, scratch)
    for i, ref in enumerate(outs):
        ref[...] = stage_ref[i]
    if halves:
        store_halves(place_ref, outs[-1], *halves)


def last_kernel(place_ref, *refs):
    tiles, refs = refs[:3], refs[3:]
    weights, bias_ref, refs = refs[:STAGE], refs[STAGE], refs[STAGE + 1 :]
    early, late, refs = refs[:STAGE], refs[STAGE : 2 * STAGE - 1], refs[2 * STAGE - 1 :]
    outs, refs = refs[:STAGE], refs[STAGE:]
    w_ref, wproj_ref, stage_ref, *scratch = refs
    place = place_ref[0]

    def route(sources):
        for i, ref in enumerate(outs):
            for b, source in enumerate(sources):

                @pl.when((place ^ i) == b)
                def _(ref=ref, source=source):
                    ref[...] = source[...]

    @pl.when(place_ref[1] == 1)
    def _():
        gather_weights(place, weights, (STAGE - 1,), w_ref, wproj_ref)

        def store(slot, packed):
            stage_ref[slot] = packed

        flags = (place_ref[2], place_ref[3])
        compute_blocks("odd", flags, tiles, bias_ref, w_ref, wproj_ref, store, scratch)
        route((*late, stage_ref.at[0]))

    @pl.when(place_ref[1] == 0)
    def _():
        route(early)


def run_part(kernel, name, place, operands, outs, blocks, tokens, width, bias_shape):
    halves = 6
    windows, piece, _ = bias_shape
    vmem = pl.BlockSpec(memory_space=pltpu.VMEM)
    bf16, f32 = jnp.bfloat16, jnp.float32
    return pl.pallas_call(
        kernel,
        out_shape=tuple(pltpu.VMEM(shape, bf16) for shape in outs),
        in_specs=[pl.BlockSpec(memory_space=pltpu.SMEM)] + [vmem] * len(operands),
        out_specs=(vmem,) * len(outs),
        scratch_shapes=[
            pltpu.VMEM((blocks, width, 2304), bf16),
            pltpu.VMEM((blocks, width, width), bf16),
            pltpu.VMEM((blocks, 3 * tokens, LANES), bf16),
            pltpu.VMEM((halves, tokens, width), bf16),
            pltpu.VMEM((halves, tokens, width), bf16),
            pltpu.VMEM((halves, tokens, width), f32),
            pltpu.VMEM((halves // 2, windows, 2 * piece, width), bf16),
            pltpu.VMEM((halves // 2, windows, 2 * piece, 256), bf16),
            pltpu.VMEM((8, LANES), f32),
            pltpu.VMEM((8, LANES), f32),
        ],
        compiler_params=pltpu.CompilerParams(vmem_limit_bytes=VMEM_LIMIT),
        name=name,
    )(place, *[in_vmem(x) for x in operands])


def finish_kernel(count, place_ref, *refs):
    out_ref, grid_ref = refs[-2:]
    _, _, rows, levels, _ = out_ref.shape
    tokens = grid_ref.shape[1]
    width = out_ref.shape[4] // WLON
    side = width - LANES
    for i, ref in enumerate(refs[:count]):

        @pl.when(pl.program_id(0) == i)
        def _(ref=ref):
            packed = ref[...].astype(jnp.float32)
            for part in range(3):
                grid_ref[part] = packed[part * tokens : (part + 1) * tokens]
            for column in range(WLON):
                half, inside = divmod(column, HALF)
                at = pl.ds(inside, rows * levels, stride=HALF)
                rest = grid_ref[1, at, :][:, half * side : (half + 1) * side]
                piece = jnp.concatenate([grid_ref[2 * half, at, :], rest], 1).reshape(rows, levels, width)
                out_ref[0, 0, :, :, column * width : (column + 1) * width] = piece.astype(jnp.bfloat16)


def finish(place, pieces, first, step, shape, buffer=None):
    tokens = pieces[0].shape[0] // 3
    count = len(pieces)
    vmem = pl.BlockSpec(memory_space=pltpu.VMEM)
    more = [] if buffer is None else [buffer]
    return pl.pallas_call(
        functools.partial(finish_kernel, count),
        out_shape=jax.ShapeDtypeStruct(shape, jnp.bfloat16),
        grid_spec=pltpu.PrefetchScalarGridSpec(
            num_scalar_prefetch=1,
            grid=(count,),
            in_specs=[vmem] * count + [pl.BlockSpec(memory_space=pl.ANY)] * len(more),
            out_specs=pl.BlockSpec((1, 1) + shape[2:], lambda i, m: (0, m[0] ^ (first + i * step), 0, 0, 0)),
            scratch_shapes=[pltpu.VMEM((3, tokens, LANES), jnp.float32)],
        ),
        input_output_aliases={1 + count: 0} if more else {},
        compiler_params=pltpu.CompilerParams(vmem_limit_bytes=VMEM_LIMIT),
        name="finish",
    )(place, *[in_vmem(x) for x in pieces], *more)


def on_device(fields, land_mask, land_vector, w_qkv, w_proj, w_up, w_down):
    micro_count, levels, rows, flat_width = fields.shape
    width = land_vector.shape[0]
    tile_count, section_count = lax.axis_size("tile"), lax.axis_size("section")
    section = lax.axis_index("section")
    tile_index = lax.axis_index("tile")
    place = jnp.stack([section % STAGE, section // STAGE, tile_index % 2, 1 - tile_index % 2]).astype(jnp.int32)
    axes = ("tile", "section")

    def exchange(value, bit):
        return lax.ppermute(value, "section", [(s, s ^ bit) for s in range(section_count)])

    def forward(value):
        return lax.ppermute(value, "section", [(s, s + STAGE) for s in range(STAGE)])

    def swap(odd_value, even_value, first, fields_first=False):
        received = {}
        for value, phase in ((odd_value, 1), (even_value, 0))[:: 1 if fields_first else -1]:
            pairs = []
            for t in range(phase, tile_count, 2):
                for s in range(first, first + STAGE):
                    here, there = t * section_count + s, (t + 1) % tile_count * section_count + s
                    pairs += [(here, there), (there, here)]
            received[phase] = lax.ppermute(value, axes, pairs)
        return received[1], received[0]

    tokens = rows * levels * HALF
    tile_shape, half_shape = (3 * tokens, LANES), (2 * tokens, LANES)
    bias = jnp.asarray(window_bias(levels, rows))
    sizes = (tokens, width, bias.shape)

    pack = pack_weights(w_qkv, w_proj, w_up, w_down.transpose(0, 2, 1))
    near, far = exchange(pack, 1), exchange(pack, 2)
    tile = embed(place, fields, land_mask, land_vector.reshape(1, width))
    halo = swap(tile, tile, 0, True)
    far, halo = lax.optimization_barrier((far, halo))
    weights = (pack, near, far, exchange(far, 1))

    def part(mode, name, blocks, tiles):
        shapes = (tile_shape,) * len(blocks) + (() if mode == "odd" else (half_shape,) * 2)
        kernel = functools.partial(part_kernel, mode, blocks, len(tiles))
        return run_part(kernel, name, place, (*tiles, *weights, bias), shapes, len(blocks), *sizes)

    y0, y1, y2, o, e = part("wide even", "blocks_0_2", (0, 1, 2), (tile, *halo))
    (y3,) = part("odd", "block_3", (3,), (y2, *swap(o, e, 0)))
    y4, o, e = part("even", "block_4", (0,), (forward(y3),))
    y5, y6, o, e = part("odd even", "blocks_5_6", (1, 2), (y4, *swap(o, e, STAGE)))
    operands = (y6, *swap(o, e, STAGE), *weights, bias, y0, y1, y2, y3, y4, y5, y6)
    outs = run_part(last_kernel, "block_7", place, operands, (tile_shape,) * STAGE, 1, *sizes)

    diagonal, far_piece, mate = (exchange(outs[i], i) for i in (3, 2, 1))
    shape = (1, micro_count, rows, levels, flat_width)
    result = finish(place, [outs[0], diagonal], 0, 3, shape)
    return finish(place, [mate, far_piece], 1, 1, shape, result).transpose(0, 1, 3, 2, 4)


def solution(mesh):
    in_specs = (
        P(None, None, None, "tile"),
        P(None, "tile"),
        P(),
        P("section", None, None),
        P("section", None, None),
        P("section", None, None),
        P("section", None, None),
    )
    out_specs = P("section", None, None, None, "tile")
    return jax.shard_map(on_device, mesh=mesh, in_specs=in_specs, out_specs=out_specs, check_vma=False)
```
